32 devices in a mesh: dp: 8 (over y, x, core), mp: 4 (over z).
Axes of the slice: x: 2, y: 2, z: 4, core: 2. Of those that a mesh axis runs over, the one named last changes fastest.
Arguments:
- row_input: bfloat16 [5120, 512], P('dp'), may hold values from -6 to 6
- first_gain: float32 [512], replicated, may hold values from 0.5 to 1.5
- first_shift: float32 [512], replicated, may hold values from -4 to 4
- query_weight: bfloat16 [512, 512], P(None, 'mp'), may hold values from -0.25 to 0.25
- key_weight: bfloat16 [512, 512], P(None, 'mp'), may hold values from -0.25 to 0.25
- value_weight: bfloat16 [512, 512], P(None, 'mp'), may hold values from -0.25 to 0.25
- out_weight: bfloat16 [512, 512], P('mp'), may hold values from -2 to 2
- out_bias: float32 [512], replicated, may hold values from -6 to 6
- second_gain: float32 [512], replicated, may hold values from 0.5 to 1.5
- second_shift: float32 [512], replicated, may hold values from -4 to 4
- up_weight: bfloat16 [512, 2048], P(None, 'mp'), may hold values from -0.25 to 0.25
- up_bias: float32 [2048], P('mp'), may hold values from -6 to 6
- down_weight: bfloat16 [2048, 512], P('mp'), may hold values from -0.125 to 0.125
- down_bias: float32 [512], replicated, may hold values from -6 to 6
- row_table: int32 [5120], P('dp'), may hold values from 0 to 5119, as said below
- row_kind: int32 [5120], P('dp'), may hold values from 0 to 1, as said below
- out_grad: bfloat16 [5120, 512], P('dp'), may hold values from -6 to 6
Outputs:
- block_output: bfloat16 [5120, 512], P('dp')
- input_grad: float32 [5120, 512], P('dp')
- first_gain_grad: float32 [512], replicated
- first_shift_grad: float32 [512], replicated
- query_weight_grad: float32 [512, 512], P(None, 'mp')
- key_weight_grad: float32 [512, 512], P(None, 'mp')
- value_weight_grad: float32 [512, 512], P(None, 'mp')
- out_weight_grad: float32 [512, 512], P('mp')
- out_bias_grad: float32 [512], replicated
- second_gain_grad: float32 [512], replicated
- second_shift_grad: float32 [512], replicated
- up_weight_grad: float32 [512, 2048], P(None, 'mp')
- up_bias_grad: float32 [2048], P('mp')
- down_weight_grad: float32 [2048, 512], P('mp')
- down_bias_grad: float32 [512], replicated
The draws below stay inside these ranges and needn't reach their ends.
Inputs may be any that keep to these rules, and one draw needn't show every extreme that they name: `row_table`: table 0 holds row 0 of every block of 640 rows, so it has rows on every device of dp; every other table is a run of consecutive rows outside table 0, its id the index of its first row, on devices at most 2 apart, and in every draw one spans exactly 2; the last row is a table of its own. `row_kind`: every table has a support row: table 0 has exactly two, on two different devices, and the first row of every other table has kind 1.
All inputs are finite; a program needn't handle non-finite values.
Results may differ from the reference program's by a relative error of at most 0.02.
Values may be sent and summed in bfloat16 or wider, within the bound.
A program may use at most 192 MiB of HBM per device.

```python
import math
import jax
import jax.numpy as jnp
from jax import lax

D = 512
HEADS = 4
HD = 128
FF = 2048
TOK_DEV = 640
NEAR = 2
TOKENS = 5120


def table_layout(key):
    device_count = TOKENS // TOK_DEV
    longest = NEAR * TOK_DEV + 1
    short_most = max(2, longest // 8)
    tier_pick = jax.random.randint(jax.random.fold_in(key, 101), (TOKENS,), 0, 8).astype(jnp.int32)
    short_limits = jax.random.randint(jax.random.fold_in(key, 102), (TOKENS,), 1, short_most + 1).astype(jnp.int32)
    kind_draw = jax.random.randint(jax.random.fold_in(key, 105), (TOKENS,), 0, 2).astype(jnp.int32)
    first_holder = jax.random.randint(jax.random.fold_in(key, 107), (), 0, device_count).astype(jnp.int32)
    holder_step = jax.random.randint(jax.random.fold_in(key, 108), (), 1, device_count).astype(jnp.int32)
    second_holder = ((first_holder + holder_step) % device_count).astype(jnp.int32)
    row_index = jnp.arange(TOKENS, dtype=jnp.int32)
    device_of = (row_index // TOK_DEV).astype(jnp.int32)
    is_wide = row_index % TOK_DEV == 0
    forced_start = (row_index == TOK_DEV - 1) | (row_index == NEAR * TOK_DEV + 1) | (row_index == TOKENS - 1)
    forced_inside = (row_index >= TOK_DEV) & (row_index <= NEAR * TOK_DEV)

    def advance(carried, pieces):
        length, bound_now = carried
        tier_now, short_limit, must_start, must_stay, wide_now = pieces
        begins = must_start | jnp.logical_not(must_stay) & (length >= bound_now)
        fresh_bound = jnp.where(tier_now == 0, longest, short_limit).astype(jnp.int32)
        new_bound = jnp.where(begins, fresh_bound, bound_now).astype(jnp.int32)
        new_length = jnp.where(begins, 1, length + 1).astype(jnp.int32)
        new_bound = jnp.where(wide_now, bound_now, new_bound).astype(jnp.int32)
        new_length = jnp.where(wide_now, length, new_length).astype(jnp.int32)
        emitted = (begins & jnp.logical_not(wide_now)).astype(jnp.int32)
        return ((new_length, new_bound), emitted)
    starts = lax.scan(advance, (jnp.int32(0), jnp.int32(0)), (tier_pick, short_limits, forced_start, forced_inside, is_wide))[1]
    tables = lax.cummax(jnp.where(starts == 1, row_index, 0).astype(jnp.int32), axis=0).astype(jnp.int32)
    tables = jnp.where(is_wide, 0, tables).astype(jnp.int32)
    wide_kind = ((device_of == first_holder) | (device_of == second_holder)).astype(jnp.int32)
    row_kinds = jnp.where(starts == 1, 1, kind_draw).astype(jnp.int32)
    row_kinds = jnp.where(is_wide, wide_kind, row_kinds).astype(jnp.int32)
    return (tables, row_kinds)


def draw_row_table(key, part):
    return table_layout(key)[0]


def draw_row_kind(key, part):
    return table_layout(key)[1]


def steps_of(stream_key, dims, cuts, smallest, high):
    loudness, own = 1.0, jax.random.fold_in(stream_key, 6)
    for axis_at, blocks in cuts:
        draws = jnp.exp(jax.random.uniform(jax.random.fold_in(own, axis_at), (blocks,), jnp.float32, smallest / len(cuts), high / len(cuts)))
        loudness = loudness * jnp.repeat(draws, dims[axis_at] // blocks).reshape([-1 if axis == axis_at else 1 for axis in range(len(dims))])
    return loudness


def normal_values(stream_key, dims, deviation, limit, cuts=(), kind=jnp.bfloat16):
    result = jax.random.normal(stream_key, dims, jnp.float32) * deviation
    if len(cuts) > 0:
        result = steps_of(stream_key, dims, cuts, -0.22, 0.18) * result
    return jnp.clip(result, min=-limit, max=limit).astype(kind)


def setup_inputs(seed: int = 0) -> dict:
    key_list = jax.random.split(jax.random.key(seed), 18)
    return {
        "row_input": normal_values(key_list[0], (TOKENS, D), 1.0, 6.0, ((0, 8),)),
        "first_gain": jnp.clip(1.0 + 0.1 * jax.random.normal(key_list[1], (D,), jnp.float32), 0.5, 1.5),
        "first_shift": normal_values(key_list[2], (D,), 0.3, 4.0, (), jnp.float32),
        "query_weight": normal_values(key_list[3], (D, D), D ** -0.5, 0.25, ((1, 4),)),
        "key_weight": normal_values(key_list[4], (D, D), D ** -0.5, 0.25, ((1, 4),)),
        "value_weight": normal_values(key_list[5], (D, D), D ** -0.5, 0.25, ((1, 4),)),
        "out_weight": normal_values(key_list[6], (D, D), 8 ** -0.5, 2.0, ((0, 4),)),
        "out_bias": normal_values(key_list[7], (D,), 0.5, 6.0, (), jnp.float32),
        "second_gain": jnp.clip(1.0 + 0.1 * jax.random.normal(key_list[8], (D,), jnp.float32), 0.5, 1.5),
        "second_shift": normal_values(key_list[9], (D,), 0.3, 4.0, (), jnp.float32),
        "up_weight": normal_values(key_list[10], (D, FF), D ** -0.5, 0.25, ((1, 4),)),
        "up_bias": normal_values(key_list[11], (FF,), 0.5, 6.0, ((0, 4),), jnp.float32),
        "down_weight": normal_values(key_list[12], (FF, D), FF ** -0.5, 0.125, ((0, 4),)),
        "down_bias": normal_values(key_list[13], (D,), 0.5, 6.0, (), jnp.float32),
        "row_table": draw_row_table(jax.random.fold_in(key_list[17], 71), 0),
        "row_kind": draw_row_kind(jax.random.fold_in(key_list[17], 71), 0),
        "out_grad": normal_values(key_list[16], (TOKENS, D), 1.0, 6.0, ((0, 8),)),
    }


norm_eps = 1e-05
masked_score = -1e+30
highest = lax.Precision.HIGHEST

@jax.custom_vjp
def low(v):
    return lax.optimization_barrier(v.astype(jnp.bfloat16)).astype(jnp.float32)

@jax.custom_vjp
def low_back(v):
    return v

def low_keep(v):
    return (low(v), None)

def low_pass(kept, grad):
    return (grad,)

def back_keep(v):
    return (v, None)

def back_low(kept, grad):
    return (low(grad),)
low.defvjp(low_keep, low_pass)
low_back.defvjp(back_keep, back_low)

def layer_norm(values_in, gain_in, shift_in):
    average = lax.optimization_barrier(jnp.mean(values_in, axis=-1, keepdims=True))
    centred = values_in - average
    spread = lax.optimization_barrier(jnp.mean(centred * centred, axis=-1, keepdims=True))
    return centred * lax.rsqrt(spread + norm_eps) * gain_in + shift_in

def gelu_exact(values_in):
    return 0.5 * values_in * (1.0 + lax.erf(values_in * 2.0 ** (-0.5)))

def product(left_side, right_side):
    return jnp.dot(left_side, right_side, preferred_element_type=jnp.float32, precision=highest)

def attention(query, keys, values_in, row_table, row_kind):
    token_count = query.shape[0]
    block_rows = math.gcd(token_count, 1024)
    block_count = token_count // block_rows
    key_heads = keys.reshape(token_count, HEADS, HD)
    value_heads = values_in.reshape(token_count, HEADS, HD)
    support = row_kind == 1

    def one_block(pieces):
        query_block, table_block = pieces
        scores = jnp.einsum('qhd,khd->hqk', query_block, key_heads, precision=highest)
        scores = low_back(scores * HD ** (-0.5))
        allowed = (table_block[:, None] == row_table[None, :]) & support[None, :]
        masked = jnp.where(allowed[None], scores, masked_score)
        largest = lax.optimization_barrier(jnp.max(masked, axis=-1, keepdims=True))
        exponents = jnp.exp(masked - largest)
        probabilities = low(exponents / lax.optimization_barrier(jnp.sum(exponents, axis=-1, keepdims=True)))
        mixed_heads = jnp.einsum('hqk,khd->qhd', probabilities, value_heads, precision=highest)
        return mixed_heads.reshape(block_rows, HEADS * HD)
    outcome = lax.map(jax.checkpoint(one_block), (query.reshape(block_count, block_rows, HEADS, HD), row_table.reshape(block_count, block_rows)))
    return outcome.reshape(token_count, HEADS * HD)

def reference(row_input, first_gain, first_shift, query_weight, key_weight, value_weight, out_weight, out_bias, second_gain, second_shift, up_weight, up_bias, down_weight, down_bias, row_table, row_kind, out_grad):
    floats = tuple((argument.astype(jnp.float32) for argument in (row_input, first_gain, first_shift, query_weight, key_weight, value_weight, out_weight, out_bias, second_gain, second_shift, up_weight, up_bias, down_weight, down_bias)))

    def forward(row_input, first_gain, first_shift, query_weight, key_weight, value_weight, out_weight, out_bias, second_gain, second_shift, up_weight, up_bias, down_weight, down_bias):
        normed = low(layer_norm(row_input, first_gain, first_shift))
        query = low_back(low(product(normed, query_weight)))
        keys = low_back(low(product(normed, key_weight)))
        values_in = low_back(low(product(normed, value_weight)))
        mixed = low_back(low(attention(query, keys, values_in, row_table, row_kind)))
        branch = low_back(product(mixed, out_weight) + out_bias)
        middle = row_input + branch
        normed_mid = low(layer_norm(middle, second_gain, second_shift))
        upper = low_back(product(normed_mid, up_weight) + up_bias)
        active = low(gelu_exact(upper))
        return middle + product(active, down_weight) + down_bias
    outcome, pullback = jax.vjp(forward, *floats)
    gradients = pullback(out_grad.astype(jnp.float32))
    return (outcome.astype(jnp.bfloat16), gradients[0], gradients[1], gradients[2], gradients[3], gradients[4], gradients[5], gradients[6], gradients[7], gradients[8], gradients[9], gradients[10], gradients[11], gradients[12], gradients[13])
```

```python
import math
import types

import jax
import jax.numpy as jnp
from jax import lax
from jax.experimental import pallas as pl
from jax.experimental.pallas import tpu as pltpu
from jax.sharding import PartitionSpec as P

HD = 128
NEAR = 2
SLOTS = 2 * NEAR + 1
OWN = NEAR
LANE = 128
CHUNK = 128
norm_eps = 1e-05
masked_score = -1e30
f32 = jnp.float32
bf16 = jnp.bfloat16
MESH = pl.DeviceIdType.MESH
SCALE = HD ** (-0.5)
EXP2_SCALE = SCALE * math.log2(math.e)
NN = (((1,), (0,)), ((), ()))
NT = (((1,), (1,)), ((), ()))
TN = (((0,), (0,)), ((), ()))


def mm(a, b, dims=NN):
    return lax.dot_general(a, b, dims, preferred_element_type=f32)


def remote(src, dst, send_sem, recv_sem, device):
    return pltpu.make_async_remote_copy(
        src_ref=src, dst_ref=dst, send_sem=send_sem, recv_sem=recv_sem,
        device_id=device, device_id_type=MESH,
    )


def when(cond, action):
    if cond is True:
        action()
    else:
        pl.when(cond)(action)


def place(n_dp, n_mp):
    d = lax.axis_index("dp")
    m = lax.axis_index("mp")
    return d, m


def near_hops(n_dp, d):
    if n_dp == 8:
        core, x, y = lax.rem(d, 2), lax.rem(d // 2, 2), d // 4
        other = d + 1 - 2 * core
        return [
            (True, OWN, other, 1 + 2 * core, True, 3 - 2 * core, None),
            (True, OWN, d + 2 - 4 * x, 4 * x, True, 4 - 4 * x, None),
            (core == x, 4 - 4 * x, other, 3 - 2 * x, core != x, 3 - 2 * x, 1),
            (x == y, 4 - 4 * y, d + 4 - 8 * y, 4 * y, x != y, 4 - 4 * y, 1),
            ((x != y) & (core == y), 4 - 4 * y, other, 3 - 2 * y,
             (x != y) & (core != y), 3 - 2 * y, 3),
        ]
    hops = []
    for step in (1, -1, 2, -2):
        to, source = d + step, d - step
        hops.append((
            (to >= 0) & (to < n_dp), OWN, lax.rem(to + n_dp, n_dp), OWN - step,
            (source >= 0) & (source < n_dp), OWN - step, None,
        ))
    return hops


def entry_barrier(n_dp, n_mp, d, m):
    barrier = pltpu.get_barrier_semaphore()

    def greet_dp(k, _):
        pl.semaphore_signal(barrier, inc=1, device_id=(lax.rem(d + k, n_dp), m), device_id_type=MESH)
        return 0

    lax.fori_loop(1, n_dp, greet_dp, 0)
    for k in range(1, n_mp):
        pl.semaphore_signal(barrier, inc=1, device_id=(d, lax.rem(m + k, n_mp)), device_id_type=MESH)
    pl.semaphore_wait(barrier, n_dp - 1 + n_mp - 1)


def layer_stats(values):
    average = jnp.mean(values, axis=-1, keepdims=True)
    centred = values - average
    spread = jnp.mean(centred * centred, axis=-1, keepdims=True)
    return centred, lax.rsqrt(spread + norm_eps)


def rows_of(index, size=CHUNK):
    return pl.ds(pl.multiple_of(index * size, size), size)


def spread_ids(ids_row, out_ref, rows):
    for r in range(rows // LANE):
        part = jnp.broadcast_to(ids_row[:, r * LANE:(r + 1) * LANE], (LANE, LANE))
        out_ref[r * LANE:(r + 1) * LANE, :] = part.T


def phase_attention_forward(r, n_dp, n_mp, rows):
    d, m = place(n_dp, n_mp)
    chunks = rows // CHUNK
    tiles = [slice(j * LANE, (j + 1) * LANE) for j in range(rows // LANE)]
    hops = near_hops(n_dp, d)

    def near_copy(hop, chunk):
        _, source, target, there, _, here, _ = hops[hop]
        part = rows_of(chunk)
        return remote(
            r.kv.at[source, part, :], r.kv.at[there, part, :],
            r.kv_send.at[hop, chunk], r.kv_recv.at[hop, chunk], (target, m),
        )

    def near_wait(hop, chunk):
        _, _, target, _, _, here, _ = hops[hop]
        part = rows_of(chunk)
        return remote(
            r.kv.at[OWN, part, :], r.kv.at[here, part, :],
            r.kv_send.at[hop, chunk], r.kv_recv.at[hop, chunk], (target, m),
        )

    table = r.row_table[...]
    own_ids = jnp.where((r.row_kind[...] == 1) & (table != 0), table, -1).astype(f32)
    r.ids[OWN] = own_ids
    r.query_ids[...] = jnp.broadcast_to(table.astype(f32), r.query_ids.shape)
    entry_barrier(n_dp, n_mp, d, m)
    id_steps = (1, -1, 2, -2)

    def id_copy(i, step):
        return remote(
            r.ids.at[OWN], r.ids.at[OWN - step], r.id_send.at[i], r.id_recv.at[i],
            (lax.rem(d + step + n_dp, n_dp), m),
        )

    for i, step in enumerate(id_steps):
        when((d + step >= 0) & (d + step < n_dp), id_copy(i, step).start)

    gain, shift = r.first_gain[...], r.first_shift[...]
    for i, w in enumerate((r.query_weight, r.key_weight, r.value_weight)):
        r.qkv_weight[:, i * HD:(i + 1) * HD] = w[...]
    first_hops = [h for h in range(len(hops)) if hops[h][6] is None]
    for c in range(chunks):
        part = slice(c * CHUNK, (c + 1) * CHUNK)
        centred, scale = layer_stats(r.row_input[part, :].astype(f32))
        normed = (centred * scale * gain + shift).astype(bf16)
        r.normed[part, :] = normed
        qkv = mm(normed, r.qkv_weight[...])
        r.kv[OWN, part, :] = qkv[:, HD:].astype(bf16)
        for h in first_hops:
            when(hops[h][0], near_copy(h, c).start)
        r.query[part, :] = qkv[:, :HD].astype(bf16)
        r.query_t[:, part] = qkv[:, :HD].T.astype(bf16)
        if c == 0:
            row = lax.broadcasted_iota(jnp.int32, (8, HD), 0)
            kind = jnp.where((r.row_kind[:, :1] == 1) & (table[:, :1] == 0), 1.0, 0.0)
            top = qkv[:8, HD:].astype(bf16).astype(f32)
            top = jnp.where(jnp.concatenate((row, row), axis=1) == 0, top, 0.0)
            mine = rows_of(d, 8)
            r.wide[mine, :2 * HD] = top
            r.wide[mine, 2 * HD:] = jnp.where(row == 0, jnp.broadcast_to(kind, (8, HD)), 0.0)

    def wide_copy(k, source):
        return remote(
            r.wide.at[rows_of(source, 8), :], r.wide.at[rows_of(source, 8), :],
            r.wide_send.at[k], r.wide_recv.at[k], (lax.rem(d + k, n_dp), m),
        )

    def wide_start(k, _):
        wide_copy(k, d).start()
        return 0

    lax.fori_loop(1, n_dp, wide_start, 0)

    r.top[...] = jnp.full_like(r.top, masked_score)
    r.total[...] = jnp.zeros_like(r.total)
    r.mixed_t[...] = jnp.zeros_like(r.mixed_t)

    def absorb(key_rows, peak):
        for j, lanes in enumerate(tiles):
            old = r.top[:, lanes]
            new = jnp.maximum(old, jnp.broadcast_to(jnp.max(peak[j], axis=0, keepdims=True), (8, LANE)))
            r.top[:, lanes] = new
            fade = jnp.exp2((old - new) * EXP2_SCALE)
            r.total[:, lanes] = r.total[:, lanes] * fade
            r.mixed_t[:, lanes] = r.mixed_t[:, lanes] * fade[:1, :]

        def weigh(t, _):
            size = min(key_rows, CHUNK)
            part = rows_of(t, size)
            for lanes in tiles:
                weight = jnp.exp2((r.scores[part, lanes] - r.top[:1, lanes]) * EXP2_SCALE)
                r.total[:, lanes] += jnp.sum(weight.reshape(size // 8, 8, LANE), axis=0)
                r.weights[part, lanes] = weight.astype(bf16)
            return 0

        lax.fori_loop(0, max(1, key_rows // CHUNK), weigh, 0, unroll=True)

    def score(key, allowed, part, peak):
        scores = mm(key, r.query_t[...])
        result = []
        for j, lanes in enumerate(tiles):
            kept = jnp.where(allowed(lanes), scores[:, lanes], masked_score)
            r.scores[part, lanes] = kept
            result.append(jnp.maximum(peak[j], jnp.max(kept.reshape(-1, 8, LANE), axis=0)))
        return tuple(result)

    no_peak = tuple(jnp.full((8, LANE), masked_score, f32) for _ in tiles)

    def attend(slot):
        spread_ids(r.ids[slot], r.id_columns.at[slot], rows)

        def one(t, peak):
            part = rows_of(t)
            ids = r.id_columns[slot, part, :]
            return score(
                r.kv[slot, part, :HD], lambda lanes: ids == r.query_ids[:1, lanes], part, peak
            )

        absorb(rows, lax.fori_loop(0, chunks, one, no_peak, unroll=True))
        r.mixed_t[...] += mm(r.kv[slot, :, HD:], r.weights[...], TN)

    def arrive(hop, chunk):
        when(hops[hop][4], near_wait(hop, chunk).wait_recv)

    attend(OWN)
    for i, step in enumerate(id_steps):
        when((d - step >= 0) & (d - step < n_dp), remote(
            r.ids.at[OWN], r.ids.at[OWN - step], r.id_send.at[i], r.id_recv.at[i],
            (lax.rem(d + step + n_dp, n_dp), m),
        ).wait_recv)
    for h in first_hops:
        for c in range(chunks):
            arrive(h, c)
            for later in range(len(hops)):
                if hops[later][6] == h:
                    when(hops[later][0], near_copy(later, c).start)
        when(hops[h][4], lambda h=h: attend(hops[h][5]))
    for h in range(len(hops)):
        if hops[h][6] is None:
            continue
        for c in range(chunks):
            arrive(h, c)
            for later in range(len(hops)):
                if hops[later][6] == h:
                    when(hops[later][0], near_copy(later, c).start)
        when(hops[h][4], lambda h=h: attend(hops[h][5]))

    def wide_arrive(k, _):
        wide_copy(k, lax.rem(d - k + n_dp, n_dp)).wait_recv()
        return 0

    lax.fori_loop(1, n_dp, wide_arrive, 0)
    wide_rows = 8 * n_dp
    key = r.wide[:, :HD].astype(bf16)
    held = r.wide[:, 2 * HD:] > 0.5
    absorb_wide = score(
        key, lambda lanes: held & (r.query_ids[:1, lanes] == 0.0), slice(0, wide_rows), no_peak
    )
    absorb(wide_rows, absorb_wide)
    r.mixed_t[...] += mm(r.wide[:, HD:2 * HD].astype(bf16), r.weights[:wide_rows, :], TN)

    for j, lanes in enumerate(tiles):
        total = jnp.sum(r.total[:, lanes], axis=0, keepdims=True)
        mixed = r.mixed_t[:, lanes] / total
        r.mixed_t[:, lanes] = mixed
        r.log_total[:, lanes] = jnp.broadcast_to(
            r.top[:1, lanes] * EXP2_SCALE + jnp.log2(total), (8, LANE)
        )
        r.mixed[lanes, pl.ds(pl.multiple_of(m * HD, HD), HD)] = mixed.T.astype(bf16)

    def head_lanes(head):
        return pl.ds(pl.multiple_of(head * HD, HD), HD)

    def line_copy(way, k, block, device):
        return remote(
            r.mixed.at[:, head_lanes(block)], r.mixed.at[:, head_lanes(block)],
            r.line_send.at[way, k], r.line_recv.at[way, k], (d, device),
        )

    for k in range(n_mp - 1):
        for way, turn in ((0, 1), (1, -1)):
            to, block = m + turn, m - turn * k
            when(
                (to >= 0) & (to < n_mp) & (block >= 0) & (block < n_mp),
                line_copy(way, k, lax.rem(block + n_mp, n_mp), lax.rem(to + n_mp, n_mp)).start,
            )
        for way, turn in ((0, 1), (1, -1)):
            block = m - turn * (k + 1)
            when(
                (block >= 0) & (block < n_mp),
                line_copy(way, k, lax.rem(block + n_mp, n_mp), m).wait_recv,
            )
    for k in range(n_mp - 1):
        for way, turn in ((0, 1), (1, -1)):
            to, block = m + turn, m - turn * k
            when(
                (to >= 0) & (to < n_mp) & (block >= 0) & (block < n_mp),
                line_copy(way, k, lax.rem(block + n_mp, n_mp), lax.rem(to + n_mp, n_mp)).wait_send,
            )
    for h in range(len(hops)):
        for c in range(chunks):
            when(hops[h][0], near_copy(h, c).wait_send)
    for i, step in enumerate(id_steps):
        when((d + step >= 0) & (d + step < n_dp), id_copy(i, step).wait_send)

    def wide_sent(k, _):
        wide_copy(k, d).wait_send()
        return 0

    lax.fori_loop(1, n_dp, wide_sent, 0)


def attention_scratch(n_dp, n_mp, rows):
    chunks = rows // CHUNK
    dma = pltpu.SemaphoreType.DMA
    return dict(
        ids=pltpu.VMEM((SLOTS, 1, rows), f32),
        query_ids=pltpu.VMEM((8, rows), f32),
        id_columns=pltpu.VMEM((SLOTS, rows, LANE), f32),
        qkv_weight=pltpu.VMEM((512, 3 * HD), bf16),
        kv=pltpu.VMEM((SLOTS, rows, 2 * HD), bf16),
        query_t=pltpu.VMEM((HD, rows), bf16),
        wide=pltpu.VMEM((8 * n_dp, 3 * HD), f32),
        top=pltpu.VMEM((8, rows), f32),
        total=pltpu.VMEM((8, rows), f32),
        scores=pltpu.VMEM((rows, rows), f32),
        weights=pltpu.VMEM((rows, rows), bf16),
        kv_send=dma((5, chunks)),
        kv_recv=dma((5, chunks)),
        id_send=dma((4,)),
        id_recv=dma((4,)),
        wide_send=dma((n_dp,)),
        wide_recv=dma((n_dp,)),
        line_send=dma((2, n_mp)),
        line_recv=dma((2, n_mp)),
    )


def attention_forward(n_dp, n_mp, args):
    rows, width = args["row_input"].shape
    names = tuple(args)
    outs = dict(
        normed=((rows, width), bf16), query=((rows, HD), bf16), mixed=((rows, width), bf16),
        mixed_t=((HD, rows), f32), log_total=((8, rows), f32), kv=((SLOTS, rows, 2 * HD), bf16),
    )
    scratch = attention_scratch(n_dp, n_mp, rows)
    scratch = {k: v for k, v in scratch.items() if k not in outs}

    def kernel(*refs):
        r = types.SimpleNamespace(**dict(zip(names + tuple(outs) + tuple(scratch), refs)))
        phase_attention_forward(r, n_dp, n_mp, rows)

    vmem = pl.BlockSpec(memory_space=pltpu.VMEM)
    result = pl.pallas_call(
        kernel,
        out_shape=[jax.ShapeDtypeStruct(*v) for v in outs.values()],
        in_specs=[vmem] * len(names),
        out_specs=[vmem] * len(outs),
        scratch_shapes=list(scratch.values()),
        compiler_params=pltpu.CompilerParams(
            collective_id=0, has_side_effects=True, vmem_limit_bytes=56 * 1024 * 1024),
        name="attention_forward",
    )(*args.values())
    return dict(zip(outs, result))


def layer_norm(values_in, gain_in, shift_in):
    average = jnp.mean(values_in, axis=-1, keepdims=True)
    centred = values_in - average
    spread = jnp.mean(centred * centred, axis=-1, keepdims=True)
    return centred * lax.rsqrt(spread + norm_eps) * gain_in + shift_in


def gelu_exact(values_in):
    return 0.5 * values_in * (1.0 + lax.erf(values_in * 2.0 ** (-0.5)))


def matmul(left_side, right_side):
    return jnp.dot(left_side, right_side, preferred_element_type=jnp.float32)


def matmul_tn(left_side, right_side):
    return lax.dot_general(
        left_side, right_side, (((0,), (0,)), ((), ())), preferred_element_type=jnp.float32
    )


def matmul_nt(left_side, right_side):
    return lax.dot_general(
        left_side, right_side, (((1,), (1,)), ((), ())), preferred_element_type=jnp.float32
    )


def head_scores(query_heads, key_heads, score_scale):
    return (
        jnp.einsum("qhd,khd->hqk", query_heads, key_heads, preferred_element_type=jnp.float32)
        * score_scale
    )


def allowed_pairs(query_tables, key_tables, key_kinds):
    return (query_tables[:, None] == key_tables[None, :]) & (key_kinds[None, :] == 1)


def score_grads(
    query_heads, key_heads, value_heads, grad_heads, allowed, log_rows, delta_rows, score_scale
):
    scores = head_scores(query_heads, key_heads, score_scale)
    probabilities = jnp.where(allowed[None], jnp.exp(scores - log_rows[..., None]), 0.0)
    grad_probs = jnp.einsum(
        "qhd,khd->hqk", grad_heads, value_heads, preferred_element_type=jnp.float32
    )
    grad_scores = (probabilities * (grad_probs - delta_rows[..., None])).astype(jnp.bfloat16)
    return (probabilities, grad_scores)


def shards(
    n_dp,
    n_mp,
    row_input,
    first_gain,
    first_shift,
    query_weight,
    key_weight,
    value_weight,
    out_weight,
    out_bias,
    second_gain,
    second_shift,
    up_weight,
    up_bias,
    down_weight,
    down_bias,
    row_table,
    row_kind,
    out_grad,
):
    head_dim = HD
    score_scale = HD ** (-0.5)
    row_count = row_input.shape[0]
    local_width = query_weight.shape[1]
    local_heads = local_width // head_dim
    inputs = row_input.astype(jnp.float32)
    got = attention_forward(n_dp, n_mp, dict(
        row_input=row_input, first_gain=first_gain[None], first_shift=first_shift[None],
        query_weight=query_weight, key_weight=key_weight, value_weight=value_weight,
        row_table=row_table[None], row_kind=row_kind[None]))
    normed_low, query = got["normed"], got["query"]
    keys, values_here = got["kv"][OWN, :, :HD], got["kv"][OWN, :, HD:]
    all_keys, all_values, all_tables, all_kinds = (
        lax.all_gather(keys, "dp", axis=0, tiled=True),
        lax.all_gather(values_here, "dp", axis=0, tiled=True),
        lax.all_gather(row_table, "dp", axis=0, tiled=True),
        lax.all_gather(row_kind, "dp", axis=0, tiled=True),
    )
    total_rows = all_keys.shape[0]
    key_span = math.gcd(total_rows, 2048)
    span_count = total_rows // key_span
    query_heads = query.reshape(row_count, local_heads, head_dim)
    key_blocks = (
        all_keys.reshape(span_count, key_span, local_heads, head_dim),
        all_values.reshape(span_count, key_span, local_heads, head_dim),
        all_tables.reshape(span_count, key_span),
        all_kinds.reshape(span_count, key_span),
    )

    log_total = got["log_total"][:1] * math.log(2.0)
    mixed_heads = got["mixed_t"].T.reshape(row_count, local_heads, head_dim)
    mixed_low = lax.dynamic_slice(got["mixed"], (0, HD * lax.axis_index("mp")), (row_count, HD))
    branch = (
        lax.psum(matmul(mixed_low, out_weight).astype(jnp.bfloat16), "mp").astype(jnp.float32)
        + out_bias
    )
    middle = inputs + branch
    normed_mid_low = layer_norm(middle, second_gain, second_shift).astype(jnp.bfloat16)
    upper = matmul(normed_mid_low, up_weight) + up_bias
    active_low = gelu_exact(upper).astype(jnp.bfloat16)
    output = (
        middle
        + lax.psum(matmul(active_low, down_weight).astype(jnp.bfloat16), "mp").astype(jnp.float32)
        + down_bias
    )
    block_output = output.astype(jnp.bfloat16)
    grad_output = out_grad.astype(jnp.float32)
    down_weight_grad = matmul_tn(active_low, out_grad)
    down_bias_grad = jnp.sum(grad_output, axis=0)
    grad_active = matmul_nt(out_grad, down_weight)
    gelu_back = jax.vjp(gelu_exact, upper)[1]
    grad_upper = gelu_back(grad_active)[0].astype(jnp.bfloat16)
    up_weight_grad = matmul_tn(normed_mid_low, grad_upper)
    up_bias_grad = jnp.sum(grad_upper.astype(jnp.float32), axis=0)
    grad_normed_mid = lax.psum(matmul_nt(grad_upper, up_weight).astype(jnp.bfloat16), "mp").astype(
        jnp.float32
    )
    second_back = jax.vjp(layer_norm, middle, second_gain, second_shift)[1]
    grad_middle_part, second_gain_grad, second_shift_grad = second_back(grad_normed_mid)
    grad_middle = grad_output + grad_middle_part
    grad_branch = grad_middle.astype(jnp.bfloat16)
    out_weight_grad = matmul_tn(mixed_low, grad_branch)
    out_bias_grad = jnp.sum(grad_branch.astype(jnp.float32), axis=0)
    grad_mixed_low = matmul_nt(grad_branch, out_weight).astype(jnp.bfloat16)
    grad_heads = grad_mixed_low.reshape(row_count, local_heads, head_dim)
    row_delta = jnp.sum(grad_heads.astype(jnp.float32) * mixed_heads, axis=-1).T
    zero_query = jnp.zeros((row_count, local_heads, head_dim), jnp.float32)

    def grad_step(totals, key_piece):
        allowed = allowed_pairs(row_table, key_piece[2], key_piece[3])
        probabilities, grad_scores = score_grads(
            query_heads,
            key_piece[0],
            key_piece[1],
            grad_heads,
            allowed,
            log_total,
            row_delta,
            score_scale,
        )
        totals = totals + score_scale * jnp.einsum(
            "hqk,khd->qhd", grad_scores, key_piece[0], preferred_element_type=jnp.float32
        )
        grad_key_heads = score_scale * jnp.einsum(
            "hqk,qhd->khd", grad_scores, query_heads, preferred_element_type=jnp.float32
        )
        grad_value_heads = jnp.einsum(
            "hqk,qhd->khd",
            probabilities.astype(jnp.bfloat16),
            grad_heads,
            preferred_element_type=jnp.float32,
        )
        stacked = jnp.concatenate(
            (
                grad_key_heads.reshape(key_span, local_width),
                grad_value_heads.reshape(key_span, local_width),
            ),
            axis=1,
        )
        return (totals, stacked)

    grad_query, key_terms = lax.scan(grad_step, zero_query, key_blocks)
    key_terms = key_terms.reshape(total_rows, 2 * local_width)
    own_terms = lax.psum_scatter(key_terms, "dp", scatter_dimension=0, tiled=True)
    grad_query_low = grad_query.reshape(row_count, local_width).astype(jnp.bfloat16)
    grad_keys_low = own_terms[:, :local_width].astype(jnp.bfloat16)
    grad_values_low = own_terms[:, local_width:].astype(jnp.bfloat16)
    query_weight_grad = matmul_tn(normed_low, grad_query_low)
    key_weight_grad = matmul_tn(normed_low, grad_keys_low)
    value_weight_grad = matmul_tn(normed_low, grad_values_low)
    grad_normed_part = (
        matmul_nt(grad_query_low, query_weight)
        + matmul_nt(grad_keys_low, key_weight)
        + matmul_nt(grad_values_low, value_weight)
    )
    grad_normed = lax.psum(grad_normed_part.astype(jnp.bfloat16), "mp").astype(jnp.float32)
    first_back = jax.vjp(layer_norm, inputs, first_gain, first_shift)[1]
    grad_input_part, first_gain_grad, first_shift_grad = first_back(grad_normed)
    input_grad = grad_middle + grad_input_part
    summed = lax.psum(
        (
            first_gain_grad,
            first_shift_grad,
            query_weight_grad,
            key_weight_grad,
            value_weight_grad,
            out_weight_grad,
            out_bias_grad,
            second_gain_grad,
            second_shift_grad,
            up_weight_grad,
            up_bias_grad,
            down_weight_grad,
            down_bias_grad,
        ),
        "dp",
    )
    return (
        block_output,
        input_grad,
        summed[0],
        summed[1],
        summed[2],
        summed[3],
        summed[4],
        summed[5],
        summed[6],
        summed[7],
        summed[8],
        summed[9],
        summed[10],
        summed[11],
        summed[12],
    )


def solution(mesh):
    in_specs = (
        P("dp", None),
        P(),
        P(),
        P(None, "mp"),
        P(None, "mp"),
        P(None, "mp"),
        P("mp", None),
        P(),
        P(),
        P(),
        P(None, "mp"),
        P("mp"),
        P("mp", None),
        P(),
        P("dp"),
        P("dp"),
        P("dp", None),
    )
    out_specs = (
        P("dp", None),
        P("dp", None),
        P(),
        P(),
        P(None, "mp"),
        P(None, "mp"),
        P(None, "mp"),
        P("mp", None),
        P(),
        P(),
        P(),
        P(None, "mp"),
        P("mp"),
        P("mp", None),
        P(),
    )
    n_dp, n_mp = mesh.shape["dp"], mesh.shape["mp"]
    return jax.shard_map(lambda *a: shards(n_dp, n_mp, *a), mesh=mesh, in_specs=in_specs, out_specs=out_specs, check_vma=False)
```

```python
import math
import types

import jax
import jax.numpy as jnp
from jax import lax
from jax.experimental import pallas as pl
from jax.experimental.pallas import tpu as pltpu
from jax.sharding import PartitionSpec as P

HD = 128
NEAR = 2
SLOTS = 2 * NEAR + 1
OWN = NEAR
LANE = 128
CHUNK = 128
PIECE = CHUNK // 2
LAG = 1
norm_eps = 1e-05
masked_score = -1e30
f32 = jnp.float32
bf16 = jnp.bfloat16
MESH = pl.DeviceIdType.MESH
SCALE = HD ** (-0.5)
EXP2_SCALE = SCALE * math.log2(math.e)
NN = (((1,), (0,)), ((), ()))
NT = (((1,), (1,)), ((), ()))
TN = (((0,), (0,)), ((), ()))
VECTORS = ("first_gain", "first_shift", "out_bias", "second_gain", "second_shift", "down_bias", "up_bias")


def mm(a, b, dims=NN):
    return lax.dot_general(a, b, dims, preferred_element_type=f32)


def remote(src, dst, send_sem, recv_sem, device):
    return pltpu.make_async_remote_copy(
        src_ref=src, dst_ref=dst, send_sem=send_sem, recv_sem=recv_sem,
        device_id=device, device_id_type=MESH,
    )


def when(cond, action):
    if cond is True:
        action()
    else:
        pl.when(cond)(action)


def both(a, b):
    return b if a is True else (a if b is True else a & b)


def near_hops(n_dp, d):
    if n_dp == 8:
        core, x, y = lax.rem(d, 2), lax.rem(d // 2, 2), d // 4
        other = d + 1 - 2 * core
        beside = d + 2 - 4 * x
        above = d + 4 - 8 * y
        return [
            (True, OWN, other, 1 + 2 * core, True, 3 - 2 * core, other, None),
            (True, OWN, beside, 4 * x, True, 4 - 4 * x, beside, None),
            (core == x, 4 - 4 * x, other, 3 - 2 * x, core != x, 3 - 2 * x, other, 1),
            (x == y, 4 - 4 * y, above, 4 * y, x != y, 4 - 4 * y, above, 1),
            ((x != y) & (core == y), 4 - 4 * y, other, 3 - 2 * y,
             (x != y) & (core != y), 3 - 2 * y, other, 3),
        ]
    hops = []
    for step in (1, -1, 2, -2):
        to, source = d + step, d - step
        hops.append((
            (to >= 0) & (to < n_dp), OWN, lax.rem(to + n_dp, n_dp), OWN - step,
            (source >= 0) & (source < n_dp), OWN - step, lax.rem(source + n_dp, n_dp), None,
        ))
    return hops


def entry_barrier(n_dp, n_mp, d, m):
    barrier = pltpu.get_barrier_semaphore()

    def greet_dp(k, _):
        pl.semaphore_signal(barrier, inc=1, device_id=(lax.rem(d + k, n_dp), m), device_id_type=MESH)
        return 0

    lax.fori_loop(1, n_dp, greet_dp, 0)
    for k in range(1, n_mp):
        pl.semaphore_signal(barrier, inc=1, device_id=(d, lax.rem(m + k, n_mp)), device_id_type=MESH)
    pl.semaphore_wait(barrier, n_dp - 1 + n_mp - 1)


def layer_stats(values):
    average = jnp.mean(values, axis=-1, keepdims=True)
    centred = values - average
    spread = jnp.mean(centred * centred, axis=-1, keepdims=True)
    return centred, lax.rsqrt(spread + norm_eps)


def layer_back(grad, gain, centred, scale):
    unit = centred * scale
    scaled = grad * gain
    along = jnp.mean(scaled * unit, axis=-1, keepdims=True)
    level = jnp.mean(scaled, axis=-1, keepdims=True)
    return scale * (scaled - level - unit * along), grad * unit


def gelu_parts(values):
    phi = 0.5 * (1.0 + lax.erf(values * 2.0 ** (-0.5)))
    slope = phi + values * (jnp.exp(values * values * (-0.5)) * (2.0 * math.pi) ** (-0.5))
    return values * phi, slope


def rows_of(index, size=CHUNK):
    return pl.ds(pl.multiple_of(index * size, size), size)


def lanes_of(index, size=HD):
    return pl.ds(pl.multiple_of(index * size, size), size)


def spread_ids(ids_row, out_ref, rows):
    for r in range(rows // LANE):
        part = jnp.broadcast_to(ids_row[:, r * LANE:(r + 1) * LANE], (LANE, LANE))
        out_ref[r * LANE:(r + 1) * LANE, :] = part.T


class Reduction:
    def __init__(self, name, rows, columns, order, n_dp):
        self.name, self.rows, self.columns, self.order = name, rows, columns, order
        self.sizes, self.halves, self.starts = [rows], [], []
        place = 0
        for _ in order:
            size = self.sizes[-1]
            halve = size // 2 >= 16
            sent = size // 2 if halve else size
            self.halves.append(halve)
            self.starts.append(place)
            place += sent
            self.sizes.append(sent)
        self.landing = max(place, 16)
        self.events = 2 * len(order) + 1

    def scratch(self):
        levels = max(len(self.order), 1)
        return {
            self.name + "_out": pltpu.VMEM((self.rows, self.columns), bf16),
            self.name + "_in": pltpu.VMEM((self.landing, self.columns), bf16),
            self.name + "_all": pltpu.VMEM((self.rows, self.columns), bf16),
            self.name + "_send": pltpu.SemaphoreType.DMA((2, levels)),
            self.name + "_recv": pltpu.SemaphoreType.DMA((2, levels)),
        }

    def bind(self, r, value, d, m):
        self.r, self.value, self.d, self.m = r, value, d, m
        self.offsets = [0]
        for bit, halve, size in zip(self.order, self.halves, self.sizes[1:]):
            mine = lax.rem(d // (1 << bit), 2)
            self.offsets.append(self.offsets[-1] + mine * size if halve else self.offsets[-1])

    def ref(self, what):
        return getattr(self.r, self.name + what)

    def part(self, offset, size):
        return pl.ds(offset if isinstance(offset, int) else pl.multiple_of(offset, 16), size)

    def geometry(self, level):
        bit, size = self.order[level], self.sizes[level + 1]
        mine = lax.rem(self.d // (1 << bit), 2)
        partner = self.d + (1 << bit) - (2 << bit) * mine
        kept = self.part(self.offsets[level + 1], size)
        if self.halves[level]:
            given = self.part(self.offsets[level] + (1 - mine) * size, size)
        else:
            given = kept
        return given, kept, (partner, self.m), self.part(self.starts[level], size)

    def down_copy(self, level):
        given, _, device, landing = self.geometry(level)
        return remote(
            self.ref("_out").at[given, :], self.ref("_in").at[landing, :],
            self.ref("_send").at[0, level], self.ref("_recv").at[0, level], device,
        )

    def up_copy(self, level, arriving=False):
        given, kept, device, _ = self.geometry(level)
        rows = given if arriving else kept
        return remote(
            self.ref("_all").at[rows, :], self.ref("_all").at[rows, :],
            self.ref("_send").at[1, level], self.ref("_recv").at[1, level], device,
        )

    def event(self, e):
        levels = len(self.order)
        if 0 < e <= levels:
            level = e - 1
            _, kept, _, landing = self.geometry(level)
            copy = self.down_copy(level)
            copy.wait_send()
            copy.wait_recv()
            mine = self.value[kept, :]
            if not self.halves[level]:
                mine = self.ref("_out")[kept, :].astype(f32)
            self.value[kept, :] = mine + self.ref("_in")[landing, :].astype(f32)
        if e < levels:
            given = self.geometry(e)[0]
            self.ref("_out")[given, :] = self.value[given, :].astype(bf16)
            self.down_copy(e).start()
            return
        if e == levels:
            kept = self.part(self.offsets[-1], self.sizes[-1])
            self.ref("_all")[kept, :] = self.value[kept, :].astype(bf16)
        done = e - levels - 1
        back = [level for level in reversed(range(levels)) if self.halves[level]]
        if 0 <= done < len(back):
            self.up_copy(back[done], True).wait_recv()
            self.up_copy(back[done]).wait_send()
        if done + 1 < len(back):
            self.up_copy(back[done + 1]).start()

    def finished(self):
        return self.ref("_all")[...].astype(f32)


class Fold:
    def __init__(self, name, n_mp, chunks, width):
        self.name, self.n, self.chunks, self.width = name, n_mp, chunks, width
        self.steps = chunks + 2 * (n_mp - 1) * LAG

    def scratch(self):
        dma = pltpu.SemaphoreType.DMA((2, self.chunks))
        return {
            self.name + "_in": pltpu.VMEM((2, self.chunks, PIECE, self.width), bf16),
            self.name + "_sums_send": dma, self.name + "_sums_recv": dma,
            self.name + "_back_send": dma, self.name + "_back_recv": dma,
        }

    def bind(self, r, d, m, terms, result, result_rows, finish):
        self.r, self.d, self.m = r, d, m
        self.terms, self.result, self.result_rows, self.finish = terms, result, result_rows, finish

    def ref(self, what):
        return getattr(self.r, self.name + what)

    def sum_rows(self, c, piece):
        return pl.ds(pl.multiple_of(c * CHUNK + piece * PIECE, PIECE), PIECE)

    def sum_copy(self, c, piece):
        to = self.m + (1 if piece else -1)
        return remote(
            self.terms.at[self.sum_rows(c, piece), :], self.ref("_in").at[piece, c],
            self.ref("_sums_send").at[piece, c], self.ref("_sums_recv").at[piece, c],
            (self.d, lax.rem(to + self.n, self.n)),
        )

    def back_copy(self, c, piece):
        to = self.m + (-1 if piece else 1)
        rows = self.result_rows(c, piece)
        return remote(
            self.result.at[rows, :], self.result.at[rows, :],
            self.ref("_back_send").at[piece, c], self.ref("_back_recv").at[piece, c],
            (self.d, lax.rem(to + self.n, self.n)),
        )

    def step(self, t):
        m, n = self.m, self.n
        for piece in (1, 0):
            far = m if piece else n - 1 - m
            c = t - far * LAG
            first, last = far == 0, far == n - 1
            valid = (c >= 0) & (c < self.chunks)
            c = jnp.clip(c, 0, self.chunks - 1)

            @pl.when(valid & jnp.logical_not(first))
            def _(c=c, piece=piece, last=last):
                self.sum_copy(c, piece).wait_recv()

                @pl.when(jnp.logical_not(last))
                def _():
                    rows = self.sum_rows(c, piece)
                    self.terms[rows, :] = (
                        self.terms[rows, :].astype(f32) + self.ref("_in")[piece, c].astype(f32)
                    ).astype(bf16)

            @pl.when(valid & jnp.logical_not(last))
            def _(c=c, piece=piece):
                self.sum_copy(c, piece).start()

            @pl.when(valid & last)
            def _(c=c, piece=piece):
                total = (
                    self.terms[self.sum_rows(c, piece), :].astype(f32)
                    + self.ref("_in")[piece, c].astype(f32)
                )
                self.finish(c, piece, total)
                self.back_copy(c, piece).start()
        for piece in (1, 0):
            far = n - 1 - m if piece else m
            c = t - (n - 1 + far) * LAG
            valid = (c >= 0) & (c < self.chunks) & (far > 0)
            c = jnp.clip(c, 0, self.chunks - 1)

            @pl.when(valid)
            def _(c=c, piece=piece, far=far):
                self.back_copy(c, piece).wait_recv()

                @pl.when(far < n - 1)
                def _():
                    self.back_copy(c, piece).start()

    def drain(self):
        m, n = self.m, self.n
        for piece in (1, 0):
            far = m if piece else n - 1 - m

            @pl.when(far < n - 1)
            def _(piece=piece):
                for c in range(self.chunks):
                    self.sum_copy(c, piece).wait_send()

            @pl.when(far > 0)
            def _(piece=piece):
                for c in range(self.chunks):
                    self.back_copy(c, piece).wait_send()


def layer_kernel(r, n_dp, n_mp, rows, reductions, folds):
    d, m = lax.axis_index("dp"), lax.axis_index("mp")
    chunks, half = rows // CHUNK, rows // 2
    tiles = [slice(j * LANE, (j + 1) * LANE) for j in range(chunks)]
    hops = near_hops(n_dp, d)
    first_hops = [h for h in range(len(hops)) if hops[h][7] is None]
    later_hops = [h for h in range(len(hops)) if hops[h][7] is not None]
    follow = {h: [k for k in range(len(hops)) if hops[k][7] == h] for h in range(len(hops))}

    def natural(c, piece):
        start = piece * half + c * PIECE
        return pl.ds(start if isinstance(start, int) else pl.multiple_of(start, PIECE), PIECE)

    def held(c, piece):
        return pl.ds(pl.multiple_of(c * CHUNK + piece * PIECE, PIECE), PIECE)

    def fetch(ref, c):
        return jnp.concatenate((ref[natural(c, 0), :], ref[natural(c, 1), :]), axis=0)

    def weight_copy(k, block):
        return remote(
            r.out_all.at[rows_of(block), :], r.out_all.at[rows_of(block), :],
            r.weight_send.at[k], r.weight_recv.at[k], (d, lax.rem(m + k, n_mp)),
        )

    def near_copy(hop, chunk):
        _, source, target, there = hops[hop][:4]
        part = rows_of(chunk)
        return remote(
            r.kv.at[source, part, :], r.kv.at[there, part, :],
            r.kv_send.at[hop, chunk], r.kv_recv.at[hop, chunk], (target, m),
        )

    def near_arrival(hop, chunk):
        part = rows_of(chunk)
        return remote(
            r.kv.at[OWN, part, :], r.kv.at[hops[hop][5], part, :],
            r.kv_send.at[hop, chunk], r.kv_recv.at[hop, chunk], (hops[hop][6], m),
        )

    id_steps = (1, -1, 2, -2)

    def id_copy(i):
        step = id_steps[i]
        return remote(
            r.ids.at[OWN], r.ids.at[OWN - step], r.id_send.at[i], r.id_recv.at[i],
            (lax.rem(d + step + n_dp, n_dp), m),
        )

    def wide_copy(k, source):
        return remote(
            r.wide.at[rows_of(source, 8), :], r.wide.at[rows_of(source, 8), :],
            r.wide_send.at[k], r.wide_recv.at[k], (lax.rem(d + k, n_dp), m),
        )

    r.out_all[rows_of(m), :] = r.out_weight[...]
    r.ids[OWN] = r.row_ids[1:2, :]
    query_ids = r.row_ids[0:1, :]
    r.vec[...] = jnp.zeros_like(r.vec)
    entry_barrier(n_dp, n_mp, d, m)
    for i, step in enumerate(id_steps):
        when((d + step >= 0) & (d + step < n_dp), id_copy(i).start)
    for k in range(1, n_mp):
        weight_copy(k, m).start()

    gain, shift = r.first_gain[...], r.first_shift[...]
    for i, w in enumerate((r.query_weight, r.key_weight, r.value_weight)):
        r.qkv_weight[:, i * HD:(i + 1) * HD] = w[...]
    for c in range(chunks):
        part = slice(c * CHUNK, (c + 1) * CHUNK)
        centred, scale = layer_stats(fetch(r.row_input, c).astype(f32))
        normed = (centred * scale * gain + shift).astype(bf16)
        r.normed[part, :] = normed
        qkv = mm(normed, r.qkv_weight[...])
        r.kv[OWN, part, :] = qkv[:, HD:].astype(bf16)
        for h in first_hops:
            when(hops[h][0], near_copy(h, c).start)
        r.query[part, :] = qkv[:, :HD].astype(bf16)
        r.query_t[:, part] = qkv[:, :HD].T.astype(bf16)
        if c == 0:
            row = lax.broadcasted_iota(jnp.int32, (8, 2 * HD), 0)
            mine = rows_of(d, 8)
            r.wide[mine, :2 * HD] = jnp.where(row == 0, qkv[:8, HD:].astype(bf16).astype(f32), 0.0)
            kind = jnp.broadcast_to(r.row_ids[2:3, :1], (8, HD))
            r.wide[mine, 2 * HD:] = jnp.where(row[:, :HD] == 0, kind, 0.0)

    def wide_start(k, _):
        wide_copy(k, d).start()
        return 0

    lax.fori_loop(1, n_dp, wide_start, 0)

    r.top[...] = jnp.full_like(r.top, masked_score)
    r.total[...] = jnp.zeros_like(r.total)
    r.mixed_t[...] = jnp.zeros_like(r.mixed_t)

    def absorb(key_rows, peak):
        for j, lanes in enumerate(tiles):
            old = r.top[:, lanes]
            new = jnp.maximum(old, jnp.broadcast_to(jnp.max(peak[j], axis=0, keepdims=True), (8, LANE)))
            r.top[:, lanes] = new
            fade = jnp.exp2((old - new) * EXP2_SCALE)
            r.total[:, lanes] = r.total[:, lanes] * fade
            r.mixed_t[:, lanes] = r.mixed_t[:, lanes] * fade[:1, :]

        def weigh(t, _):
            size = min(key_rows, CHUNK)
            part = rows_of(t, size)
            for lanes in tiles:
                weight = jnp.exp2((r.scores[part, lanes] - r.top[:1, lanes]) * EXP2_SCALE)
                r.total[:, lanes] += jnp.sum(weight.reshape(size // 8, 8, LANE), axis=0)
                r.weights[part, lanes] = weight.astype(bf16)
            return 0

        lax.fori_loop(0, max(1, key_rows // CHUNK), weigh, 0, unroll=True)

    def score(key, allowed, part, peak):
        scores = mm(key, r.query_t[...])
        result = []
        for j, lanes in enumerate(tiles):
            kept = jnp.where(allowed(lanes), scores[:, lanes], masked_score)
            r.scores[part, lanes] = kept
            result.append(jnp.maximum(peak[j], jnp.max(kept.reshape(-1, 8, LANE), axis=0)))
        return tuple(result)

    no_peak = tuple(jnp.full((8, LANE), masked_score, f32) for _ in tiles)

    def attend(slot):
        spread_ids(r.ids[slot], r.id_columns.at[slot], rows)

        def one(t, peak):
            part = rows_of(t)
            ids = r.id_columns[slot, part, :]
            return score(
                r.kv[slot, part, :HD], lambda lanes: ids == query_ids[:, lanes], part, peak
            )

        absorb(rows, lax.fori_loop(0, chunks, one, no_peak, unroll=True))
        r.mixed_t[...] += mm(r.kv[slot, :, HD:], r.weights[...], TN)

    attend(OWN)
    for c in range(chunks):
        r.out_grad_held[c * CHUNK:(c + 1) * CHUNK, :] = fetch(r.out_grad, c)
    r.grad_active[...] = mm(r.out_grad_held[...], r.down_weight[...], NT)
    r.up_weight_t[...] = r.up_weight[...].T
    r.qkv_weight_t[...] = r.qkv_weight[...].T
    for i, step in enumerate(id_steps):
        when((d - step >= 0) & (d - step < n_dp), id_copy(i).wait_recv)
    for h in first_hops + later_hops:
        for c in range(chunks):
            when(hops[h][4], near_arrival(h, c).wait_recv)
            for later in follow[h]:
                when(hops[later][0], near_copy(later, c).start)
        when(hops[h][4], lambda h=h: attend(hops[h][5]))

    def wide_arrive(k, _):
        wide_copy(k, lax.rem(d - k + n_dp, n_dp)).wait_recv()
        return 0

    lax.fori_loop(1, n_dp, wide_arrive, 0)
    wide_rows = 8 * n_dp

    def wide_allowed(lanes):
        return (r.wide[:, 2 * HD:] > 0.5) & (query_ids[:, lanes] == 0.0)

    absorb(wide_rows, score(r.wide[:, :HD].astype(bf16), wide_allowed, slice(0, wide_rows), no_peak))
    r.mixed_t[...] += mm(r.wide[:, HD:2 * HD].astype(bf16), r.weights[:wide_rows, :], TN)

    for j, lanes in enumerate(tiles):
        total = jnp.sum(r.total[:, lanes], axis=0, keepdims=True)
        mixed = r.mixed_t[:, lanes] / total
        r.mixed_t[:, lanes] = mixed
        r.log_total[:, lanes] = jnp.broadcast_to(
            r.top[:1, lanes] * EXP2_SCALE + jnp.log2(total), (8, LANE)
        )
        r.mixed[lanes, lanes_of(m)] = mixed.T.astype(bf16)

    def head_copy(way, block, c):
        to = m + (1 if way == 0 else -1)
        distance = m - block if way == 0 else block - m
        at = r.mixed.at[rows_of(c), lanes_of(lax.rem(block + n_mp, n_mp))]
        return remote(
            at, at, r.head_send.at[way, distance, c], r.head_recv.at[way, distance, c],
            (d, lax.rem(to + n_mp, n_mp)),
        )

    def head_arrival(way, block, c):
        distance = (m - block if way == 0 else block - m) - 1
        at = r.mixed.at[rows_of(c), lanes_of(lax.rem(block + n_mp, n_mp))]
        return remote(
            at, at, r.head_send.at[way, distance, c], r.head_recv.at[way, distance, c], (d, m),
        )

    def head_step(s):
        c = jnp.clip(s, 0, chunks - 1)
        for way in (0, 1):
            room = m + 1 < n_mp if way == 0 else m > 0

            @pl.when((s < chunks) & room)
            def _(way=way):
                head_copy(way, m, c).start()
        for distance in range(1, n_mp):
            t = s - distance * LAG
            valid = (t >= 0) & (t < chunks)
            t = jnp.clip(t, 0, chunks - 1)
            for way in (0, 1):
                block = m - distance if way == 0 else m + distance
                room = m + 1 < n_mp if way == 0 else m > 0

                @pl.when(valid & (block >= 0) & (block < n_mp))
                def _(way=way, block=block, t=t, room=room):
                    head_arrival(way, block, t).wait_recv()

                    @pl.when(room)
                    def _():
                        head_copy(way, block, t).start()

    def add_vector(name, values):
        i = VECTORS.index(name)
        r.vec[i] += jnp.sum(values.reshape(-1, 8, values.shape[-1]), axis=0)

    def feed_forward(c):
        part = rows_of(c)
        branch = mm(r.mixed[part, :], r.out_all[...]) + r.out_bias[...]
        middle = fetch(r.row_input, c).astype(f32) + branch
        r.middle[part, :] = middle
        centred, scale = layer_stats(middle)
        normed = (centred * scale * r.second_gain[...] + r.second_shift[...]).astype(bf16)
        r.normed_mid[part, :] = normed
        active, slope = gelu_parts(mm(normed, r.up_weight[...]) + r.up_bias[...])
        active = active.astype(bf16)
        r.active[part, :] = active
        grad_upper = (slope * r.grad_active[part, :]).astype(bf16)
        r.grad_upper[part, :] = grad_upper
        add_vector("up_bias", grad_upper.astype(f32))
        r.mid_terms[part, :] = mm(grad_upper, r.up_weight_t[...]).astype(bf16)
        r.out_terms[part, :] = mm(active, r.down_weight[...]).astype(bf16)

    def finish_mid(c, piece, grad):
        centred, scale = layer_stats(r.middle[held(c, piece), :])
        back, gain_terms = layer_back(grad, r.second_gain[...], centred, scale)
        grad_middle = r.out_grad[natural(c, piece), :].astype(f32) + back
        r.grad_middle[held(c, piece), :] = grad_middle
        branch = grad_middle.astype(bf16)
        r.grad_branch[held(c, piece), :] = branch
        add_vector("second_gain", gain_terms)
        add_vector("second_shift", grad)
        add_vector("out_bias", branch.astype(f32))

    def finish_out(c, piece, total):
        r.block_output[natural(c, piece), :] = (
            r.middle[held(c, piece), :] + total + r.down_bias[...]
        ).astype(bf16)

    def finish_first(c, piece, grad):
        centred, scale = layer_stats(r.row_input[natural(c, piece), :].astype(f32))
        back, gain_terms = layer_back(grad, r.first_gain[...], centred, scale)
        r.grad_low[natural(c, piece), :] = (r.grad_middle[held(c, piece), :] + back).astype(bf16)
        add_vector("first_gain", gain_terms)
        add_vector("first_shift", grad)

    fold_mid, fold_out, fold_first = folds
    fold_mid.bind(r, d, m, r.mid_terms, r.grad_branch, held, finish_mid)
    fold_out.bind(r, d, m, r.out_terms, r.block_output, natural, finish_out)
    fold_first.bind(r, d, m, r.first_terms, r.grad_low, natural, finish_first)
    up_sum, down_sum, out_sum, qkv_sum = reductions
    up_sum.bind(r, r.up_weight_sum, d, m)
    down_sum.bind(r, r.down_weight_sum, d, m)
    out_sum.bind(r, r.out_weight_sum, d, m)
    qkv_sum.bind(r, r.qkv_weight_sum, d, m)

    def down_weight_grad():
        r.down_weight_sum[...] = mm(r.active[...], r.out_grad_held[...], TN)

    def up_weight_grad():
        r.up_weight_sum[...] = mm(r.normed_mid[...], r.grad_upper[...], TN)

    queue = [down_weight_grad, up_weight_grad]
    for e in range(up_sum.events):
        queue.append(lambda e=e: down_sum.event(e))
        queue.append(lambda e=e: up_sum.event(e))

    for k in range(1, n_mp):
        weight_copy(k, lax.rem(m - k + n_mp, n_mp)).wait_recv()
    feed_from = (n_mp - 1) * LAG
    steps = feed_from + fold_mid.steps

    def middle_step(s, _):
        head_step(s)
        c = s - feed_from
        valid = (c >= 0) & (c < chunks)

        @pl.when(valid)
        def _():
            feed_forward(c)

        fold_mid.step(s - feed_from)
        return 0

    lax.fori_loop(0, feed_from + chunks, middle_step, 0)

    def late_step(s, _):
        fold_mid.step(s)
        return 0

    for s in range(chunks, fold_mid.steps):
        fold_mid.step(jnp.int32(s))
        for _ in range(2):
            if queue:
                queue.pop(0)()

    for c in range(chunks):
        part = slice(c * CHUNK, (c + 1) * CHUNK)
        grad = mm(r.grad_branch[part, :], r.out_weight[...], NT)
        low = grad.astype(bf16)
        r.grad_heads[part, :] = low
        turned = grad.T.astype(bf16)
        r.grad_heads_t[:, part] = turned
        r.row_delta[:, part] = jnp.broadcast_to(
            jnp.sum(turned.astype(f32) * r.mixed_t[:, part], axis=0, keepdims=True), (8, LANE)
        )
    r.out_weight_sum[...] = mm(r.mixed[:, lanes_of(m)], r.grad_branch[...], TN)
    for e in range(out_sum.events):
        queue.append(lambda e=e: out_sum.event(e))
    r.grad_query_t[...] = jnp.zeros_like(r.grad_query_t)

    def score_back(key, value, allowed, size):
        scores = mm(key, r.query_t[...])
        grad_probs = mm(value, r.grad_heads_t[...])
        probs, grads = [], []
        for lanes in tiles:
            prob = jnp.exp2(scores[:, lanes] * EXP2_SCALE - r.log_total[:1, lanes])
            prob = jnp.where(allowed(lanes), prob, 0.0)
            probs.append(prob.astype(bf16))
            grads.append((prob * (grad_probs[:, lanes] - r.row_delta[:1, lanes])).astype(bf16))
        probs, grads = jnp.concatenate(probs, axis=1), jnp.concatenate(grads, axis=1)
        r.grad_query_t[...] += mm(key, grads, TN)
        return mm(grads, r.query[...]) * SCALE, mm(probs, r.grad_heads[...])

    def attend_back(slot, store):
        def one(t, _):
            part = rows_of(t)
            ids = r.id_columns[slot, part, :]
            key_grad, value_grad = score_back(
                r.kv[slot, part, :HD], r.kv[slot, part, HD:],
                lambda lanes: ids == query_ids[:, lanes], CHUNK,
            )
            store(part, key_grad, value_grad)
            return 0

        lax.fori_loop(0, chunks, one, 0)

    def store_terms(slot):
        def store(part, key_grad, value_grad):
            r.kv_terms[slot, part, :HD] = key_grad.astype(bf16)
            r.kv_terms[slot, part, HD:] = value_grad.astype(bf16)
        return store

    def store_own(part, key_grad, value_grad):
        r.kv_grad[part, :HD] = key_grad
        r.kv_grad[part, HD:] = value_grad

    def back_copy(hop, chunk):
        part = rows_of(chunk)
        return remote(
            r.kv_terms.at[hops[hop][5], part, :], r.kv_back.at[hop, part, :],
            r.back_send.at[hop, chunk], r.back_recv.at[hop, chunk], (hops[hop][6], m),
        )

    def add_back(hop, chunk):
        part = rows_of(chunk)
        back_copy(hop, chunk).wait_recv()
        slot = hops[hop][1]
        r.kv_terms[slot, part, :] = (
            r.kv_terms[slot, part, :].astype(f32) + r.kv_back[hop, part, :].astype(f32)
        ).astype(bf16)

    out_steps = list(range(fold_out.steps))

    def side_work(count):
        for _ in range(count):
            if out_steps:
                fold_out.step(jnp.int32(out_steps.pop(0)))
            if queue:
                queue.pop(0)()

    for h in reversed(first_hops + later_hops):
        when(hops[h][4], lambda h=h: attend_back(hops[h][5], store_terms(hops[h][5])))
        for c in range(chunks):
            for later in follow[h]:
                when(hops[later][0], lambda later=later, c=c: add_back(later, c))
            when(hops[h][4], back_copy(h, c).start)
        side_work(2)
    attend_back(OWN, store_own)
    wide_key, wide_value = score_back(
        r.wide[:, :HD].astype(bf16), r.wide[:, HD:2 * HD].astype(bf16), wide_allowed, wide_rows
    )
    r.wide_terms[:, :HD] = wide_key
    r.wide_terms[:, HD:] = wide_value

    def wide_back_copy(k, target, source):
        return remote(
            r.wide_terms.at[rows_of(target, 8), :], r.wide_back.at[source],
            r.wide_back_send.at[k], r.wide_back_recv.at[k], (target, m),
        )

    def wide_back_start(k, _):
        wide_back_copy(k, lax.rem(d + k, n_dp), d).start()
        return 0

    def wide_back_arrive(k, _):
        wide_back_copy(k, lax.rem(d + k, n_dp), lax.rem(d - k + n_dp, n_dp)).wait_recv()
        return 0

    lax.fori_loop(1, n_dp, wide_back_start, 0)
    r.wide_back[d] = r.wide_terms[rows_of(d, 8), :]
    side_work(4)
    lax.fori_loop(1, n_dp, wide_back_arrive, 0)
    r.kv_grad[:8, :] += jnp.sum(r.wide_back[...], axis=0)
    for c in range(chunks):
        part = slice(c * CHUNK, (c + 1) * CHUNK)
        r.qkv_grad[part, :HD] = (r.grad_query_t[:, part].T * SCALE).astype(bf16)
    while out_steps or queue:
        side_work(1)

    def last_step(s, _):
        @pl.when(s < chunks)
        def _():
            c = jnp.clip(s, 0, chunks - 1)
            part = rows_of(c)
            total = r.kv_grad[part, :]
            for h in first_hops:
                @pl.when(True if hops[h][0] is True else hops[h][0])
                def _(h=h):
                    back_copy(h, c).wait_recv()
                    r.kv_grad[part, :] += r.kv_back[h, part, :].astype(f32)
            r.qkv_grad[part, HD:] = r.kv_grad[part, :].astype(bf16)
            r.first_terms[part, :] = mm(r.qkv_grad[part, :], r.qkv_weight_t[...]).astype(bf16)

        fold_first.step(s)
        return 0

    lax.fori_loop(0, chunks, last_step, 0)
    r.qkv_weight_sum[...] = mm(r.normed[...], r.qkv_grad[...], TN)
    for e in range(qkv_sum.events):
        queue.append(lambda e=e: qkv_sum.event(e))
    for s in range(chunks, fold_first.steps):
        fold_first.step(jnp.int32(s))
        if queue:
            queue.pop(0)()
    while queue:
        queue.pop(0)()

    share = rows // n_mp
    mine = r.out_grad[pl.ds(pl.multiple_of(m * share, 16), share), :].astype(f32)
    add_vector("down_bias", mine)
    for i in range(len(VECTORS)):
        r.line_vec[m, i:i + 1, :] = jnp.sum(r.vec[i], axis=0, keepdims=True)
    r.line_vec[m, len(VECTORS):, :] = jnp.zeros_like(r.line_vec[m, len(VECTORS):, :])

    def line_vec_copy(k, block):
        return remote(
            r.line_vec.at[block], r.line_vec.at[block],
            r.line_vec_send.at[k], r.line_vec_recv.at[k], (d, lax.rem(m + k, n_mp)),
        )

    for k in range(1, n_mp):
        line_vec_copy(k, m).start()
    for k in range(1, n_mp):
        line_vec_copy(k, lax.rem(m - k + n_mp, n_mp)).wait_recv()
    summed = r.line_vec[0]
    for k in range(1, n_mp):
        summed = summed + r.line_vec[k]
    row = lax.broadcasted_iota(jnp.int32, summed.shape, 0)
    r.all_vec[d] = jnp.where(row == VECTORS.index("up_bias"), r.line_vec[m], summed)

    def all_vec_copy(k, block):
        return remote(
            r.all_vec.at[block], r.all_vec.at[block],
            r.all_vec_send.at[k], r.all_vec_recv.at[k], (lax.rem(d + k, n_dp), m),
        )

    def all_vec_start(k, _):
        all_vec_copy(k, d).start()
        return 0

    def all_vec_arrive(k, _):
        all_vec_copy(k, lax.rem(d - k + n_dp, n_dp)).wait_recv()
        return 0

    lax.fori_loop(1, n_dp, all_vec_start, 0)
    r.input_grad[...] = r.grad_low[...].astype(f32)
    r.up_weight_grad[...] = up_sum.finished()
    r.down_weight_grad[...] = down_sum.finished()
    r.out_weight_grad[...] = out_sum.finished()
    qkv = qkv_sum.finished()
    r.query_weight_grad[...] = qkv[:, :HD]
    r.key_weight_grad[...] = qkv[:, HD:2 * HD]
    r.value_weight_grad[...] = qkv[:, 2 * HD:]
    lax.fori_loop(1, n_dp, all_vec_arrive, 0)
    r.vectors[...] = jnp.sum(r.all_vec[...], axis=0)

    for k in range(1, n_mp):
        weight_copy(k, m).wait_send()
        line_vec_copy(k, m).wait_send()
    for h in range(len(hops)):
        for c in range(chunks):
            when(hops[h][0], near_copy(h, c).wait_send)
            when(hops[h][4], back_copy(h, c).wait_send)
    for i, step in enumerate(id_steps):
        when((d + step >= 0) & (d + step < n_dp), id_copy(i).wait_send)
    for way in (0, 1):
        room = m + 1 < n_mp if way == 0 else m > 0
        for distance in range(n_mp - 1):
            block = m - distance if way == 0 else m + distance

            @pl.when(room & (block >= 0) & (block < n_mp))
            def _(way=way, block=block):
                for c in range(chunks):
                    head_copy(way, block, c).wait_send()
    for fold in folds:
        fold.drain()

    def sent(k, _):
        wide_copy(k, d).wait_send()
        wide_back_copy(k, lax.rem(d + k, n_dp), d).wait_send()
        all_vec_copy(k, d).wait_send()
        return 0

    lax.fori_loop(1, n_dp, sent, 0)


def layer(n_dp, n_mp, args):
    rows, width = args["row_input"].shape
    hidden = args["up_weight"].shape[1]
    chunks = rows // CHUNK
    names = tuple(args)
    outs = dict(
        block_output=((rows, width), bf16), input_grad=((rows, width), f32),
        query_weight_grad=((width, HD), f32), key_weight_grad=((width, HD), f32),
        value_weight_grad=((width, HD), f32), out_weight_grad=((HD, width), f32),
        up_weight_grad=((width, hidden), f32), down_weight_grad=((hidden, width), f32),
        vectors=((8, width), f32),
    )
    bits = tuple(range(n_dp.bit_length() - 1))
    turned = bits[:1] + bits[:0:-1]
    reductions = (
        Reduction("up_sum", width, hidden, bits, n_dp),
        Reduction("down_sum", hidden, width, turned, n_dp),
        Reduction("out_sum", HD, width, turned, n_dp),
        Reduction("qkv_sum", width, 3 * HD, bits, n_dp),
    )
    folds = tuple(Fold(name, n_mp, chunks, width) for name in ("fold_mid", "fold_out", "fold_first"))
    dma = pltpu.SemaphoreType.DMA
    v = pltpu.VMEM
    scratch = dict(
        normed=v((rows, width), bf16), query=v((rows, HD), bf16), query_t=v((HD, rows), bf16),
        mixed=v((rows, width), bf16), mixed_t=v((HD, rows), f32), log_total=v((8, rows), f32),
        ids=v((SLOTS, 1, rows), f32), id_columns=v((SLOTS, rows, LANE), f32),
        qkv_weight=v((width, 3 * HD), bf16), qkv_weight_t=v((3 * HD, width), bf16),
        up_weight_t=v((hidden, width), bf16), out_all=v((width, width), bf16),
        kv=v((SLOTS, rows, 2 * HD), bf16), kv_terms=v((SLOTS, rows, 2 * HD), bf16),
        kv_back=v((5, rows, 2 * HD), bf16), kv_grad=v((rows, 2 * HD), f32),
        wide=v((8 * n_dp, 3 * HD), f32), wide_terms=v((8 * n_dp, 2 * HD), f32),
        wide_back=v((n_dp, 8, 2 * HD), f32),
        top=v((8, rows), f32), total=v((8, rows), f32),
        scores=v((rows, rows), f32), weights=v((rows, rows), bf16),
        out_grad_held=v((rows, width), bf16), grad_active=v((rows, hidden), f32),
        middle=v((rows, width), f32), normed_mid=v((rows, width), bf16),
        active=v((rows, hidden), bf16), grad_upper=v((rows, hidden), bf16),
        mid_terms=v((rows, width), bf16), out_terms=v((rows, width), bf16),
        first_terms=v((rows, width), bf16), grad_middle=v((rows, width), f32),
        grad_branch=v((rows, width), bf16), grad_low=v((rows, width), bf16),
        grad_heads=v((rows, HD), bf16), grad_heads_t=v((HD, rows), bf16),
        row_delta=v((8, rows), f32), grad_query_t=v((HD, rows), f32),
        qkv_grad=v((rows, 3 * HD), bf16),
        up_weight_sum=v((width, hidden), f32), down_weight_sum=v((hidden, width), f32),
        out_weight_sum=v((HD, width), f32), qkv_weight_sum=v((width, 3 * HD), f32),
        vec=v((len(VECTORS), 8, width), f32), line_vec=v((n_mp, 8, width), f32),
        all_vec=v((n_dp, 8, width), f32),
        kv_send=dma((5, chunks)), kv_recv=dma((5, chunks)),
        back_send=dma((5, chunks)), back_recv=dma((5, chunks)),
        id_send=dma((4,)), id_recv=dma((4,)),
        weight_send=dma((n_mp,)), weight_recv=dma((n_mp,)),
        wide_send=dma((n_dp,)), wide_recv=dma((n_dp,)),
        wide_back_send=dma((n_dp,)), wide_back_recv=dma((n_dp,)),
        head_send=dma((2, n_mp, chunks)), head_recv=dma((2, n_mp, chunks)),
        line_vec_send=dma((n_mp,)), line_vec_recv=dma((n_mp,)),
        all_vec_send=dma((n_dp,)), all_vec_recv=dma((n_dp,)),
    )
    for part in reductions + folds:
        scratch.update(part.scratch())

    def kernel(*refs):
        r = types.SimpleNamespace(**dict(zip(names + tuple(outs) + tuple(scratch), refs)))
        layer_kernel(r, n_dp, n_mp, rows, reductions, folds)

    vmem = pl.BlockSpec(memory_space=pltpu.VMEM)
    result = pl.pallas_call(
        kernel,
        out_shape=[jax.ShapeDtypeStruct(*o) for o in outs.values()],
        in_specs=[vmem] * len(names),
        out_specs=[vmem] * len(outs),
        scratch_shapes=list(scratch.values()),
        compiler_params=pltpu.CompilerParams(
            collective_id=0, has_side_effects=True, vmem_limit_bytes=58 * 1024 * 1024),
        name="layer",
    )(*args.values())
    return dict(zip(outs, result))


def shards(
    n_dp, n_mp, row_input, first_gain, first_shift, query_weight, key_weight, value_weight,
    out_weight, out_bias, second_gain, second_shift, up_weight, up_bias, down_weight, down_bias,
    row_table, row_kind, out_grad,
):
    rows = row_input.shape[0]

    def spread(values):
        return values.reshape(2, rows // CHUNK, PIECE).transpose(1, 0, 2).reshape(1, rows)

    support = row_kind == 1
    ids = jnp.where(support & (row_table != 0), row_table, -1)
    wide = jnp.where(support & (row_table == 0), 1, 0)
    row_ids = jnp.concatenate(
        [spread(v.astype(f32)) for v in (row_table, ids, wide)] + [jnp.zeros((5, rows), f32)]
    )
    got = layer(n_dp, n_mp, dict(
        row_input=row_input, first_gain=first_gain[None], first_shift=first_shift[None],
        query_weight=query_weight, key_weight=key_weight, value_weight=value_weight,
        out_weight=out_weight, out_bias=out_bias[None], second_gain=second_gain[None],
        second_shift=second_shift[None], up_weight=up_weight, up_bias=up_bias[None],
        down_weight=down_weight, down_bias=down_bias[None], row_ids=row_ids, out_grad=out_grad,
    ))
    vector = {name: got["vectors"][i] for i, name in enumerate(VECTORS)}
    return (
        got["block_output"], got["input_grad"], vector["first_gain"], vector["first_shift"],
        got["query_weight_grad"], got["key_weight_grad"], got["value_weight_grad"],
        got["out_weight_grad"], vector["out_bias"], vector["second_gain"], vector["second_shift"],
        got["up_weight_grad"], vector["up_bias"], got["down_weight_grad"], vector["down_bias"],
    )


def solution(mesh):
    n_dp, n_mp = mesh.shape["dp"], mesh.shape["mp"]
    in_specs = (
        P("dp", None), P(), P(), P(None, "mp"), P(None, "mp"), P(None, "mp"), P("mp", None),
        P(), P(), P(), P(None, "mp"), P("mp"), P("mp", None), P(), P("dp"), P("dp"), P("dp", None),
    )
    out_specs = (
        P("dp", None), P("dp", None), P(), P(), P(None, "mp"), P(None, "mp"), P(None, "mp"),
        P("mp", None), P(), P(), P(), P(None, "mp"), P("mp"), P("mp", None), P(),
    )
    return jax.shard_map(
        lambda *a: shards(n_dp, n_mp, *a), mesh=mesh, in_specs=in_specs, out_specs=out_specs,
        check_vma=False,
    )
```

```python
import math
import types

import jax
import jax.numpy as jnp
from jax import lax
from jax.experimental import pallas as pl
from jax.experimental.pallas import tpu as pltpu
from jax.sharding import PartitionSpec as P

HD = 128
NEAR = 2
SLOTS = 2 * NEAR + 1
OWN = NEAR
LANE = 128
CHUNK = 128
SUB = 2
PART = CHUNK // SUB
HEAD_LAG = 1
LAG = 2
norm_eps = 1e-05
masked_score = -1e30
f32 = jnp.float32
bf16 = jnp.bfloat16
MESH = pl.DeviceIdType.MESH
SCALE = HD ** (-0.5)
EXP2_SCALE = SCALE * math.log2(math.e)
NN = (((1,), (0,)), ((), ()))
NT = (((1,), (1,)), ((), ()))
TN = (((0,), (0,)), ((), ()))
RESULTS = ("block_output", "grad_low", "up_sum_all", "down_sum_all", "out_sum_all", "qkv_sum_all", "vectors")
VECTORS = ("first_gain", "first_shift", "out_bias", "second_gain", "second_shift", "down_bias", "up_bias")


def mm(a, b, dims=NN):
    return lax.dot_general(a, b, dims, preferred_element_type=f32)


def remote(src, dst, send_sem, recv_sem, device):
    return pltpu.make_async_remote_copy(
        src_ref=src, dst_ref=dst, send_sem=send_sem, recv_sem=recv_sem,
        device_id=device, device_id_type=MESH,
    )


def when(cond, action):
    if cond is True:
        action()
    else:
        pl.when(cond)(action)


def both(a, b):
    return b if a is True else (a if b is True else a & b)


def near_hops(n_dp, d):
    if n_dp == 8:
        core, x, y = lax.rem(d, 2), lax.rem(d // 2, 2), d // 4
        other = d + 1 - 2 * core
        beside = d + 2 - 4 * x
        above = d + 4 - 8 * y
        return [
            (True, OWN, other, 1 + 2 * core, True, 3 - 2 * core, other, None),
            (True, OWN, beside, 4 * x, True, 4 - 4 * x, beside, None),
            (core == x, 4 - 4 * x, other, 3 - 2 * x, core != x, 3 - 2 * x, other, 1),
            (x == y, 4 - 4 * y, above, 4 * y, x != y, 4 - 4 * y, above, 1),
            ((x != y) & (core == y), 4 - 4 * y, other, 3 - 2 * y,
             (x != y) & (core != y), 3 - 2 * y, other, 3),
        ]
    hops = []
    for step in (1, -1, 2, -2):
        to, source = d + step, d - step
        hops.append((
            (to >= 0) & (to < n_dp), OWN, lax.rem(to + n_dp, n_dp), OWN - step,
            (source >= 0) & (source < n_dp), OWN - step, lax.rem(source + n_dp, n_dp), None,
        ))
    return hops


def entry_barrier(n_dp, n_mp, d, m):
    barrier = pltpu.get_barrier_semaphore()

    def greet_dp(k, _):
        pl.semaphore_signal(barrier, inc=1, device_id=(lax.rem(d + k, n_dp), m), device_id_type=MESH)
        return 0

    lax.fori_loop(1, n_dp, greet_dp, 0)
    for k in range(1, n_mp):
        pl.semaphore_signal(barrier, inc=1, device_id=(d, lax.rem(m + k, n_mp)), device_id_type=MESH)
    return lambda: pl.semaphore_wait(barrier, n_dp - 1 + n_mp - 1)


def layer_stats(values):
    average = jnp.mean(values, axis=-1, keepdims=True)
    centred = values - average
    spread = jnp.mean(centred * centred, axis=-1, keepdims=True)
    return centred, lax.rsqrt(spread + norm_eps)


def layer_back(grad, gain, centred, scale):
    unit = centred * scale
    scaled = grad * gain
    along = jnp.mean(scaled * unit, axis=-1, keepdims=True)
    level = jnp.mean(scaled, axis=-1, keepdims=True)
    return scale * (scaled - level - unit * along), grad * unit


def gelu_parts(values):
    phi = 0.5 * (1.0 + lax.erf(values * 2.0 ** (-0.5)))
    slope = phi + values * (jnp.exp(values * values * (-0.5)) * (2.0 * math.pi) ** (-0.5))
    return values * phi, slope


def rows_of(index, size=CHUNK):
    return pl.ds(pl.multiple_of(index * size, size), size)


def lanes_of(index, size=HD):
    return pl.ds(pl.multiple_of(index * size, size), size)


def spread_ids(ids_row, out_ref, rows):
    for r in range(rows // LANE):
        part = jnp.broadcast_to(ids_row[:, r * LANE:(r + 1) * LANE], (LANE, LANE))
        out_ref[r * LANE:(r + 1) * LANE, :] = part.T


class Reduction:
    def __init__(self, name, rows, columns, groups):
        self.name, self.rows, self.columns, self.groups = name, rows, columns, groups
        self.sizes, self.split = [rows], []
        for bits in groups:
            size = self.sizes[-1]
            split = (size >> len(bits)) % 16 == 0 and (size >> len(bits)) > 0
            self.split.append(split)
            self.sizes.append(size >> len(bits) if split else size)
        self.events = 2 * len(groups) + 1

    def scratch(self):
        found = {
            self.name + "_out": pltpu.VMEM((self.rows, self.columns), bf16),
            self.name + "_all": pltpu.VMEM((self.rows, self.columns), bf16),
        }
        for level, bits in enumerate(self.groups):
            members = 1 << len(bits)
            found[f"{self.name}_in{level}"] = pltpu.VMEM(
                (members, self.sizes[level + 1], self.columns), bf16
            )
            for what in ("send", "recv"):
                found[f"{self.name}_{what}{level}"] = pltpu.SemaphoreType.DMA((2, members))
        return found

    def bind(self, r, value, d, m):
        self.r, self.value, self.d, self.m = r, value, d, m
        self.offsets, self.ranks = [0], []
        for bits, split, size in zip(self.groups, self.split, self.sizes[1:]):
            rank = lax.rem(lax.div(d, 1 << bits[0]), 1 << len(bits))
            self.ranks.append(rank)
            self.offsets.append(self.offsets[-1] + rank * size if split else self.offsets[-1])

    def ref(self, what):
        return getattr(self.r, self.name + what + ("_held" if what == "_all" else ""))

    def rows_at(self, level, rank):
        offset = self.offsets[level]
        if self.split[level]:
            offset = offset + rank * self.sizes[level + 1]
        if not isinstance(offset, int):
            offset = pl.multiple_of(offset, 16)
        return pl.ds(offset, self.sizes[level + 1])

    def peer(self, level, turn):
        bits = self.groups[level]
        members = 1 << len(bits)
        rank = lax.rem(self.ranks[level] + turn, members)
        return self.d + (rank - self.ranks[level]) * (1 << bits[0]), rank

    def members(self, level):
        return 1 << len(self.groups[level])

    def down_copy(self, level, turn, arriving=False):
        device, rank = self.peer(level, turn)
        landing = rank if arriving else self.ranks[level]
        return remote(
            self.ref("_out").at[self.rows_at(level, rank), :], self.ref(f"_in{level}").at[landing],
            self.ref(f"_send{level}").at[0, rank], self.ref(f"_recv{level}").at[0, landing],
            (device, self.m),
        )

    def up_copy(self, level, turn, arriving=False):
        device, rank = self.peer(level, turn)
        source = rank if arriving else self.ranks[level]
        rows = self.rows_at(level, source)
        return remote(
            self.ref("_all").at[rows, :], self.ref("_all").at[rows, :],
            self.ref(f"_send{level}").at[1, rank], self.ref(f"_recv{level}").at[1, source],
            (device, self.m),
        )

    def event(self, e):
        levels = len(self.groups)
        if 0 < e <= levels:
            level = e - 1
            kept = self.rows_at(level, self.ranks[level])
            turns = range(1, self.members(level))
            for turn in turns:
                self.down_copy(level, turn).wait_send()
            for turn in turns:
                self.down_copy(level, turn, True).wait_recv()
            if self.split[level]:
                total = self.value[kept, :]
                for turn in turns:
                    total += self.ref(f"_in{level}")[self.peer(level, turn)[1]].astype(f32)
            else:
                self.ref(f"_in{level}")[self.ranks[level]] = self.ref("_out")[kept, :]
                total = self.ref(f"_in{level}")[0].astype(f32)
                for rank in range(1, self.members(level)):
                    total += self.ref(f"_in{level}")[rank].astype(f32)
            self.value[kept, :] = total
        if e < levels:
            for turn in range(1, self.members(e)):
                if self.split[e]:
                    given = self.rows_at(e, self.peer(e, turn)[1])
                    self.ref("_out")[given, :] = self.value[given, :].astype(bf16)
                elif turn == 1:
                    kept = self.rows_at(e, self.ranks[e])
                    self.ref("_out")[kept, :] = self.value[kept, :].astype(bf16)
                self.down_copy(e, turn).start()
            return
        back = [level for level in reversed(range(levels)) if self.split[level]]
        if e == levels:
            kept = self.rows_at(levels - 1, self.ranks[-1])
            self.ref("_all")[kept, :] = self.value[kept, :].astype(bf16)
        done = e - levels - 1
        if 0 <= done < len(back):
            for turn in range(1, self.members(back[done])):
                self.up_copy(back[done], turn).wait_send()
                self.up_copy(back[done], turn, True).wait_recv()
        if done + 1 < len(back):
            level = back[done + 1]
            if done >= 0:
                pass
            for turn in range(1, self.members(level)):
                self.up_copy(level, turn).start()


class Tree:
    def __init__(self, name, n_mp, parts, width):
        self.name, self.n, self.parts, self.width = name, n_mp, parts, width
        self.depth = n_mp // 2 - 1
        self.finished = parts + (self.depth + 1) * LAG
        self.steps = parts + (2 * self.depth + 1) * LAG

    def scratch(self):
        found = {}
        for what in ("in", "cross"):
            found[f"{self.name}_{what}"] = pltpu.VMEM((self.parts, PART, self.width), bf16)
        for what in ("sums", "back"):
            for way in ("send", "recv"):
                found[f"{self.name}_{what}_{way}"] = pltpu.SemaphoreType.DMA((self.parts,))
        found[f"{self.name}_cross_recv"] = pltpu.SemaphoreType.DMA((self.parts,))
        return found

    def bind(self, r, d, m, terms, result, finish):
        self.r, self.d, self.m = r, d, m
        self.terms, self.result, self.finish = terms, result, finish
        left = m < self.n // 2
        self.near = jnp.where(left, m, self.n - 1 - m)
        side = 1 - 2 * lax.div(m, self.n // 2)
        self.inward, self.outward = m + side, m - side
        self.inner = self.near == self.depth

    def ref(self, what):
        return getattr(self.r, self.name + what)

    def sum_copy(self, c):
        return remote(
            self.terms.at[rows_of(c, PART), :], self.ref("_in").at[c],
            self.ref("_sums_send").at[c], self.ref("_sums_recv").at[c], (self.d, self.inward),
        )

    def cross_copy(self, c):
        return remote(
            self.terms.at[rows_of(c, PART), :], self.ref("_cross").at[c],
            self.ref("_sums_send").at[c], self.ref("_cross_recv").at[c], (self.d, self.inward),
        )

    def back_copy(self, c):
        rows = rows_of(c, PART)
        to = lax.rem(self.outward + self.n, self.n)
        return remote(
            self.result.at[rows, :], self.result.at[rows, :],
            self.ref("_back_send").at[c], self.ref("_back_recv").at[c], (self.d, to),
        )

    def at(self, t, when_valid, extra=None):
        valid = (t >= 0) & (t < self.parts)
        if extra is not None:
            valid = valid & extra
        c = jnp.clip(t, 0, self.parts - 1)
        pl.when(valid)(lambda: when_valid(c))

    def step(self, t):
        inner, outer = self.inner, jnp.logical_not(self.inner)

        def pass_in(c):
            @pl.when(self.near > 0)
            def _():
                self.sum_copy(c).wait_recv()
                rows = rows_of(c, PART)
                self.terms[rows, :] = (
                    self.terms[rows, :].astype(f32) + self.ref("_in")[c].astype(f32)
                ).astype(bf16)

            pl.when(inner)(self.cross_copy(c).start)
            pl.when(outer)(self.sum_copy(c).start)

        def work(c):
            self.cross_copy(c).wait_recv()
            rows = rows_of(c, PART)
            self.finish(rows, self.terms[rows, :].astype(f32) + self.ref("_cross")[c].astype(f32))
            if self.depth > 0:
                self.back_copy(c).start()

        def pass_out(c):
            self.back_copy(c).wait_recv()
            pl.when(self.near > 0)(self.back_copy(c).start)

        self.at(t - self.near * LAG, pass_in)
        self.at(t - (self.depth + 1) * LAG, work, inner)
        if self.depth > 0:
            self.at(t - (2 * self.depth + 1 - self.near) * LAG, pass_out, outer)

    def drain(self):
        for c in range(self.parts):
            self.sum_copy(c).wait_send()
        if self.depth > 0:
            @pl.when(self.near > 0)
            def _():
                for c in range(self.parts):
                    self.back_copy(c).wait_send()


def layer_kernel(r, n_dp, n_mp, rows, reductions, trees):
    d, m = lax.axis_index("dp"), lax.axis_index("mp")
    chunks = rows // CHUNK
    tiles = [slice(j * LANE, (j + 1) * LANE) for j in range(chunks)]
    hops = near_hops(n_dp, d)
    first_hops = [h for h in range(len(hops)) if hops[h][7] is None]
    later_hops = [h for h in range(len(hops)) if hops[h][7] is not None]
    follow = {h: [k for k in range(len(hops)) if hops[k][7] == h] for h in range(len(hops))}
    drains = []

    loads = {}
    for i, name in enumerate(("out_weight", "out_grad", "up_weight", "down_weight")):
        target = r.out_all.at[rows_of(m), :] if name == "out_weight" else getattr(r, name + "_held")
        loads[name] = pltpu.make_async_copy(getattr(r, name), target, r.load_sem.at[i])
        loads[name].start()

    def emit(name):
        i = RESULTS.index(name)
        copy = pltpu.make_async_copy(getattr(r, name + "_held"), getattr(r, name), r.emit_sem.at[i])
        copy.start()
        drains.append(copy.wait)

    def weight_copy(k, block):
        return remote(
            r.out_all.at[rows_of(block), :], r.out_all.at[rows_of(block), :],
            r.weight_send.at[k], r.weight_recv.at[k], (d, lax.rem(m + k, n_mp)),
        )

    def near_copy(hop, chunk):
        _, source, target, there = hops[hop][:4]
        part = rows_of(chunk)
        return remote(
            r.kv.at[source, part, :], r.kv.at[there, part, :],
            r.kv_send.at[hop, chunk], r.kv_recv.at[hop, chunk], (target, m),
        )

    def near_arrival(hop, chunk):
        part = rows_of(chunk)
        return remote(
            r.kv.at[OWN, part, :], r.kv.at[hops[hop][5], part, :],
            r.kv_send.at[hop, chunk], r.kv_recv.at[hop, chunk], (hops[hop][6], m),
        )

    id_steps = (1, -1, 2, -2)

    def id_copy(i):
        step = id_steps[i]
        return remote(
            r.ids.at[OWN], r.ids.at[OWN - step], r.id_send.at[i], r.id_recv.at[i],
            (lax.rem(d + step + n_dp, n_dp), m),
        )

    def wide_copy(k, source):
        return remote(
            r.wide.at[source], r.wide.at[source],
            r.wide_send.at[k], r.wide_recv.at[k], (lax.rem(d + k, n_dp), m),
        )

    leave_barrier = entry_barrier(n_dp, n_mp, d, m)
    query_ids = r.row_table[...].astype(f32).reshape(1, rows)
    support = r.row_kind[...].astype(f32).reshape(1, rows) == 1.0
    r.ids[OWN] = jnp.where(support & (query_ids != 0.0), query_ids, -1.0)
    wide_held = jnp.where(support & (query_ids == 0.0), 1.0, 0.0)[:, :1]
    r.vec[...] = jnp.zeros_like(r.vec)

    def send_early():
        leave_barrier()
        for h in first_hops:
            when(hops[h][0], near_copy(h, 0).start)
        for i, step in enumerate(id_steps):
            when((d + step >= 0) & (d + step < n_dp), id_copy(i).start)
        loads["out_weight"].wait()
        for k in range(1, n_mp):
            weight_copy(k, m).start()

    def drain_early():
        for i, step in enumerate(id_steps):
            when((d + step >= 0) & (d + step < n_dp), id_copy(i).wait_send)
        for k in range(1, n_mp):
            weight_copy(k, m).wait_send()
        for h in range(len(hops)):
            for c in range(chunks):
                when(hops[h][0], near_copy(h, c).wait_send)

    drains.append(drain_early)
    gain, shift = r.first_gain[...], r.first_shift[...]
    for i, w in enumerate((r.query_weight, r.key_weight, r.value_weight)):
        r.qkv_weight[:, i * HD:(i + 1) * HD] = w[...]
    for c in range(chunks):
        part = slice(c * CHUNK, (c + 1) * CHUNK)
        centred, scale = layer_stats(r.row_input[part, :].astype(f32))
        normed = (centred * scale * gain + shift).astype(bf16)
        r.normed[part, :] = normed
        qkv = mm(normed, r.qkv_weight[...])
        r.kv[OWN, part, :] = qkv[:, HD:].astype(bf16)
        if c == 0:
            r.wide[d, :, :2 * HD] = qkv[:1, HD:].astype(bf16).astype(f32)
            r.wide[d, :, 2 * HD:] = jnp.broadcast_to(wide_held, (1, HD))
            send_early()
        else:
            for h in first_hops:
                when(hops[h][0], near_copy(h, c).start)
        r.query[part, :] = qkv[:, :HD].astype(bf16)
        r.query_t[:, part] = qkv[:, :HD].T.astype(bf16)

    def wide_start(k, _):
        wide_copy(k, d).start()
        return 0

    lax.fori_loop(1, n_dp, wide_start, 0)

    def wide_sent(k, _):
        wide_copy(k, d).wait_send()
        return 0

    drains.append(lambda: lax.fori_loop(1, n_dp, wide_sent, 0))

    r.top[...] = jnp.full_like(r.top, masked_score)
    r.total[...] = jnp.zeros_like(r.total)
    r.mixed_t[...] = jnp.zeros_like(r.mixed_t)

    def absorb(key_rows, peak):
        for j, lanes in enumerate(tiles):
            old = r.top[:, lanes]
            new = jnp.maximum(old, jnp.broadcast_to(jnp.max(peak[j], axis=0, keepdims=True), (8, LANE)))
            r.top[:, lanes] = new
            fade = jnp.exp2((old - new) * EXP2_SCALE)
            r.total[:, lanes] = r.total[:, lanes] * fade
            r.mixed_t[:, lanes] = r.mixed_t[:, lanes] * fade[:1, :]

        def weigh(t, _):
            size = min(key_rows, CHUNK)
            part = rows_of(t, size)
            for lanes in tiles:
                weight = jnp.exp2((r.scores[part, lanes] - r.top[:1, lanes]) * EXP2_SCALE)
                r.total[:, lanes] += jnp.sum(weight.reshape(size // 8, 8, LANE), axis=0)
                r.weights[part, lanes] = weight.astype(bf16)
            return 0

        lax.fori_loop(0, max(1, key_rows // CHUNK), weigh, 0, unroll=True)

    def score(key, allowed, part, peak):
        scores = mm(key, r.query_t[...])
        result = []
        for j, lanes in enumerate(tiles):
            kept = jnp.where(allowed(lanes), scores[:, lanes], masked_score)
            r.scores[part, lanes] = kept
            result.append(jnp.maximum(peak[j], jnp.max(kept.reshape(-1, 8, LANE), axis=0)))
        return tuple(result)

    no_peak = tuple(jnp.full((8, LANE), masked_score, f32) for _ in tiles)

    def attend(slot):
        spread_ids(r.ids[slot], r.id_columns.at[slot], rows)

        def one(t, peak):
            part = rows_of(t)
            ids = r.id_columns[slot, part, :]
            return score(
                r.kv[slot, part, :HD], lambda lanes: ids == query_ids[:, lanes], part, peak
            )

        absorb(rows, lax.fori_loop(0, chunks, one, no_peak, unroll=True))
        r.mixed_t[...] += mm(r.kv[slot, :, HD:], r.weights[...], TN)

    attend(OWN)
    for i, step in enumerate(id_steps):
        when((d - step >= 0) & (d - step < n_dp), id_copy(i).wait_recv)

    def idle_work():
        loads["out_grad"].wait()
        loads["down_weight"].wait()
        r.grad_active[...] = mm(r.out_grad_held[...], r.down_weight_held[...], NT)
        loads["up_weight"].wait()
        r.up_weight_t[...] = r.up_weight_held[...].T
        r.qkv_weight_t[...] = r.qkv_weight[...].T

    for h in first_hops + later_hops:
        if h == first_hops[1]:
            idle_work()
        for c in range(chunks):
            when(hops[h][4], near_arrival(h, c).wait_recv)
            for later in follow[h]:
                when(hops[later][0], near_copy(later, c).start)
        when(hops[h][4], lambda h=h: attend(hops[h][5]))

    def wide_arrive(k, _):
        wide_copy(k, lax.rem(d - k + n_dp, n_dp)).wait_recv()
        return 0

    lax.fori_loop(1, n_dp, wide_arrive, 0)
    wide_rows = n_dp
    r.wide_rows[...] = r.wide[...].reshape(n_dp, 3 * HD)

    def wide_allowed(lanes):
        return (r.wide_rows[:, 2 * HD:] > 0.5) & (query_ids[:, lanes] == 0.0)

    absorb(wide_rows, score(r.wide_rows[:, :HD].astype(bf16), wide_allowed, slice(0, wide_rows), no_peak))
    r.mixed_t[...] += mm(r.wide_rows[:, HD:2 * HD].astype(bf16), r.weights[:wide_rows, :], TN)

    for j, lanes in enumerate(tiles):
        total = jnp.sum(r.total[:, lanes], axis=0, keepdims=True)
        mixed = r.mixed_t[:, lanes] / total
        r.mixed_t[:, lanes] = mixed
        r.log_total[:, lanes] = jnp.broadcast_to(
            r.top[:1, lanes] * EXP2_SCALE + jnp.log2(total), (8, LANE)
        )
        r.mixed[lanes, lanes_of(m)] = mixed.T.astype(bf16)

    def head_copy(way, block, c):
        to = m + (1 if way == 0 else -1)
        distance = m - block if way == 0 else block - m
        at = r.mixed.at[rows_of(c), lanes_of(lax.rem(block + n_mp, n_mp))]
        return remote(
            at, at, r.head_send.at[way, distance, c], r.head_recv.at[way, distance, c],
            (d, lax.rem(to + n_mp, n_mp)),
        )

    def head_arrival(way, block, c):
        distance = (m - block if way == 0 else block - m) - 1
        at = r.mixed.at[rows_of(c), lanes_of(lax.rem(block + n_mp, n_mp))]
        return remote(
            at, at, r.head_send.at[way, distance, c], r.head_recv.at[way, distance, c], (d, m),
        )

    def head_step(s):
        c = jnp.clip(s, 0, chunks - 1)
        for way in (0, 1):
            room = m + 1 < n_mp if way == 0 else m > 0

            @pl.when((s < chunks) & room)
            def _(way=way):
                head_copy(way, m, c).start()
        for distance in range(1, n_mp):
            t = s - distance * HEAD_LAG
            valid = (t >= 0) & (t < chunks)
            t = jnp.clip(t, 0, chunks - 1)
            for way in (0, 1):
                block = m - distance if way == 0 else m + distance
                room = m + 1 < n_mp if way == 0 else m > 0

                @pl.when(valid & (block >= 0) & (block < n_mp))
                def _(way=way, block=block, t=t, room=room):
                    head_arrival(way, block, t).wait_recv()

                    @pl.when(room)
                    def _():
                        head_copy(way, block, t).start()

    def add_vector(name, values):
        i = VECTORS.index(name)
        r.vec[i] += jnp.sum(values.reshape(-1, 8, values.shape[-1]), axis=0)

    def feed_forward(c):
        part = rows_of(c)
        branch = mm(r.mixed[part, :], r.out_all[...]) + r.out_bias[...]
        middle = r.row_input[part, :].astype(f32) + branch
        r.middle[part, :] = middle
        centred, scale = layer_stats(middle)
        normed = (centred * scale * r.second_gain[...] + r.second_shift[...]).astype(bf16)
        r.normed_mid[part, :] = normed
        active, slope = gelu_parts(mm(normed, r.up_weight_held[...]) + r.up_bias[...])
        active = active.astype(bf16)
        r.active[part, :] = active
        grad_upper = (slope * r.grad_active[part, :]).astype(bf16)
        r.grad_upper[part, :] = grad_upper
        add_vector("up_bias", grad_upper.astype(f32))
        r.mid_terms[part, :] = mm(grad_upper, r.up_weight_t[...]).astype(bf16)

    def finish_mid(part, grad):
        centred, scale = layer_stats(r.middle[part, :])
        back, gain_terms = layer_back(grad, r.second_gain[...], centred, scale)
        grad_middle = r.out_grad_held[part, :].astype(f32) + back
        r.grad_middle[part, :] = grad_middle
        branch = grad_middle.astype(bf16)
        r.grad_branch[part, :] = branch
        add_vector("second_gain", gain_terms)
        add_vector("second_shift", grad)
        add_vector("out_bias", branch.astype(f32))

    def finish_out(part, total):
        r.block_output_held[part, :] = (r.middle[part, :] + total + r.down_bias[...]).astype(bf16)

    def finish_first(part, grad):
        centred, scale = layer_stats(r.row_input[part, :].astype(f32))
        back, gain_terms = layer_back(grad, r.first_gain[...], centred, scale)
        r.grad_low_held[part, :] = (r.grad_middle[part, :] + back).astype(bf16)
        add_vector("first_gain", gain_terms)
        add_vector("first_shift", grad)

    tree_mid, tree_out, tree_first = trees
    tree_mid.bind(r, d, m, r.mid_terms, r.grad_branch, finish_mid)
    tree_out.bind(r, d, m, r.out_terms, r.block_output_held, finish_out)
    tree_first.bind(r, d, m, r.first_terms, r.grad_low_held, finish_first)
    up_sum, down_sum, out_sum, qkv_sum = reductions
    up_sum.bind(r, r.up_weight_sum, d, m)
    down_sum.bind(r, r.down_weight_sum, d, m)
    out_sum.bind(r, r.out_weight_sum, d, m)
    qkv_sum.bind(r, r.qkv_weight_sum, d, m)

    def probabilities(slot):
        def one(t, _):
            part = rows_of(t)
            ids = r.id_columns[slot, part, :]
            scores = mm(r.kv[slot, part, :HD], r.query_t[...])
            for lanes in tiles:
                prob = jnp.exp2(scores[:, lanes] * EXP2_SCALE - r.log_total[:1, lanes])
                r.probs[slot, part, lanes] = jnp.where(
                    ids == query_ids[:, lanes], prob, 0.0
                ).astype(bf16)
            return 0

        lax.fori_loop(0, chunks, one, 0, unroll=True)

    for k in range(1, n_mp):
        weight_copy(k, lax.rem(m - k + n_mp, n_mp)).wait_recv()
    feed_from = (n_mp - 1) * HEAD_LAG
    stages = [(True, OWN)] + [(hops[h][4], hops[h][5]) for h in range(len(hops))]

    def middle_step(s, _):
        head_step(s)
        for i, (cond, slot) in enumerate(stages):
            pl.when(both(s == i, cond))(lambda slot=slot: probabilities(slot))
        c = s - feed_from

        @pl.when((c >= 0) & (c < chunks))
        def _():
            feed_forward(c)

        for u in range(SUB):
            tree_mid.step(c * SUB + u)
        return 0

    lax.fori_loop(0, feed_from + chunks, middle_step, 0)

    def drain_heads():
        for way in (0, 1):
            room = m + 1 < n_mp if way == 0 else m > 0
            for distance in range(n_mp - 1):
                block = m - distance if way == 0 else m + distance

                @pl.when(room & (block >= 0) & (block < n_mp))
                def _(way=way, block=block):
                    for c in range(chunks):
                        head_copy(way, block, c).wait_send()

    drains.append(drain_heads)

    def down_weight_grad():
        r.down_weight_sum[...] = mm(r.active[...], r.out_grad_held[...], TN)
        down_sum.event(0)

    def up_weight_grad():
        r.up_weight_sum[...] = mm(r.normed_mid[...], r.grad_upper[...], TN)
        up_sum.event(0)

    def out_terms():
        r.out_terms[...] = mm(r.active[...], r.down_weight_held[...]).astype(bf16)

    def column_sums():
        add_vector("down_bias", r.out_grad_held[...].astype(f32))

    queue = [down_weight_grad, up_weight_grad, out_terms]
    for e in range(1, up_sum.events):
        queue.append(lambda e=e: down_sum.event(e))
        queue.append(lambda e=e: up_sum.event(e))
        if e == 1:
            queue.append(column_sums)
    queue.append(lambda: (emit("up_sum_all"), emit("down_sum_all")))

    for s in range(chunks * SUB, tree_mid.steps):
        tree_mid.step(jnp.int32(s))
        if queue:
            queue.pop(0)()
    drains.append(tree_mid.drain)

    for c in range(chunks):
        part = slice(c * CHUNK, (c + 1) * CHUNK)
        grad = mm(r.grad_branch[part, :], r.out_all[rows_of(m), :], NT)
        r.grad_heads[part, :] = grad.astype(bf16)
        turned = grad.T.astype(bf16)
        r.grad_heads_t[:, part] = turned
        r.row_delta[:, part] = jnp.broadcast_to(
            jnp.sum(turned.astype(f32) * r.mixed_t[:, part], axis=0, keepdims=True), (8, LANE)
        )
    r.grad_query_t[...] = jnp.zeros_like(r.grad_query_t)

    def score_back(prob, value, part):
        grad_probs = mm(value, r.grad_heads_t[...])
        for lanes in tiles:
            r.weights[part, lanes] = (
                prob(lanes).astype(f32) * (grad_probs[:, lanes] - r.row_delta[:1, lanes])
            ).astype(bf16)

    def attend_back(slot, store):
        def one(t, _):
            part = rows_of(t)
            score_back(lambda lanes: r.probs[slot, part, lanes], r.kv[slot, part, HD:], part)
            store(
                t, part, mm(r.weights[part, :], r.query[...]) * SCALE,
                mm(r.probs[slot, part, :], r.grad_heads[...]),
            )
            return 0

        lax.fori_loop(0, chunks, one, 0, unroll=True)
        r.grad_query_t[...] += mm(r.kv[slot, :, :HD], r.weights[...], TN)

    def store_terms(slot, sent):
        def store(t, part, key_grad, value_grad):
            r.kv_terms[slot, part, :HD] = key_grad.astype(bf16)
            r.kv_terms[slot, part, HD:] = value_grad.astype(bf16)
            sent(t)
        return store

    def store_own(t, part, key_grad, value_grad):
        r.kv_grad[part, :HD] = key_grad
        r.kv_grad[part, HD:] = value_grad

    def back_copy(hop, chunk):
        part = rows_of(chunk)
        return remote(
            r.kv_terms.at[hops[hop][5], part, :], r.kv_back.at[hop, part, :],
            r.back_send.at[hop, chunk], r.back_recv.at[hop, chunk], (hops[hop][6], m),
        )

    def add_back(hop, chunk):
        part = rows_of(chunk)
        back_copy(hop, chunk).wait_recv()
        slot = hops[hop][1]
        r.kv_terms[slot, part, :] = (
            r.kv_terms[slot, part, :].astype(f32) + r.kv_back[hop, part, :].astype(f32)
        ).astype(bf16)

    out_steps = list(range(tree_out.steps))

    def side_work(steps, tasks):
        for _ in range(steps):
            if out_steps:
                tree_out.step(jnp.int32(out_steps.pop(0)))
        for _ in range(tasks):
            if queue:
                queue.pop(0)()

    def pass_back(h):
        for c in range(chunks):
            for later in follow[h]:
                when(hops[later][0], lambda later=later, c=c: add_back(later, c))
            when(hops[h][4], back_copy(h, c).start)

    def out_weight_grad():
        r.out_weight_sum[...] = mm(r.mixed[:, lanes_of(m)], r.grad_branch[...], TN)
        out_sum.event(0)

    queue.append(out_weight_grad)
    for e in range(1, out_sum.events):
        queue.append(lambda e=e: out_sum.event(e))
    queue.append(lambda: emit("out_sum_all"))
    for h in reversed(first_hops + later_hops):
        def sent(t, h=h):
            if not follow[h]:
                back_copy(h, t).start()

        when(hops[h][4], lambda h=h, sent=sent: attend_back(hops[h][5], store_terms(hops[h][5], sent)))
        if follow[h] and h in later_hops:
            pass_back(h)
        side_work(2, 1)
    attend_back(OWN, store_own)
    wide_scores = mm(r.wide_rows[:, :HD].astype(bf16), r.query_t[...])

    def wide_prob(lanes):
        prob = jnp.exp2(wide_scores[:, lanes] * EXP2_SCALE - r.log_total[:1, lanes])
        return jnp.where(wide_allowed(lanes), prob, 0.0)

    wide_part = slice(0, wide_rows)
    score_back(wide_prob, r.wide_rows[:, HD:2 * HD].astype(bf16), wide_part)
    grads = r.weights[wide_part, :]
    r.grad_query_t[...] += mm(r.wide_rows[:, :HD].astype(bf16), grads, TN)
    wide_probs = jnp.concatenate([wide_prob(lanes).astype(bf16) for lanes in tiles], axis=1)
    wide_terms = jnp.concatenate(
        (mm(grads, r.query[...]) * SCALE, mm(wide_probs, r.grad_heads[...])), axis=1
    )
    r.wide_terms[...] = wide_terms.reshape(n_dp, 1, 2 * HD)

    def wide_back_copy(k, target, source):
        return remote(
            r.wide_terms.at[target], r.wide_back.at[source],
            r.wide_back_send.at[k], r.wide_back_recv.at[k], (target, m),
        )

    def wide_back_start(k, _):
        wide_back_copy(k, lax.rem(d + k, n_dp), d).start()
        return 0

    def wide_back_arrive(k, _):
        wide_back_copy(k, lax.rem(d + k, n_dp), lax.rem(d - k + n_dp, n_dp)).wait_recv()
        return 0

    lax.fori_loop(1, n_dp, wide_back_start, 0)

    def back_sent(k, _):
        wide_back_copy(k, lax.rem(d + k, n_dp), d).wait_send()
        return 0

    def drain_back():
        lax.fori_loop(1, n_dp, back_sent, 0)
        for h in range(len(hops)):
            for c in range(chunks):
                when(hops[h][4], back_copy(h, c).wait_send)

    drains.append(drain_back)
    r.wide_back[d] = r.wide_terms[d]
    for h in first_hops:
        if follow[h]:
            pass_back(h)
    for c in range(chunks):
        part = slice(c * CHUNK, (c + 1) * CHUNK)
        r.qkv_grad[part, :HD] = (r.grad_query_t[:, part].T * SCALE).astype(bf16)
    lax.fori_loop(1, n_dp, wide_back_arrive, 0)
    r.kv_grad[:1, :] += jnp.sum(r.wide_back[...], axis=0)

    inner_rows = [VECTORS.index(name) for name in VECTORS if name not in ("up_bias", "down_bias")]

    def line_vec_copy(arriving=False):
        to = lax.rem(tree_mid.outward + n_mp, n_mp)
        return remote(
            r.line_vec.at[0] if not arriving else r.line_vec.at[1], r.line_vec.at[1],
            r.line_vec_send.at[0], r.line_vec_recv.at[0], (d, to),
        )

    def vectors_along_line():
        for i in range(len(VECTORS)):
            r.line_vec[0, i:i + 1, :] = jnp.sum(r.vec[i], axis=0, keepdims=True)
        r.line_vec[0, len(VECTORS):, :] = jnp.zeros_like(r.line_vec[0, len(VECTORS):, :])
        if tree_mid.depth > 0:
            pl.when(tree_mid.inner)(line_vec_copy().start)

    def all_vec_copy(k, block):
        return remote(
            r.all_vec.at[block], r.all_vec.at[block],
            r.all_vec_send.at[k], r.all_vec_recv.at[k], (lax.rem(d + k, n_dp), m),
        )

    def all_vec_start(k, _):
        all_vec_copy(k, d).start()
        return 0

    def all_vec_arrive(k, _):
        all_vec_copy(k, lax.rem(d - k + n_dp, n_dp)).wait_recv()
        return 0

    def vec_sent(k, _):
        all_vec_copy(k, d).wait_send()
        return 0

    def vectors_over_all():
        if tree_mid.depth > 0:
            @pl.when(jnp.logical_not(tree_mid.inner))
            def _():
                line_vec_copy(True).wait_recv()
                row = lax.broadcasted_iota(jnp.int32, r.line_vec.shape[1:], 0)
                given = row < 0
                for i in inner_rows:
                    given = given | (row == i)
                r.line_vec[0] = jnp.where(given, r.line_vec[1], r.line_vec[0])
                if tree_mid.depth > 1:
                    pl.when(tree_mid.near > 0)(line_vec_copy().start)
        r.all_vec[d] = r.line_vec[0]
        lax.fori_loop(1, n_dp, all_vec_start, 0)

    def vectors_done():
        lax.fori_loop(1, n_dp, all_vec_arrive, 0)
        r.vectors_held[...] = jnp.sum(r.all_vec[...], axis=0)
        emit("vectors")

    def drain_vectors():
        if tree_mid.depth > 0:
            sends = tree_mid.inner if tree_mid.depth == 1 else tree_mid.near > 0
            pl.when(sends)(line_vec_copy().wait_send)
        lax.fori_loop(1, n_dp, vec_sent, 0)

    def last_step(s):
        part = slice(s * CHUNK, (s + 1) * CHUNK)
        for h in first_hops:
            def add(h=h):
                back_copy(h, s).wait_recv()
                r.kv_grad[part, :] += r.kv_back[h, part, :].astype(f32)
            when(hops[h][0], add)
        r.qkv_grad[part, HD:] = r.kv_grad[part, :].astype(bf16)
        r.first_terms[part, :] = mm(r.qkv_grad[part, :], r.qkv_weight_t[...]).astype(bf16)
        for u in range(SUB):
            tree_first.step(jnp.int32(s * SUB + u))

    for s in range(chunks):
        last_step(s)
        side_work(2, 1)
    r.qkv_weight_sum[...] = mm(r.normed[...], r.qkv_grad[...], TN)
    qkv_sum.event(0)
    waiting = [lambda e=e: qkv_sum.event(e) for e in range(1, qkv_sum.events)]
    for s in range(chunks * SUB, tree_first.steps):
        tree_first.step(jnp.int32(s))
        side_work(2, 1)
        if s % 2 == 1 and waiting:
            waiting.pop(0)()
        if s == tree_first.finished - 1:
            vectors_along_line()
        if s == min(tree_first.finished + 1, tree_first.steps - 1):
            vectors_over_all()
    drains.append(drain_vectors)
    drains.append(tree_first.drain)
    emit("grad_low")
    while out_steps or queue:
        side_work(1, 1)
    drains.append(tree_out.drain)
    emit("block_output")
    while waiting:
        waiting.pop(0)()
    emit("qkv_sum_all")
    vectors_done()

    for drain in drains:
        drain()


def layer(n_dp, n_mp, args):
    rows, width = args["row_input"].shape
    hidden = args["up_weight"].shape[1]
    chunks = rows // CHUNK
    names = tuple(args)
    outs = dict(
        block_output=((rows, width), bf16), grad_low=((rows, width), bf16),
        up_sum_all=((width, hidden), bf16), down_sum_all=((hidden, width), bf16),
        out_sum_all=((HD, width), bf16), qkv_sum_all=((width, 3 * HD), bf16),
        vectors=((8, width), f32),
    )
    bits = list(range(n_dp.bit_length() - 1))
    groups = [tuple(bits[:1])] + [tuple(bits[i:i + 2]) for i in range(1, len(bits), 2)]
    reductions = (
        Reduction("up_sum", width, hidden, groups), Reduction("down_sum", hidden, width, groups),
        Reduction("out_sum", HD, width, groups), Reduction("qkv_sum", width, 3 * HD, groups),
    )
    trees = tuple(Tree(name, n_mp, chunks * SUB, width) for name in ("tree_mid", "tree_out", "tree_first"))
    dma = pltpu.SemaphoreType.DMA
    v = pltpu.VMEM
    scratch = dict(
        normed=v((rows, width), bf16), query=v((rows, HD), bf16), query_t=v((HD, rows), bf16),
        mixed=v((rows, width), bf16), mixed_t=v((HD, rows), f32), log_total=v((8, rows), f32),
        ids=v((SLOTS, 1, rows), f32), id_columns=v((SLOTS, rows, LANE), f32),
        qkv_weight=v((width, 3 * HD), bf16), qkv_weight_t=v((3 * HD, width), bf16),
        up_weight_t=v((hidden, width), bf16), out_all=v((width, width), bf16),
        kv=v((SLOTS, rows, 2 * HD), bf16), kv_terms=v((SLOTS, rows, 2 * HD), bf16),
        kv_back=v((5, rows, 2 * HD), bf16), kv_grad=v((rows, 2 * HD), f32),
        wide=v((n_dp, 1, 3 * HD), f32), wide_rows=v((n_dp, 3 * HD), f32),
        wide_terms=v((n_dp, 1, 2 * HD), f32), wide_back=v((n_dp, 1, 2 * HD), f32),
        top=v((8, rows), f32), total=v((8, rows), f32),
        scores=v((rows, rows), f32), weights=v((rows, rows), bf16),
        out_grad_held=v((rows, width), bf16), up_weight_held=v((width, hidden), bf16),
        down_weight_held=v((hidden, width), bf16), block_output_held=v((rows, width), bf16),
        grad_low_held=v((rows, width), bf16), vectors_held=v((8, width), f32),
        probs=v((SLOTS, rows, rows), bf16), grad_active=v((rows, hidden), f32),
        middle=v((rows, width), f32), normed_mid=v((rows, width), bf16),
        active=v((rows, hidden), bf16), grad_upper=v((rows, hidden), bf16),
        mid_terms=v((rows, width), bf16), out_terms=v((rows, width), bf16),
        first_terms=v((rows, width), bf16), grad_middle=v((rows, width), f32),
        grad_branch=v((rows, width), bf16),
        grad_heads=v((rows, HD), bf16), grad_heads_t=v((HD, rows), bf16),
        row_delta=v((8, rows), f32), grad_query_t=v((HD, rows), f32),
        qkv_grad=v((rows, 3 * HD), bf16),
        up_weight_sum=v((width, hidden), f32), down_weight_sum=v((hidden, width), f32),
        out_weight_sum=v((HD, width), f32), qkv_weight_sum=v((width, 3 * HD), f32),
        vec=v((len(VECTORS), 8, width), f32), line_vec=v((2, 8, width), f32),
        all_vec=v((n_dp, 8, width), f32),
        kv_send=dma((5, chunks)), kv_recv=dma((5, chunks)),
        back_send=dma((5, chunks)), back_recv=dma((5, chunks)),
        id_send=dma((4,)), id_recv=dma((4,)),
        weight_send=dma((n_mp,)), weight_recv=dma((n_mp,)),
        wide_send=dma((n_dp,)), wide_recv=dma((n_dp,)),
        wide_back_send=dma((n_dp,)), wide_back_recv=dma((n_dp,)),
        head_send=dma((2, n_mp, chunks)), head_recv=dma((2, n_mp, chunks)),
        line_vec_send=dma((1,)), line_vec_recv=dma((1,)),
        load_sem=dma((4,)), emit_sem=dma((len(RESULTS),)),
        all_vec_send=dma((n_dp,)), all_vec_recv=dma((n_dp,)),
    )
    for part in reductions + trees:
        found = part.scratch()
        scratch.update({k + "_held" if k in outs else k: held for k, held in found.items()})

    def kernel(*refs):
        r = types.SimpleNamespace(**dict(zip(names + tuple(outs) + tuple(scratch), refs)))
        layer_kernel(r, n_dp, n_mp, rows, reductions, trees)

    vmem, hbm = pl.BlockSpec(memory_space=pltpu.VMEM), pl.BlockSpec(memory_space=pl.ANY)
    late = ("out_weight", "out_grad", "up_weight", "down_weight")
    result = pl.pallas_call(
        kernel,
        out_shape=[jax.ShapeDtypeStruct(*o) for o in outs.values()],
        in_specs=[hbm if name in late else vmem for name in names],
        out_specs=[hbm] * len(outs),
        scratch_shapes=list(scratch.values()),
        compiler_params=pltpu.CompilerParams(
            collective_id=0, has_side_effects=True, vmem_limit_bytes=58 * 1024 * 1024),
        name="layer",
    )(*args.values())
    return dict(zip(outs, result))


def write_out(got):
    names = tuple(got)
    rows, width = got["block_output"].shape
    hidden = got["up_sum_all"].shape[1]
    wide = dict(
        input_grad=(rows, width), query=(width, HD), key=(width, HD), value=(width, HD),
        out=(HD, width), up=(width, hidden), down=(hidden, width),
    )
    outs = dict(block_output=((rows, width), bf16))
    outs.update({name: (shape, f32) for name, shape in wide.items()})
    outs.update({name: ((1, width), f32) for name in VECTORS})

    def kernel(*refs):
        given = dict(zip(names, refs))
        out = dict(zip(outs, refs[len(names):]))
        held = dict(zip(tuple(given) + tuple(wide), refs[len(names) + len(outs):]))
        in_sems, out_sems = refs[-2:]
        loads, copies = {}, []
        for i, name in enumerate(names):
            loads[name] = pltpu.make_async_copy(given[name], held[name], in_sems.at[i])
            loads[name].start()

        def send(source, name):
            copy = pltpu.make_async_copy(source, out[name], out_sems.at[len(copies)])
            copy.start()
            copies.append(copy)

        for name, low in (
            ("input_grad", "grad_low"), ("up", "up_sum_all"), ("down", "down_sum_all"),
            ("out", "out_sum_all"),
        ):
            loads[low].wait()
            held[name][...] = held[low][...].astype(f32)
            send(held[name], name)
        loads["qkv_sum_all"].wait()
        for i, name in enumerate(("query", "key", "value")):
            held[name][...] = held["qkv_sum_all"][:, i * HD:(i + 1) * HD].astype(f32)
            send(held[name], name)
        loads["block_output"].wait()
        send(held["block_output"], "block_output")
        loads["vectors"].wait()
        for i, name in enumerate(VECTORS):
            send(held["vectors"].at[i:i + 1, :], name)
        for copy in copies:
            copy.wait()

    hbm = pl.BlockSpec(memory_space=pl.ANY)
    result = pl.pallas_call(
        kernel,
        out_shape=[jax.ShapeDtypeStruct(*o) for o in outs.values()],
        in_specs=[hbm] * len(names),
        out_specs=[hbm] * len(outs),
        scratch_shapes=[pltpu.VMEM(a.shape, a.dtype) for a in got.values()]
        + [pltpu.VMEM(shape, f32) for shape in wide.values()]
        + [pltpu.SemaphoreType.DMA((len(names),)), pltpu.SemaphoreType.DMA((len(outs),))],
        compiler_params=pltpu.CompilerParams(vmem_limit_bytes=60 * 1024 * 1024),
        name="write_out",
    )(*got.values())
    return dict(zip(outs, result))


def shards(
    n_dp, n_mp, row_input, first_gain, first_shift, query_weight, key_weight, value_weight,
    out_weight, out_bias, second_gain, second_shift, up_weight, up_bias, down_weight, down_bias,
    row_table, row_kind, out_grad,
):
    got = write_out(layer(n_dp, n_mp, dict(
        row_input=row_input, first_gain=first_gain[None], first_shift=first_shift[None],
        query_weight=query_weight, key_weight=key_weight, value_weight=value_weight,
        out_weight=out_weight, out_bias=out_bias[None], second_gain=second_gain[None],
        second_shift=second_shift[None], up_weight=up_weight, up_bias=up_bias[None],
        down_weight=down_weight, down_bias=down_bias[None], row_table=row_table,
        row_kind=row_kind, out_grad=out_grad,
    )))
    vector = {name: got[name][0] for name in VECTORS}
    return (
        got["block_output"], got["input_grad"], vector["first_gain"], vector["first_shift"],
        got["query"], got["key"], got["value"], got["out"],
        vector["out_bias"], vector["second_gain"], vector["second_shift"],
        got["up"], vector["up_bias"], got["down"], vector["down_bias"],
    )


def solution(mesh):
    n_dp, n_mp = mesh.shape["dp"], mesh.shape["mp"]
    in_specs = (
        P("dp", None), P(), P(), P(None, "mp"), P(None, "mp"), P(None, "mp"), P("mp", None),
        P(), P(), P(), P(None, "mp"), P("mp"), P("mp", None), P(), P("dp"), P("dp"), P("dp", None),
    )
    out_specs = (
        P("dp", None), P("dp", None), P(), P(), P(None, "mp"), P(None, "mp"), P(None, "mp"),
        P("mp", None), P(), P(), P(), P(None, "mp"), P("mp"), P("mp", None), P(),
    )
    return jax.shard_map(
        lambda *a: shards(n_dp, n_mp, *a), mesh=mesh, in_specs=in_specs, out_specs=out_specs,
        check_vma=False,
    )
```

```python
import math
import types

import jax
import jax.numpy as jnp
from jax import lax
from jax.experimental import pallas as pl
from jax.experimental.pallas import tpu as pltpu
from jax.sharding import PartitionSpec as P

HD = 128
NEAR = 2
SLOTS = 2 * NEAR + 1
OWN = NEAR
LANE = 128
CHUNK = 128
SUB = 2
PART = CHUNK // SUB
HEAD_LAG = 2
GATHER_LAG = 2
WORK_LAG = 3
norm_eps = 1e-05
masked_score = -1e30
f32 = jnp.float32
bf16 = jnp.bfloat16
MESH = pl.DeviceIdType.MESH
SCALE = HD ** (-0.5)
EXP2_SCALE = SCALE * math.log2(math.e)
NN = (((1,), (0,)), ((), ()))
NT = (((1,), (1,)), ((), ()))
TN = (((0,), (0,)), ((), ()))
RESULTS = ("block_output", "grad_low", "up_sum_all", "down_sum_all", "out_final", "qkv_sum_all", "vectors")
VECTORS = ("first_gain", "first_shift", "out_bias", "second_gain", "second_shift", "down_bias", "up_bias")


def mm(a, b, dims=NN):
    return lax.dot_general(a, b, dims, preferred_element_type=f32)


def remote(src, dst, send_sem, recv_sem, device):
    return pltpu.make_async_remote_copy(
        src_ref=src, dst_ref=dst, send_sem=send_sem, recv_sem=recv_sem,
        device_id=device, device_id_type=MESH,
    )


def when(cond, action):
    if cond is True:
        action()
    else:
        pl.when(cond)(action)


def both(a, b):
    return b if a is True else (a if b is True else a & b)


def near_hops(n_dp, d):
    if n_dp == 8:
        core, x, y = lax.rem(d, 2), lax.rem(d // 2, 2), d // 4
        other = d + 1 - 2 * core
        beside = d + 2 - 4 * x
        above = d + 4 - 8 * y
        return [
            (True, OWN, other, 1 + 2 * core, True, 3 - 2 * core, other, None),
            (True, OWN, beside, 4 * x, True, 4 - 4 * x, beside, None),
            (core == x, 4 - 4 * x, other, 3 - 2 * x, core != x, 3 - 2 * x, other, 1),
            (x == y, 4 - 4 * y, above, 4 * y, x != y, 4 - 4 * y, above, 1),
            ((x != y) & (core == y), 4 - 4 * y, other, 3 - 2 * y,
             (x != y) & (core != y), 3 - 2 * y, other, 3),
        ]
    hops = []
    for step in (1, -1, 2, -2):
        to, source = d + step, d - step
        hops.append((
            (to >= 0) & (to < n_dp), OWN, lax.rem(to + n_dp, n_dp), OWN - step,
            (source >= 0) & (source < n_dp), OWN - step, lax.rem(source + n_dp, n_dp), None,
        ))
    return hops


def entry_barrier(n_dp, n_mp, d, m):
    barrier = pltpu.get_barrier_semaphore()

    def greet_dp(k, _):
        pl.semaphore_signal(barrier, inc=1, device_id=(lax.rem(d + k, n_dp), m), device_id_type=MESH)
        return 0

    lax.fori_loop(1, n_dp, greet_dp, 0)
    for k in range(1, n_mp):
        pl.semaphore_signal(barrier, inc=1, device_id=(d, lax.rem(m + k, n_mp)), device_id_type=MESH)
    return lambda: pl.semaphore_wait(barrier, n_dp - 1 + n_mp - 1)


def layer_stats(values):
    average = jnp.mean(values, axis=-1, keepdims=True)
    centred = values - average
    spread = jnp.mean(centred * centred, axis=-1, keepdims=True)
    return centred, lax.rsqrt(spread + norm_eps)


def layer_back(grad, gain, centred, scale):
    unit = centred * scale
    scaled = grad * gain
    along = jnp.mean(scaled * unit, axis=-1, keepdims=True)
    level = jnp.mean(scaled, axis=-1, keepdims=True)
    return scale * (scaled - level - unit * along), grad * unit


def gelu_parts(values):
    phi = 0.5 * (1.0 + lax.erf(values * 2.0 ** (-0.5)))
    slope = phi + values * (jnp.exp(values * values * (-0.5)) * (2.0 * math.pi) ** (-0.5))
    return values * phi, slope


def rows_of(index, size=CHUNK):
    return pl.ds(pl.multiple_of(index * size, size), size)


def lanes_of(index, size=HD):
    return pl.ds(pl.multiple_of(index * size, size), size)


def spread_ids(ids_row, out_ref, rows):
    for r in range(rows // LANE):
        part = jnp.broadcast_to(ids_row[:, r * LANE:(r + 1) * LANE], (LANE, LANE))
        out_ref[r * LANE:(r + 1) * LANE, :] = part.T


class Reduction:
    def __init__(self, name, rows, columns, groups):
        self.name, self.rows, self.columns, self.groups = name, rows, columns, groups
        self.sizes, self.split = [rows], []
        for bits in groups:
            size = self.sizes[-1]
            split = (size >> len(bits)) % 16 == 0 and (size >> len(bits)) > 0
            self.split.append(split)
            self.sizes.append(size >> len(bits) if split else size)
        self.events = 2 * len(groups) + 1

    def scratch(self):
        found = {
            self.name + "_out": pltpu.VMEM((self.rows, self.columns), bf16),
            self.name + "_all": pltpu.VMEM((self.rows, self.columns), bf16),
        }
        for level, bits in enumerate(self.groups):
            members = 1 << len(bits)
            found[f"{self.name}_in{level}"] = pltpu.VMEM(
                (members, self.sizes[level + 1], self.columns), bf16
            )
            for what in ("send", "recv"):
                found[f"{self.name}_{what}{level}"] = pltpu.SemaphoreType.DMA((2, members))
        return found

    def bind(self, r, value, d, m):
        self.r, self.value, self.d, self.m = r, value, d, m
        self.offsets, self.ranks = [0], []
        for bits, split, size in zip(self.groups, self.split, self.sizes[1:]):
            rank = lax.rem(lax.div(d, 1 << bits[0]), 1 << len(bits))
            self.ranks.append(rank)
            self.offsets.append(self.offsets[-1] + rank * size if split else self.offsets[-1])

    def ref(self, what):
        return getattr(self.r, self.name + what + ("_held" if what == "_all" else ""))

    def rows_at(self, level, rank):
        offset = self.offsets[level]
        if self.split[level]:
            offset = offset + rank * self.sizes[level + 1]
        if not isinstance(offset, int):
            offset = pl.multiple_of(offset, 16)
        return pl.ds(offset, self.sizes[level + 1])

    def peer(self, level, turn):
        bits = self.groups[level]
        members = 1 << len(bits)
        rank = lax.rem(self.ranks[level] + turn, members)
        return self.d + (rank - self.ranks[level]) * (1 << bits[0]), rank

    def members(self, level):
        return 1 << len(self.groups[level])

    def down_copy(self, level, turn, arriving=False):
        device, rank = self.peer(level, turn)
        landing = rank if arriving else self.ranks[level]
        return remote(
            self.ref("_out").at[self.rows_at(level, rank), :], self.ref(f"_in{level}").at[landing],
            self.ref(f"_send{level}").at[0, rank], self.ref(f"_recv{level}").at[0, landing],
            (device, self.m),
        )

    def up_copy(self, level, turn, arriving=False):
        device, rank = self.peer(level, turn)
        source = rank if arriving else self.ranks[level]
        rows = self.rows_at(level, source)
        return remote(
            self.ref("_all").at[rows, :], self.ref("_all").at[rows, :],
            self.ref(f"_send{level}").at[1, rank], self.ref(f"_recv{level}").at[1, source],
            (device, self.m),
        )

    def event(self, e):
        levels = len(self.groups)
        if 0 < e <= levels:
            level = e - 1
            kept = self.rows_at(level, self.ranks[level])
            turns = range(1, self.members(level))
            for turn in turns:
                self.down_copy(level, turn).wait_send()
            for turn in turns:
                self.down_copy(level, turn, True).wait_recv()
            if self.split[level]:
                total = self.value[kept, :]
                for turn in turns:
                    total += self.ref(f"_in{level}")[self.peer(level, turn)[1]].astype(f32)
            else:
                self.ref(f"_in{level}")[self.ranks[level]] = self.ref("_out")[kept, :]
                total = self.ref(f"_in{level}")[0].astype(f32)
                for rank in range(1, self.members(level)):
                    total += self.ref(f"_in{level}")[rank].astype(f32)
            self.value[kept, :] = total
        if e < levels:
            for turn in range(1, self.members(e)):
                if self.split[e]:
                    given = self.rows_at(e, self.peer(e, turn)[1])
                    self.ref("_out")[given, :] = self.value[given, :].astype(bf16)
                elif turn == 1:
                    kept = self.rows_at(e, self.ranks[e])
                    self.ref("_out")[kept, :] = self.value[kept, :].astype(bf16)
                self.down_copy(e, turn).start()
            return
        back = [level for level in reversed(range(levels)) if self.split[level]]
        if e == levels:
            kept = self.rows_at(levels - 1, self.ranks[-1])
            self.ref("_all")[kept, :] = self.value[kept, :].astype(bf16)
        done = e - levels - 1
        if 0 <= done < len(back):
            for turn in range(1, self.members(back[done])):
                self.up_copy(back[done], turn).wait_send()
                self.up_copy(back[done], turn, True).wait_recv()
        if done + 1 < len(back):
            level = back[done + 1]
            if done >= 0:
                pass
            for turn in range(1, self.members(level)):
                self.up_copy(level, turn).start()


class Tree:
    def __init__(self, name, n_mp, parts, width, scatter=False):
        self.name, self.n, self.parts, self.width, self.scatter = name, n_mp, parts, width, scatter

    def scratch(self):
        dma, found = pltpu.SemaphoreType.DMA, {}
        for what in ("in", "cross"):
            found[f"{self.name}_{what}"] = pltpu.VMEM((self.parts, PART, self.width), bf16)
        for what in ("sums_send", "in_recv", "cross_recv", "back_recv"):
            found[f"{self.name}_{what}"] = dma((self.parts,))
        found[f"{self.name}_back_send"] = dma((self.n, self.parts))
        return found

    def bind(self, r, d, m, terms, result, finish):
        self.r, self.d, self.m = r, d, m
        self.terms, self.result, self.finish = terms, result, finish
        self.half = lax.div(m, 2)
        side = 1 - 2 * self.half
        self.inward, self.outward = m + side, m - side
        self.end = (m == 0) | (m == self.n - 1)
        self.inner = jnp.logical_not(self.end)

    def ref(self, what):
        return getattr(self.r, self.name + what)

    def mine(self, c):
        return self.inner & (lax.rem(c, 2) == self.half)

    def other(self, c):
        return self.inner & (lax.rem(c, 2) != self.half)

    def sum_copy(self, c, landing):
        return remote(
            self.terms.at[rows_of(c, PART), :], self.ref("_" + landing).at[c],
            self.ref("_sums_send").at[c], self.ref(f"_{landing}_recv").at[c],
            (self.d, self.inward),
        )

    def back_copy(self, c, k, to):
        rows = rows_of(c, PART)
        to = lax.rem(to + self.n, self.n)
        if self.scatter:
            source, target = self.result[0].at[rows, lanes_of(to)], self.result[1].at[rows, :]
        else:
            source, target = self.result.at[rows, :], self.result.at[rows, :]
        return remote(
            source, target, self.ref("_back_send").at[k, c], self.ref("_back_recv").at[c],
            (self.d, to),
        )

    def back_copies(self, c):
        if self.scatter:
            return [self.back_copy(c, k, self.m + k) for k in range(1, self.n)]
        return [self.back_copy(c, 0, self.outward), self.back_copy(c, 1, self.inward)]

    def send(self, c):
        pl.when(self.end)(self.sum_copy(c, "in").start)

    def gather(self, c):
        @pl.when(self.other(c))
        def _():
            self.sum_copy(c, "in").wait_recv()
            rows = rows_of(c, PART)
            self.terms[rows, :] = (
                self.terms[rows, :].astype(f32) + self.ref("_in")[c].astype(f32)
            ).astype(bf16)
            self.sum_copy(c, "cross").start()

    def work(self, c):
        @pl.when(self.mine(c))
        def _():
            self.sum_copy(c, "in").wait_recv()
            self.sum_copy(c, "cross").wait_recv()
            rows = rows_of(c, PART)
            self.finish(
                rows, self.terms[rows, :].astype(f32) + self.ref("_in")[c].astype(f32)
                + self.ref("_cross")[c].astype(f32),
            )
            for copy in self.back_copies(c):
                copy.start()

    def forward(self, c):
        @pl.when(self.other(c))
        def _():
            self.back_copy(c, 0, self.outward).wait_recv()
            if not self.scatter:
                self.back_copy(c, 0, self.outward).start()

    def collect(self, c):
        pl.when(self.end)(self.back_copy(c, 0, self.outward).wait_recv)

    def drain(self):
        for c in range(self.parts):
            pl.when(jnp.logical_not(self.mine(c)))(self.sum_copy(c, "cross").wait_send)

            @pl.when(self.mine(c))
            def _(c=c):
                for copy in self.back_copies(c):
                    copy.wait_send()

            if not self.scatter:
                pl.when(self.other(c))(self.back_copy(c, 0, self.outward).wait_send)


def layer_kernel(r, n_dp, n_mp, rows, reductions, trees):
    d, m = lax.axis_index("dp"), lax.axis_index("mp")
    chunks = rows // CHUNK
    tiles = [slice(j * LANE, (j + 1) * LANE) for j in range(chunks)]
    hops = near_hops(n_dp, d)
    first_hops = [h for h in range(len(hops)) if hops[h][7] is None]
    later_hops = [h for h in range(len(hops)) if hops[h][7] is not None]
    follow = {h: [k for k in range(len(hops)) if hops[k][7] == h] for h in range(len(hops))}
    drains = []

    loads = {}
    for i, name in enumerate(("out_weight", "out_grad", "up_weight", "down_weight")):
        target = r.out_all.at[rows_of(m), :] if name == "out_weight" else getattr(r, name + "_held")
        loads[name] = pltpu.make_async_copy(getattr(r, name), target, r.load_sem.at[i])
        loads[name].start()

    def emit(name):
        i = RESULTS.index(name)
        copy = pltpu.make_async_copy(getattr(r, name + "_held"), getattr(r, name), r.emit_sem.at[i])
        copy.start()
        drains.append(copy.wait)

    def weight_copy(k, block):
        return remote(
            r.out_all.at[rows_of(block), :], r.out_all.at[rows_of(block), :],
            r.weight_send.at[k], r.weight_recv.at[k], (d, lax.rem(m + k, n_mp)),
        )

    def near_copy(hop, chunk):
        _, source, target, there = hops[hop][:4]
        part = rows_of(chunk)
        return remote(
            r.kv.at[source, part, :], r.kv.at[there, part, :],
            r.kv_send.at[hop, chunk], r.kv_recv.at[hop, chunk], (target, m),
        )

    def near_arrival(hop, chunk):
        part = rows_of(chunk)
        return remote(
            r.kv.at[OWN, part, :], r.kv.at[hops[hop][5], part, :],
            r.kv_send.at[hop, chunk], r.kv_recv.at[hop, chunk], (hops[hop][6], m),
        )

    id_steps = (1, -1, 2, -2)

    def id_copy(i):
        step = id_steps[i]
        return remote(
            r.ids.at[OWN], r.ids.at[OWN - step], r.id_send.at[i], r.id_recv.at[i],
            (lax.rem(d + step + n_dp, n_dp), m),
        )

    def wide_copy(k, source):
        return remote(
            r.wide.at[source], r.wide.at[source],
            r.wide_send.at[k], r.wide_recv.at[k], (lax.rem(d + k, n_dp), m),
        )

    leave_barrier = entry_barrier(n_dp, n_mp, d, m)
    query_ids = r.row_table[...].astype(f32).reshape(1, rows)
    support = r.row_kind[...].astype(f32).reshape(1, rows) == 1.0
    r.ids[OWN] = jnp.where(support & (query_ids != 0.0), query_ids, -1.0)
    wide_held = jnp.where(support & (query_ids == 0.0), 1.0, 0.0)[:, :1]
    r.vec[...] = jnp.zeros_like(r.vec)

    def send_early():
        leave_barrier()
        for h in first_hops:
            when(hops[h][0], near_copy(h, 0).start)
        for i, step in enumerate(id_steps):
            when((d + step >= 0) & (d + step < n_dp), id_copy(i).start)
        loads["out_weight"].wait()
        for k in range(1, n_mp):
            weight_copy(k, m).start()

    def drain_early():
        for i, step in enumerate(id_steps):
            when((d + step >= 0) & (d + step < n_dp), id_copy(i).wait_send)
        for k in range(1, n_mp):
            weight_copy(k, m).wait_send()
        for h in range(len(hops)):
            for c in range(chunks):
                when(hops[h][0], near_copy(h, c).wait_send)

    drains.append(drain_early)
    gain, shift = r.first_gain[...], r.first_shift[...]
    for i, w in enumerate((r.query_weight, r.key_weight, r.value_weight)):
        r.qkv_weight[:, i * HD:(i + 1) * HD] = w[...]
    for c in range(chunks):
        part = slice(c * CHUNK, (c + 1) * CHUNK)
        centred, scale = layer_stats(r.row_input[part, :].astype(f32))
        normed = (centred * scale * gain + shift).astype(bf16)
        r.normed[part, :] = normed
        qkv = mm(normed, r.qkv_weight[:, HD:])
        r.kv[OWN, part, :] = qkv.astype(bf16)
        if c == 0:
            r.wide[d, :, :2 * HD] = qkv[:1, :].astype(bf16).astype(f32)
            r.wide[d, :, 2 * HD:] = jnp.broadcast_to(wide_held, (1, HD))
            send_early()
        else:
            for h in first_hops:
                when(hops[h][0], near_copy(h, c).start)

    def wide_start(k, _):
        wide_copy(k, d).start()
        return 0

    lax.fori_loop(1, n_dp, wide_start, 0)
    for c in range(chunks):
        part = slice(c * CHUNK, (c + 1) * CHUNK)
        query = mm(r.normed[part, :], r.qkv_weight[:, :HD])
        r.query[part, :] = query.astype(bf16)
        r.query_t[:, part] = query.T.astype(bf16)

    def wide_sent(k, _):
        wide_copy(k, d).wait_send()
        return 0

    drains.append(lambda: lax.fori_loop(1, n_dp, wide_sent, 0))

    r.top[...] = jnp.full_like(r.top, masked_score)
    r.total[...] = jnp.zeros_like(r.total)
    r.mixed_t[...] = jnp.zeros_like(r.mixed_t)

    def absorb(key_rows, peak):
        for j, lanes in enumerate(tiles):
            old = r.top[:, lanes]
            new = jnp.maximum(old, jnp.broadcast_to(jnp.max(peak[j], axis=0, keepdims=True), (8, LANE)))
            r.top[:, lanes] = new
            fade = jnp.exp2((old - new) * EXP2_SCALE)
            r.total[:, lanes] = r.total[:, lanes] * fade
            r.mixed_t[:, lanes] = r.mixed_t[:, lanes] * fade[:1, :]

        def weigh(t, _):
            size = min(key_rows, CHUNK)
            part = rows_of(t, size)
            for lanes in tiles:
                weight = jnp.exp2((r.scores[part, lanes] - r.top[:1, lanes]) * EXP2_SCALE)
                r.total[:, lanes] += jnp.sum(weight.reshape(size // 8, 8, LANE), axis=0)
                r.weights[part, lanes] = weight.astype(bf16)
            return 0

        lax.fori_loop(0, max(1, key_rows // CHUNK), weigh, 0, unroll=True)

    def score(key, allowed, part, peak):
        scores = mm(key, r.query_t[...])
        result = []
        for j, lanes in enumerate(tiles):
            kept = jnp.where(allowed(lanes), scores[:, lanes], masked_score)
            r.scores[part, lanes] = kept
            result.append(jnp.maximum(peak[j], jnp.max(kept.reshape(-1, 8, LANE), axis=0)))
        return tuple(result)

    no_peak = tuple(jnp.full((8, LANE), masked_score, f32) for _ in tiles)

    def attend(slot):
        spread_ids(r.ids[slot], r.id_columns.at[slot], rows)

        def one(t, peak):
            part = rows_of(t)
            ids = r.id_columns[slot, part, :]
            return score(
                r.kv[slot, part, :HD], lambda lanes: ids == query_ids[:, lanes], part, peak
            )

        absorb(rows, lax.fori_loop(0, chunks, one, no_peak, unroll=True))
        r.mixed_t[...] += mm(r.kv[slot, :, HD:], r.weights[...], TN)

    attend(OWN)
    for i, step in enumerate(id_steps):
        when((d - step >= 0) & (d - step < n_dp), id_copy(i).wait_recv)

    def idle_work():
        loads["out_grad"].wait()
        loads["down_weight"].wait()
        r.grad_active[...] = mm(r.out_grad_held[...], r.down_weight_held[...], NT)
        loads["up_weight"].wait()
        r.up_weight_t[...] = r.up_weight_held[...].T
        r.qkv_weight_t[...] = r.qkv_weight[...].T

    for h in first_hops + later_hops:
        if h == first_hops[1]:
            idle_work()
        for c in range(chunks):
            when(hops[h][4], near_arrival(h, c).wait_recv)
            for later in follow[h]:
                when(hops[later][0], near_copy(later, c).start)
        when(hops[h][4], lambda h=h: attend(hops[h][5]))

    def wide_arrive(k, _):
        wide_copy(k, lax.rem(d - k + n_dp, n_dp)).wait_recv()
        return 0

    lax.fori_loop(1, n_dp, wide_arrive, 0)
    wide_rows = n_dp
    r.wide_rows[...] = r.wide[...].reshape(n_dp, 3 * HD)

    def wide_allowed(lanes):
        return (r.wide_rows[:, 2 * HD:] > 0.5) & (query_ids[:, lanes] == 0.0)

    absorb(wide_rows, score(r.wide_rows[:, :HD].astype(bf16), wide_allowed, slice(0, wide_rows), no_peak))
    r.mixed_t[...] += mm(r.wide_rows[:, HD:2 * HD].astype(bf16), r.weights[:wide_rows, :], TN)

    for j, lanes in enumerate(tiles):
        total = jnp.sum(r.total[:, lanes], axis=0, keepdims=True)
        mixed = r.mixed_t[:, lanes] / total
        r.mixed_t[:, lanes] = mixed
        r.log_total[:, lanes] = jnp.broadcast_to(
            r.top[:1, lanes] * EXP2_SCALE + jnp.log2(total), (8, LANE)
        )
        r.mixed[lanes, lanes_of(m)] = mixed.T.astype(bf16)

    def head_copy(way, block, c):
        to = m + (1 if way == 0 else -1)
        distance = m - block if way == 0 else block - m
        at = r.mixed.at[rows_of(c), lanes_of(lax.rem(block + n_mp, n_mp))]
        return remote(
            at, at, r.head_send.at[way, distance, c], r.head_recv.at[way, distance, c],
            (d, lax.rem(to + n_mp, n_mp)),
        )

    def head_arrival(way, block, c):
        distance = (m - block if way == 0 else block - m) - 1
        at = r.mixed.at[rows_of(c), lanes_of(lax.rem(block + n_mp, n_mp))]
        return remote(
            at, at, r.head_send.at[way, distance, c], r.head_recv.at[way, distance, c], (d, m),
        )

    def head_step(s):
        c = jnp.clip(s, 0, chunks - 1)
        for way in (0, 1):
            room = m + 1 < n_mp if way == 0 else m > 0

            @pl.when((s < chunks) & room)
            def _(way=way):
                head_copy(way, m, c).start()
        for distance in range(1, n_mp):
            t = s - distance * HEAD_LAG
            valid = (t >= 0) & (t < chunks)
            t = jnp.clip(t, 0, chunks - 1)
            for way in (0, 1):
                block = m - distance if way == 0 else m + distance
                room = m + 1 < n_mp if way == 0 else m > 0

                @pl.when(valid & (block >= 0) & (block < n_mp))
                def _(way=way, block=block, t=t, room=room):
                    head_arrival(way, block, t).wait_recv()

                    @pl.when(room)
                    def _():
                        head_copy(way, block, t).start()

    def add_vector(name, values):
        i = VECTORS.index(name)
        r.vec[i] += jnp.sum(values.reshape(-1, 8, values.shape[-1]), axis=0)

    def feed_forward(c):
        part = rows_of(c)
        branch = mm(r.mixed[part, :], r.out_all[...]) + r.out_bias[...]
        middle = r.row_input[part, :].astype(f32) + branch
        r.middle[part, :] = middle
        centred, scale = layer_stats(middle)
        normed = (centred * scale * r.second_gain[...] + r.second_shift[...]).astype(bf16)
        r.normed_mid[part, :] = normed
        active, slope = gelu_parts(mm(normed, r.up_weight_held[...]) + r.up_bias[...])
        active = active.astype(bf16)
        r.active[part, :] = active
        grad_upper = (slope * r.grad_active[part, :]).astype(bf16)
        r.grad_upper[part, :] = grad_upper
        add_vector("up_bias", grad_upper.astype(f32))
        r.mid_terms[part, :] = mm(grad_upper, r.up_weight_t[...]).astype(bf16)
        for u in range(SUB):
            tree_mid.send(c * SUB + u)

    def finish_mid(part, grad):
        centred, scale = layer_stats(r.middle[part, :])
        back, gain_terms = layer_back(grad, r.second_gain[...], centred, scale)
        grad_middle = r.out_grad_held[part, :].astype(f32) + back
        r.grad_middle[part, :] = grad_middle
        branch = grad_middle.astype(bf16)
        r.grad_branch[part, :] = branch
        heads = mm(branch, r.out_all_t[...]).astype(bf16)
        r.heads_terms[part, :] = heads
        for head in range(1, n_mp - 1):
            @pl.when(m == head)
            def _(head=head):
                r.grad_heads[part, :] = heads[:, head * HD:(head + 1) * HD]
        add_vector("second_gain", gain_terms)
        add_vector("second_shift", grad)
        add_vector("out_bias", branch.astype(f32))

    def finish_out(part, total):
        r.block_output_held[part, :] = (r.middle[part, :] + total + r.down_bias[...]).astype(bf16)

    def finish_first(part, grad):
        centred, scale = layer_stats(r.row_input[part, :].astype(f32))
        back, gain_terms = layer_back(grad, r.first_gain[...], centred, scale)
        r.grad_low_held[part, :] = (r.grad_middle[part, :] + back).astype(bf16)
        add_vector("first_gain", gain_terms)
        add_vector("first_shift", grad)

    tree_mid, tree_out, tree_first = trees
    tree_mid.bind(r, d, m, r.mid_terms, (r.heads_terms, r.grad_heads), finish_mid)
    tree_out.bind(r, d, m, r.out_terms, r.block_output_held, finish_out)
    tree_first.bind(r, d, m, r.first_terms, r.grad_low_held, finish_first)
    up_sum, down_sum, out_sum, qkv_sum = reductions
    up_sum.bind(r, r.up_weight_sum, d, m)
    down_sum.bind(r, r.down_weight_sum, d, m)
    out_sum.bind(r, r.out_weight_sum, d, m)
    qkv_sum.bind(r, r.qkv_weight_sum, d, m)

    def probabilities(slot):
        def one(t, _):
            part = rows_of(t)
            ids = r.id_columns[slot, part, :]
            scores = mm(r.kv[slot, part, :HD], r.query_t[...])
            for lanes in tiles:
                prob = jnp.exp2(scores[:, lanes] * EXP2_SCALE - r.log_total[:1, lanes])
                r.probs[slot, part, lanes] = jnp.where(
                    ids == query_ids[:, lanes], prob, 0.0
                ).astype(bf16)
            return 0

        lax.fori_loop(0, chunks, one, 0, unroll=True)

    for k in range(1, n_mp):
        weight_copy(k, lax.rem(m - k + n_mp, n_mp)).wait_recv()
    feed_from = (n_mp - 1) * HEAD_LAG
    stages = [(True, OWN)] + [(hops[h][4], hops[h][5]) for h in range(len(hops))]

    def middle_step(s, _):
        head_step(s)
        for i, (cond, slot) in enumerate(stages):
            pl.when(both(s == i, cond))(lambda slot=slot: probabilities(slot))

        @pl.when(s == 0)
        def _():
            r.out_all_t[...] = r.out_all[...].T

        c = s - feed_from

        @pl.when((c >= 0) & (c < chunks))
        def _():
            feed_forward(c)

        for lag, act in ((GATHER_LAG, tree_mid.gather), (WORK_LAG, tree_mid.work)):
            @pl.when((c >= lag) & (c < chunks + lag))
            def _(lag=lag, act=act):
                for u in range(SUB):
                    act((c - lag) * SUB + u)
        return 0

    lax.fori_loop(0, feed_from + chunks, middle_step, 0)

    def drain_heads():
        for way in (0, 1):
            room = m + 1 < n_mp if way == 0 else m > 0
            for distance in range(n_mp - 1):
                block = m - distance if way == 0 else m + distance

                @pl.when(room & (block >= 0) & (block < n_mp))
                def _(way=way, block=block):
                    for c in range(chunks):
                        head_copy(way, block, c).wait_send()

    drains.append(drain_heads)

    def down_weight_grad():
        r.down_weight_sum[...] = mm(r.active[...], r.out_grad_held[...], TN)
        down_sum.event(0)

    def up_weight_grad():
        r.up_weight_sum[...] = mm(r.normed_mid[...], r.grad_upper[...], TN)
        up_sum.event(0)

    parts = chunks * SUB
    tree_parts = [list(range(c * SUB, (c + 1) * SUB)) for c in range(chunks)]

    def act(tree, chunk, what):
        if 0 <= chunk < chunks:
            for c in tree_parts[chunk]:
                getattr(tree, what)(c)

    down_weight_grad()
    for i in range(chunks - WORK_LAG, chunks):
        if i + WORK_LAG - GATHER_LAG < chunks:
            act(tree_mid, i + WORK_LAG - GATHER_LAG, "gather")
        if i < chunks - 1:
            act(tree_mid, i, "work")
    up_weight_grad()
    r.out_terms[...] = mm(r.active[...], r.down_weight_held[...]).astype(bf16)
    act(tree_mid, chunks - 1, "work")
    for c in range(parts):
        tree_out.send(c)

    def branch_copy(c):
        rows_c = rows_of(c, PART)
        return remote(
            r.grad_branch.at[rows_c, :], r.grad_branch.at[rows_c, :],
            r.branch_send.at[c], r.branch_recv.at[c], (d, tree_mid.inward),
        )

    for c in range(parts):
        pl.when(tree_mid.mine(c))(branch_copy(c).start)
    down_sum.event(1)
    up_sum.event(1)
    for c in range(parts):
        tree_mid.forward(c)
        tree_mid.collect(c)
    drains.append(tree_mid.drain)

    for c in range(chunks):
        part = slice(c * CHUNK, (c + 1) * CHUNK)
        turned = r.grad_heads[part, :].astype(f32).T
        r.grad_heads_t[:, part] = turned.astype(bf16)
        r.row_delta[:, part] = jnp.broadcast_to(
            jnp.sum(turned * r.mixed_t[:, part], axis=0, keepdims=True), (8, LANE)
        )
    r.grad_query_t[...] = jnp.zeros_like(r.grad_query_t)

    def score_back(prob, value, part):
        grad_probs = mm(value, r.grad_heads_t[...])
        for lanes in tiles:
            r.weights[part, lanes] = (
                prob(lanes).astype(f32) * (grad_probs[:, lanes] - r.row_delta[:1, lanes])
            ).astype(bf16)

    def attend_back(slot, store):
        def one(t, _):
            part = rows_of(t)
            score_back(lambda lanes: r.probs[slot, part, lanes], r.kv[slot, part, HD:], part)
            store(
                t, part, mm(r.weights[part, :], r.query[...]) * SCALE,
                mm(r.probs[slot, part, :], r.grad_heads[...]),
            )
            return 0

        lax.fori_loop(0, chunks, one, 0, unroll=True)
        r.grad_query_t[...] += mm(r.kv[slot, :, :HD], r.weights[...], TN)

    def store_terms(slot, sent):
        def store(t, part, key_grad, value_grad):
            r.kv_terms[slot, part, :HD] = key_grad.astype(bf16)
            r.kv_terms[slot, part, HD:] = value_grad.astype(bf16)
            sent(t)
        return store

    def store_own(t, part, key_grad, value_grad):
        r.kv_grad[part, :HD] = key_grad
        r.kv_grad[part, HD:] = value_grad

    def back_copy(hop, chunk):
        part = rows_of(chunk)
        return remote(
            r.kv_terms.at[hops[hop][5], part, :], r.kv_back.at[hop, part, :],
            r.back_send.at[hop, chunk], r.back_recv.at[hop, chunk], (hops[hop][6], m),
        )

    def add_back(hop, chunk):
        part = rows_of(chunk)
        back_copy(hop, chunk).wait_recv()
        slot = hops[hop][1]
        r.kv_terms[slot, part, :] = (
            r.kv_terms[slot, part, :].astype(f32) + r.kv_back[hop, part, :].astype(f32)
        ).astype(bf16)

    def pass_back(h, cond):
        for c in range(chunks):
            for later in follow[h]:
                when(both(hops[later][0], cond), lambda later=later, c=c: add_back(later, c))
            when(both(hops[h][4], cond), back_copy(h, c).start)

    def back_stage(h, sends):
        def sent(t):
            when(sends, back_copy(h, t).start)

        when(hops[h][4], lambda: attend_back(hops[h][5], store_terms(hops[h][5], sent)))

    out_work = []
    for i in range(chunks + 2):
        out_work.append(lambda i=i: (
            act(tree_out, i, "gather"), act(tree_out, i - 1, "work"), act(tree_out, i - 2, "forward")
        ))

    def side_work():
        if out_work:
            out_work.pop(0)()

    def head_pair_grad():
        for c in range(parts):
            pl.when(tree_mid.other(c))(branch_copy(c).wait_recv)

        @pl.when(tree_mid.inner)
        def _():
            pair = pl.ds(pl.multiple_of(tree_mid.half * 2 * HD, 2 * HD), 2 * HD)
            r.out_weight_sum[...] = mm(r.mixed[:, pair], r.grad_branch[...], TN)
            out_sum.event(0)

    def branch_drain():
        for c in range(parts):
            pl.when(tree_mid.mine(c))(branch_copy(c).wait_send)

    drains.append(branch_drain)
    inner = tree_mid.inner

    def out_event(e):
        pl.when(inner)(lambda: out_sum.event(e))

    if len(hops) == 5 and later_hops:
        adds_core, adds_row, adds_corner = hops[4][0], hops[2][0], hops[3][0]
        no = jnp.logical_not
        back_stage(3, no(adds_core))
        back_stage(4, True)
        back_stage(2, True)
        side_work()
        pass_back(3, adds_core)
        back_stage(1, no(adds_row) & no(adds_corner))
        down_sum.event(2)
        up_sum.event(2)
        back_stage(0, True)
        side_work()
        pass_back(1, adds_row & no(adds_corner))
        late_back = [(1, adds_corner)]
    else:
        for h in range(len(hops)):
            back_stage(h, True)
            side_work()
        down_sum.event(2)
        up_sum.event(2)
        late_back = []
    attend_back(OWN, store_own)
    side_work()
    wide_scores = mm(r.wide_rows[:, :HD].astype(bf16), r.query_t[...])

    def wide_prob(lanes):
        prob = jnp.exp2(wide_scores[:, lanes] * EXP2_SCALE - r.log_total[:1, lanes])
        return jnp.where(wide_allowed(lanes), prob, 0.0)

    wide_part = slice(0, wide_rows)
    score_back(wide_prob, r.wide_rows[:, HD:2 * HD].astype(bf16), wide_part)
    grads = r.weights[wide_part, :]
    r.grad_query_t[...] += mm(r.wide_rows[:, :HD].astype(bf16), grads, TN)
    wide_probs = jnp.concatenate([wide_prob(lanes).astype(bf16) for lanes in tiles], axis=1)
    wide_terms = jnp.concatenate(
        (mm(grads, r.query[...]) * SCALE, mm(wide_probs, r.grad_heads[...])), axis=1
    )
    r.wide_terms[...] = wide_terms.reshape(n_dp, 1, 2 * HD)

    def wide_back_copy(k, target, source):
        return remote(
            r.wide_terms.at[target], r.wide_back.at[source],
            r.wide_back_send.at[k], r.wide_back_recv.at[k], (target, m),
        )

    def wide_back_start(k, _):
        wide_back_copy(k, lax.rem(d + k, n_dp), d).start()
        return 0

    def wide_back_arrive(k, _):
        wide_back_copy(k, lax.rem(d + k, n_dp), lax.rem(d - k + n_dp, n_dp)).wait_recv()
        return 0

    lax.fori_loop(1, n_dp, wide_back_start, 0)

    def back_sent(k, _):
        wide_back_copy(k, lax.rem(d + k, n_dp), d).wait_send()
        return 0

    def drain_back():
        lax.fori_loop(1, n_dp, back_sent, 0)
        for h in range(len(hops)):
            for c in range(chunks):
                when(hops[h][4], back_copy(h, c).wait_send)

    drains.append(drain_back)
    r.wide_back[d] = r.wide_terms[d]
    for h, cond in late_back:
        pass_back(h, cond)
    side_work()
    for c in range(chunks):
        part = slice(c * CHUNK, (c + 1) * CHUNK)
        r.qkv_grad[part, :HD] = (r.grad_query_t[:, part].T * SCALE).astype(bf16)
    lax.fori_loop(1, n_dp, wide_back_arrive, 0)
    r.kv_grad[:1, :] += jnp.sum(r.wide_back[...], axis=0)
    head_pair_grad()
    side_work()

    inner_rows = [VECTORS.index(name) for name in VECTORS if name not in ("up_bias", "down_bias")]

    def line_vec_copy(k, half):
        return remote(
            r.line_vec.at[half], r.line_vec.at[half],
            r.line_vec_send.at[k], r.line_vec_recv.at[half], (d, lax.rem(m + k, n_mp)),
        )

    def vectors_along_line():
        for i in range(len(VECTORS)):
            r.own_vec[i:i + 1, :] = jnp.sum(r.vec[i], axis=0, keepdims=True)
        r.own_vec[len(VECTORS):, :] = jnp.zeros_like(r.own_vec[len(VECTORS):, :])

        @pl.when(inner)
        def _():
            r.line_vec[tree_mid.half] = r.own_vec[...]
            for k in range(1, n_mp):
                line_vec_copy(k, tree_mid.half).start()

    def all_vec_copy(k, block):
        return remote(
            r.all_vec.at[block], r.all_vec.at[block],
            r.all_vec_send.at[k], r.all_vec_recv.at[k], (lax.rem(d + k, n_dp), m),
        )

    def all_vec_start(k, _):
        all_vec_copy(k, d).start()
        return 0

    def all_vec_arrive(k, _):
        all_vec_copy(k, lax.rem(d - k + n_dp, n_dp)).wait_recv()
        return 0

    def vec_sent(k, _):
        all_vec_copy(k, d).wait_send()
        return 0

    def vectors_over_all():
        for half in (0, 1):
            pl.when(tree_mid.end | (tree_mid.half != half))(line_vec_copy(1, half).wait_recv)
        row = lax.broadcasted_iota(jnp.int32, r.own_vec.shape, 0)
        summed = row < 0
        for i in inner_rows:
            summed = summed | (row == i)
        r.all_vec[d] = jnp.where(summed, r.line_vec[0] + r.line_vec[1], r.own_vec[...])
        lax.fori_loop(1, n_dp, all_vec_start, 0)

    def vectors_done():
        lax.fori_loop(1, n_dp, all_vec_arrive, 0)
        r.vectors_held[...] = jnp.sum(r.all_vec[...], axis=0)
        emit("vectors")

    def drain_vectors():
        @pl.when(inner)
        def _():
            for k in range(1, n_mp):
                line_vec_copy(k, tree_mid.half).wait_send()
        lax.fori_loop(1, n_dp, vec_sent, 0)

    def last_step(s):
        part = slice(s * CHUNK, (s + 1) * CHUNK)
        for h in first_hops:
            def add(h=h):
                back_copy(h, s).wait_recv()
                r.kv_grad[part, :] += r.kv_back[h, part, :].astype(f32)
            when(hops[h][0], add)
        r.qkv_grad[part, HD:] = r.kv_grad[part, :].astype(bf16)
        r.first_terms[part, :] = mm(r.qkv_grad[part, :], r.qkv_weight_t[...]).astype(bf16)
        act(tree_first, s, "send")

    def out_share_copy():
        block = rows_of(tree_mid.half, HD)
        return remote(
            r.out_sum_all_held.at[block, :], r.out_final_held,
            r.share_sem.at[0], r.share_sem.at[1], (d, lax.rem(tree_mid.outward + n_mp, n_mp)),
        )

    def out_share():
        @pl.when(inner)
        def _():
            r.out_final_held[...] = r.out_sum_all_held[rows_of(1 - tree_mid.half, HD), :]
            out_share_copy().start()

    for s in range(chunks):
        last_step(s)
        act(tree_first, s - 1, "gather")
        act(tree_first, s - 2, "work")
        act(tree_first, s - 3, "forward")
        side_work()
        if s == 1:
            add_vector("down_bias", r.out_grad_held[...].astype(f32))
            down_sum.event(3)
            up_sum.event(3)
            out_event(1)
    r.qkv_weight_sum[...] = mm(r.normed[...], r.qkv_grad[...], TN)
    qkv_sum.event(0)
    act(tree_first, chunks - 1, "gather")
    act(tree_first, chunks - 2, "work")
    act(tree_first, chunks - 3, "forward")
    out_event(2)
    qkv_sum.event(1)
    act(tree_first, chunks - 1, "work")
    vectors_along_line()
    act(tree_first, chunks - 2, "forward")
    down_sum.event(4)
    up_sum.event(4)
    for level in range(5, up_sum.events):
        down_sum.event(level)
        up_sum.event(level)
    emit("up_sum_all")
    emit("down_sum_all")
    qkv_sum.event(2)
    out_event(3)
    act(tree_first, chunks - 1, "forward")
    vectors_over_all()
    while out_work:
        side_work()
    for c in range(parts):
        tree_out.collect(c)
    emit("block_output")
    qkv_sum.event(3)
    for level in range(4, out_sum.events):
        out_event(level)
    out_share()
    for c in range(parts):
        tree_first.collect(c)
    emit("grad_low")
    for level in range(4, qkv_sum.events):
        qkv_sum.event(level)
    emit("qkv_sum_all")
    pl.when(tree_mid.end)(out_share_copy().wait_recv)
    emit("out_final")
    pl.when(inner)(out_share_copy().wait_send)
    vectors_done()
    drains.append(drain_vectors)
    drains.append(tree_first.drain)
    drains.append(tree_out.drain)

    for drain in drains:
        drain()


def layer(n_dp, n_mp, args):
    rows, width = args["row_input"].shape
    hidden = args["up_weight"].shape[1]
    chunks = rows // CHUNK
    names = tuple(args)
    outs = dict(
        block_output=((rows, width), bf16), grad_low=((rows, width), bf16),
        up_sum_all=((width, hidden), bf16), down_sum_all=((hidden, width), bf16),
        out_final=((HD, width), bf16), qkv_sum_all=((width, 3 * HD), bf16),
        vectors=((8, width), f32),
    )
    bits = list(range(n_dp.bit_length() - 1))
    groups = [tuple(bits[:1])] + [tuple(bits[i:i + 2]) for i in range(1, len(bits), 2)]
    reductions = (
        Reduction("up_sum", width, hidden, groups), Reduction("down_sum", hidden, width, groups),
        Reduction("out_sum", 2 * HD, width, groups), Reduction("qkv_sum", width, 3 * HD, groups),
    )
    trees = (
        Tree("tree_mid", n_mp, chunks * SUB, width, scatter=True),
        Tree("tree_out", n_mp, chunks * SUB, width), Tree("tree_first", n_mp, chunks * SUB, width),
    )
    dma = pltpu.SemaphoreType.DMA
    v = pltpu.VMEM
    scratch = dict(
        normed=v((rows, width), bf16), query=v((rows, HD), bf16), query_t=v((HD, rows), bf16),
        mixed=v((rows, width), bf16), mixed_t=v((HD, rows), f32), log_total=v((8, rows), f32),
        ids=v((SLOTS, 1, rows), f32), id_columns=v((SLOTS, rows, LANE), f32),
        qkv_weight=v((width, 3 * HD), bf16), qkv_weight_t=v((3 * HD, width), bf16),
        up_weight_t=v((hidden, width), bf16), out_all=v((width, width), bf16),
        kv=v((SLOTS, rows, 2 * HD), bf16), kv_terms=v((SLOTS, rows, 2 * HD), bf16),
        kv_back=v((5, rows, 2 * HD), bf16), kv_grad=v((rows, 2 * HD), f32),
        wide=v((n_dp, 1, 3 * HD), f32), wide_rows=v((n_dp, 3 * HD), f32),
        wide_terms=v((n_dp, 1, 2 * HD), f32), wide_back=v((n_dp, 1, 2 * HD), f32),
        top=v((8, rows), f32), total=v((8, rows), f32),
        scores=v((rows, rows), f32), weights=v((rows, rows), bf16),
        out_grad_held=v((rows, width), bf16), up_weight_held=v((width, hidden), bf16),
        down_weight_held=v((hidden, width), bf16), block_output_held=v((rows, width), bf16),
        grad_low_held=v((rows, width), bf16), vectors_held=v((8, width), f32),
        probs=v((SLOTS, rows, rows), bf16), grad_active=v((rows, hidden), f32),
        middle=v((rows, width), f32), normed_mid=v((rows, width), bf16),
        active=v((rows, hidden), bf16), grad_upper=v((rows, hidden), bf16),
        mid_terms=v((rows, width), bf16), out_terms=v((rows, width), bf16),
        first_terms=v((rows, width), bf16), grad_middle=v((rows, width), f32),
        grad_branch=v((rows, width), bf16),
        grad_heads=v((rows, HD), bf16), grad_heads_t=v((HD, rows), bf16),
        row_delta=v((8, rows), f32), grad_query_t=v((HD, rows), f32),
        qkv_grad=v((rows, 3 * HD), bf16),
        up_weight_sum=v((width, hidden), f32), down_weight_sum=v((hidden, width), f32),
        out_weight_sum=v((2 * HD, width), f32), qkv_weight_sum=v((width, 3 * HD), f32),
        vec=v((len(VECTORS), 8, width), f32), line_vec=v((2, 8, width), f32), own_vec=v((8, width), f32),
        heads_terms=v((rows, width), bf16), out_all_t=v((width, width), bf16),
        out_final_held=v((HD, width), bf16),
        all_vec=v((n_dp, 8, width), f32),
        kv_send=dma((5, chunks)), kv_recv=dma((5, chunks)),
        back_send=dma((5, chunks)), back_recv=dma((5, chunks)),
        id_send=dma((4,)), id_recv=dma((4,)),
        weight_send=dma((n_mp,)), weight_recv=dma((n_mp,)),
        wide_send=dma((n_dp,)), wide_recv=dma((n_dp,)),
        wide_back_send=dma((n_dp,)), wide_back_recv=dma((n_dp,)),
        head_send=dma((2, n_mp, chunks)), head_recv=dma((2, n_mp, chunks)),
        line_vec_send=dma((n_mp,)), line_vec_recv=dma((2,)),
        branch_send=dma((chunks * SUB,)), branch_recv=dma((chunks * SUB,)), share_sem=dma((2,)),
        load_sem=dma((4,)), emit_sem=dma((len(RESULTS),)),
        all_vec_send=dma((n_dp,)), all_vec_recv=dma((n_dp,)),
    )
    for part in reductions + trees:
        found = part.scratch()
        scratch.update({k + "_held" if k.endswith("_all") else k: held for k, held in found.items()})

    def kernel(*refs):
        r = types.SimpleNamespace(**dict(zip(names + tuple(outs) + tuple(scratch), refs)))
        layer_kernel(r, n_dp, n_mp, rows, reductions, trees)

    vmem, hbm = pl.BlockSpec(memory_space=pltpu.VMEM), pl.BlockSpec(memory_space=pl.ANY)
    late = ("out_weight", "out_grad", "up_weight", "down_weight")
    result = pl.pallas_call(
        kernel,
        out_shape=[jax.ShapeDtypeStruct(*o) for o in outs.values()],
        in_specs=[hbm if name in late else vmem for name in names],
        out_specs=[hbm] * len(outs),
        scratch_shapes=list(scratch.values()),
        compiler_params=pltpu.CompilerParams(
            collective_id=0, has_side_effects=True, vmem_limit_bytes=58 * 1024 * 1024),
        name="layer",
    )(*args.values())
    return dict(zip(outs, result))


def write_out(got):
    names = tuple(got)
    rows, width = got["block_output"].shape
    hidden = got["up_sum_all"].shape[1]
    wide = dict(
        input_grad=(rows, width), query=(width, HD), key=(width, HD), value=(width, HD),
        out=(HD, width), up=(width, hidden), down=(hidden, width),
    )
    outs = dict(block_output=((rows, width), bf16))
    outs.update({name: (shape, f32) for name, shape in wide.items()})
    outs.update({name: ((1, width), f32) for name in VECTORS})

    def kernel(*refs):
        given = dict(zip(names, refs))
        out = dict(zip(outs, refs[len(names):]))
        held = dict(zip(tuple(given) + tuple(wide), refs[len(names) + len(outs):]))
        in_sems, out_sems = refs[-2:]
        loads, copies = {}, []
        for i, name in enumerate(names):
            loads[name] = pltpu.make_async_copy(given[name], held[name], in_sems.at[i])
            loads[name].start()

        def send(source, name):
            copy = pltpu.make_async_copy(source, out[name], out_sems.at[len(copies)])
            copy.start()
            copies.append(copy)

        for name, low in (
            ("input_grad", "grad_low"), ("up", "up_sum_all"), ("down", "down_sum_all"),
            ("out", "out_final"),
        ):
            loads[low].wait()
            held[name][...] = held[low][...].astype(f32)
            send(held[name], name)
        loads["qkv_sum_all"].wait()
        for i, name in enumerate(("query", "key", "value")):
            held[name][...] = held["qkv_sum_all"][:, i * HD:(i + 1) * HD].astype(f32)
            send(held[name], name)
        loads["block_output"].wait()
        send(held["block_output"], "block_output")
        loads["vectors"].wait()
        for i, name in enumerate(VECTORS):
            send(held["vectors"].at[i:i + 1, :], name)
        for copy in copies:
            copy.wait()

    hbm = pl.BlockSpec(memory_space=pl.ANY)
    result = pl.pallas_call(
        kernel,
        out_shape=[jax.ShapeDtypeStruct(*o) for o in outs.values()],
        in_specs=[hbm] * len(names),
        out_specs=[hbm] * len(outs),
        scratch_shapes=[pltpu.VMEM(a.shape, a.dtype) for a in got.values()]
        + [pltpu.VMEM(shape, f32) for shape in wide.values()]
        + [pltpu.SemaphoreType.DMA((len(names),)), pltpu.SemaphoreType.DMA((len(outs),))],
        compiler_params=pltpu.CompilerParams(vmem_limit_bytes=60 * 1024 * 1024),
        name="write_out",
    )(*got.values())
    return dict(zip(outs, result))


def shards(
    n_dp, n_mp, row_input, first_gain, first_shift, query_weight, key_weight, value_weight,
    out_weight, out_bias, second_gain, second_shift, up_weight, up_bias, down_weight, down_bias,
    row_table, row_kind, out_grad,
):
    got = write_out(layer(n_dp, n_mp, dict(
        row_input=row_input, first_gain=first_gain[None], first_shift=first_shift[None],
        query_weight=query_weight, key_weight=key_weight, value_weight=value_weight,
        out_weight=out_weight, out_bias=out_bias[None], second_gain=second_gain[None],
        second_shift=second_shift[None], up_weight=up_weight, up_bias=up_bias[None],
        down_weight=down_weight, down_bias=down_bias[None], row_table=row_table,
        row_kind=row_kind, out_grad=out_grad,
    )))
    vector = {name: got[name][0] for name in VECTORS}
    return (
        got["block_output"], got["input_grad"], vector["first_gain"], vector["first_shift"],
        got["query"], got["key"], got["value"], got["out"],
        vector["out_bias"], vector["second_gain"], vector["second_shift"],
        got["up"], vector["up_bias"], got["down"], vector["down_bias"],
    )


def solution(mesh):
    n_dp, n_mp = mesh.shape["dp"], mesh.shape["mp"]
    in_specs = (
        P("dp", None), P(), P(), P(None, "mp"), P(None, "mp"), P(None, "mp"), P("mp", None),
        P(), P(), P(), P(None, "mp"), P("mp"), P("mp", None), P(), P("dp"), P("dp"), P("dp", None),
    )
    out_specs = (
        P("dp", None), P("dp", None), P(), P(), P(None, "mp"), P(None, "mp"), P(None, "mp"),
        P("mp", None), P(), P(), P(), P(None, "mp"), P("mp"), P("mp", None), P(),
    )
    return jax.shard_map(
        lambda *a: shards(n_dp, n_mp, *a), mesh=mesh, in_specs=in_specs, out_specs=out_specs,
        check_vma=False,
    )
```

```python
import math
import types

import jax
import jax.numpy as jnp
from jax import lax
from jax.experimental import pallas as pl
from jax.experimental.pallas import tpu as pltpu
from jax.sharding import PartitionSpec as P

HD = 128
NEAR = 2
SLOTS = 2 * NEAR + 1
OWN = NEAR
LANE = 128
CHUNK = 128
SUB = 4
PART = CHUNK // SUB
HEAD_LAG = 2
GATHER_LAG = 2
WORK_LAG = 3
norm_eps = 1e-05
masked_score = -1e30
f32 = jnp.float32
bf16 = jnp.bfloat16
MESH = pl.DeviceIdType.MESH
SCALE = HD ** (-0.5)
EXP2_SCALE = SCALE * math.log2(math.e)
NN = (((1,), (0,)), ((), ()))
NT = (((1,), (1,)), ((), ()))
TN = (((0,), (0,)), ((), ()))
RESULTS = ("block_output", "grad_low", "up_sum_all", "down_sum_all", "out_final", "qkv_sum_all", "vectors")
VECTORS = ("first_gain", "first_shift", "out_bias", "second_gain", "second_shift", "down_bias", "up_bias")


def mm(a, b, dims=NN):
    return lax.dot_general(a, b, dims, preferred_element_type=f32)


def remote(src, dst, send_sem, recv_sem, device):
    return pltpu.make_async_remote_copy(
        src_ref=src, dst_ref=dst, send_sem=send_sem, recv_sem=recv_sem,
        device_id=device, device_id_type=MESH,
    )


def when(cond, action):
    if cond is True:
        action()
    else:
        pl.when(cond)(action)


def both(a, b):
    return b if a is True else (a if b is True else a & b)


def near_hops(n_dp, d):
    if n_dp == 8:
        core, x, y = lax.rem(d, 2), lax.rem(d // 2, 2), d // 4
        other = d + 1 - 2 * core
        beside = d + 2 - 4 * x
        above = d + 4 - 8 * y
        return [
            (True, OWN, other, 1 + 2 * core, True, 3 - 2 * core, other, None),
            (True, OWN, beside, 4 * x, True, 4 - 4 * x, beside, None),
            (core == x, 4 - 4 * x, other, 3 - 2 * x, core != x, 3 - 2 * x, other, 1),
            (x == y, 4 - 4 * y, above, 4 * y, x != y, 4 - 4 * y, above, 1),
            ((x != y) & (core == y), 4 - 4 * y, other, 3 - 2 * y,
             (x != y) & (core != y), 3 - 2 * y, other, 3),
        ]
    hops = []
    for step in (1, -1, 2, -2):
        to, source = d + step, d - step
        hops.append((
            (to >= 0) & (to < n_dp), OWN, lax.rem(to + n_dp, n_dp), OWN - step,
            (source >= 0) & (source < n_dp), OWN - step, lax.rem(source + n_dp, n_dp), None,
        ))
    return hops


def entry_barrier(n_dp, n_mp, d, m):
    barrier = pltpu.get_barrier_semaphore()

    def greet_dp(k, _):
        pl.semaphore_signal(barrier, inc=1, device_id=(lax.rem(d + k, n_dp), m), device_id_type=MESH)
        return 0

    lax.fori_loop(1, n_dp, greet_dp, 0)
    for k in range(1, n_mp):
        pl.semaphore_signal(barrier, inc=1, device_id=(d, lax.rem(m + k, n_mp)), device_id_type=MESH)
    return lambda: pl.semaphore_wait(barrier, n_dp - 1 + n_mp - 1)


def layer_stats(values):
    average = jnp.mean(values, axis=-1, keepdims=True)
    centred = values - average
    spread = jnp.mean(centred * centred, axis=-1, keepdims=True)
    return centred, lax.rsqrt(spread + norm_eps)


def layer_back(grad, gain, centred, scale):
    unit = centred * scale
    scaled = grad * gain
    along = jnp.mean(scaled * unit, axis=-1, keepdims=True)
    level = jnp.mean(scaled, axis=-1, keepdims=True)
    return scale * (scaled - level - unit * along), grad * unit


def gelu_parts(values):
    phi = 0.5 * (1.0 + lax.erf(values * 2.0 ** (-0.5)))
    slope = phi + values * (jnp.exp(values * values * (-0.5)) * (2.0 * math.pi) ** (-0.5))
    return values * phi, slope


def rows_of(index, size=CHUNK):
    return pl.ds(pl.multiple_of(index * size, size), size)


def lanes_of(index, size=HD):
    return pl.ds(pl.multiple_of(index * size, size), size)


def spread_ids(ids_row, out_ref, rows):
    for r in range(rows // LANE):
        part = jnp.broadcast_to(ids_row[:, r * LANE:(r + 1) * LANE], (LANE, LANE))
        out_ref[r * LANE:(r + 1) * LANE, :] = part.T


class Reduction:
    def __init__(self, name, rows, columns, groups):
        self.name, self.rows, self.columns, self.groups = name, rows, columns, groups
        self.sizes, self.split = [rows], []
        for bits in groups:
            size = self.sizes[-1]
            split = (size >> len(bits)) % 16 == 0 and (size >> len(bits)) > 0
            self.split.append(split)
            self.sizes.append(size >> len(bits) if split else size)
        self.events = 2 * len(groups) + 1

    def scratch(self):
        found = {
            self.name + "_out": pltpu.VMEM((self.rows, self.columns), bf16),
            self.name + "_all": pltpu.VMEM((self.rows, self.columns), bf16),
        }
        for level, bits in enumerate(self.groups):
            members = 1 << len(bits)
            found[f"{self.name}_in{level}"] = pltpu.VMEM(
                (members, self.sizes[level + 1], self.columns), bf16
            )
            for what in ("send", "recv"):
                found[f"{self.name}_{what}{level}"] = pltpu.SemaphoreType.DMA((2, members))
        return found

    def bind(self, r, value, d, m):
        self.r, self.value, self.d, self.m = r, value, d, m
        self.offsets, self.ranks = [0], []
        for bits, split, size in zip(self.groups, self.split, self.sizes[1:]):
            rank = lax.rem(lax.div(d, 1 << bits[0]), 1 << len(bits))
            self.ranks.append(rank)
            self.offsets.append(self.offsets[-1] + rank * size if split else self.offsets[-1])

    def ref(self, what):
        return getattr(self.r, self.name + what + ("_held" if what == "_all" else ""))

    def rows_at(self, level, rank):
        offset = self.offsets[level]
        if self.split[level]:
            offset = offset + rank * self.sizes[level + 1]
        if not isinstance(offset, int):
            offset = pl.multiple_of(offset, 16)
        return pl.ds(offset, self.sizes[level + 1])

    def peer(self, level, turn):
        bits = self.groups[level]
        members = 1 << len(bits)
        rank = lax.rem(self.ranks[level] + turn, members)
        return self.d + (rank - self.ranks[level]) * (1 << bits[0]), rank

    def members(self, level):
        return 1 << len(self.groups[level])

    def down_copy(self, level, turn, arriving=False):
        device, rank = self.peer(level, turn)
        landing = rank if arriving else self.ranks[level]
        return remote(
            self.ref("_out").at[self.rows_at(level, rank), :], self.ref(f"_in{level}").at[landing],
            self.ref(f"_send{level}").at[0, rank], self.ref(f"_recv{level}").at[0, landing],
            (device, self.m),
        )

    def up_copy(self, level, turn, arriving=False):
        device, rank = self.peer(level, turn)
        source = rank if arriving else self.ranks[level]
        rows = self.rows_at(level, source)
        return remote(
            self.ref("_all").at[rows, :], self.ref("_all").at[rows, :],
            self.ref(f"_send{level}").at[1, rank], self.ref(f"_recv{level}").at[1, source],
            (device, self.m),
        )

    def event(self, e):
        levels = len(self.groups)
        if 0 < e <= levels:
            level = e - 1
            kept = self.rows_at(level, self.ranks[level])
            turns = range(1, self.members(level))
            for turn in turns:
                self.down_copy(level, turn).wait_send()
            for turn in turns:
                self.down_copy(level, turn, True).wait_recv()
            if self.split[level]:
                total = self.value[kept, :]
                for turn in turns:
                    total += self.ref(f"_in{level}")[self.peer(level, turn)[1]].astype(f32)
            else:
                self.ref(f"_in{level}")[self.ranks[level]] = self.ref("_out")[kept, :]
                total = self.ref(f"_in{level}")[0].astype(f32)
                for rank in range(1, self.members(level)):
                    total += self.ref(f"_in{level}")[rank].astype(f32)
            self.value[kept, :] = total
        if e < levels:
            for turn in range(1, self.members(e)):
                if self.split[e]:
                    given = self.rows_at(e, self.peer(e, turn)[1])
                    self.ref("_out")[given, :] = self.value[given, :].astype(bf16)
                elif turn == 1:
                    kept = self.rows_at(e, self.ranks[e])
                    self.ref("_out")[kept, :] = self.value[kept, :].astype(bf16)
                self.down_copy(e, turn).start()
            return
        back = [level for level in reversed(range(levels)) if self.split[level]]
        if e == levels:
            kept = self.rows_at(levels - 1, self.ranks[-1])
            self.ref("_all")[kept, :] = self.value[kept, :].astype(bf16)
        done = e - levels - 1
        if 0 <= done < len(back):
            for turn in range(1, self.members(back[done])):
                self.up_copy(back[done], turn).wait_send()
                self.up_copy(back[done], turn, True).wait_recv()
        if done + 1 < len(back):
            level = back[done + 1]
            if done >= 0:
                pass
            for turn in range(1, self.members(level)):
                self.up_copy(level, turn).start()


class Tree:
    def __init__(self, name, n_mp, parts, width, scatter=False):
        self.name, self.n, self.parts, self.width, self.scatter = name, n_mp, parts, width, scatter

    def scratch(self):
        dma, found = pltpu.SemaphoreType.DMA, {}
        for what in ("in", "cross"):
            found[f"{self.name}_{what}"] = pltpu.VMEM((self.parts, PART, self.width), bf16)
        for what in ("sums_send", "in_recv", "cross_recv", "back_recv"):
            found[f"{self.name}_{what}"] = dma((self.parts,))
        found[f"{self.name}_back_send"] = dma((self.n, self.parts))
        return found

    def bind(self, r, d, m, terms, result, finish):
        self.r, self.d, self.m = r, d, m
        self.terms, self.result, self.finish = terms, result, finish
        self.half = lax.div(m, 2)
        side = 1 - 2 * self.half
        self.inward, self.outward = m + side, m - side
        self.end = (m == 0) | (m == self.n - 1)
        self.inner = jnp.logical_not(self.end)

    def ref(self, what):
        return getattr(self.r, self.name + what)

    def mine(self, c):
        return self.inner & (lax.rem(c, 2) == self.half)

    def other(self, c):
        return self.inner & (lax.rem(c, 2) != self.half)

    def sum_copy(self, c, landing):
        return remote(
            self.terms.at[rows_of(c, PART), :], self.ref("_" + landing).at[c],
            self.ref("_sums_send").at[c], self.ref(f"_{landing}_recv").at[c],
            (self.d, self.inward),
        )

    def back_copy(self, c, k, to):
        rows = rows_of(c, PART)
        to = lax.rem(to + self.n, self.n)
        if self.scatter:
            source, target = self.result[0].at[rows, lanes_of(to)], self.result[1].at[rows, :]
        else:
            source, target = self.result.at[rows, :], self.result.at[rows, :]
        return remote(
            source, target, self.ref("_back_send").at[k, c], self.ref("_back_recv").at[c],
            (self.d, to),
        )

    def back_copies(self, c):
        if self.scatter:
            return [self.back_copy(c, k, self.m + k) for k in range(1, self.n)]
        return [self.back_copy(c, 0, self.outward), self.back_copy(c, 1, self.inward)]

    def send(self, c):
        pl.when(self.end)(self.sum_copy(c, "in").start)

    def gather(self, c):
        @pl.when(self.other(c))
        def _():
            self.sum_copy(c, "in").wait_recv()
            rows = rows_of(c, PART)
            self.terms[rows, :] = (
                self.terms[rows, :].astype(f32) + self.ref("_in")[c].astype(f32)
            ).astype(bf16)
            self.sum_copy(c, "cross").start()

    def work(self, c):
        @pl.when(self.mine(c))
        def _():
            self.sum_copy(c, "in").wait_recv()
            self.sum_copy(c, "cross").wait_recv()
            rows = rows_of(c, PART)
            self.finish(
                rows, self.terms[rows, :].astype(f32) + self.ref("_in")[c].astype(f32)
                + self.ref("_cross")[c].astype(f32),
            )
            for copy in self.back_copies(c):
                copy.start()

    def forward(self, c):
        @pl.when(self.other(c))
        def _():
            self.back_copy(c, 0, self.outward).wait_recv()
            if not self.scatter:
                self.back_copy(c, 0, self.outward).start()

    def collect(self, c):
        pl.when(self.end)(self.back_copy(c, 0, self.outward).wait_recv)

    def drain(self):
        for c in range(self.parts):
            pl.when(jnp.logical_not(self.mine(c)))(self.sum_copy(c, "cross").wait_send)

            @pl.when(self.mine(c))
            def _(c=c):
                for copy in self.back_copies(c):
                    copy.wait_send()

            if not self.scatter:
                pl.when(self.other(c))(self.back_copy(c, 0, self.outward).wait_send)


def layer_kernel(r, n_dp, n_mp, rows, reductions, trees):
    d, m = lax.axis_index("dp"), lax.axis_index("mp")
    chunks = rows // CHUNK
    tiles = [slice(j * LANE, (j + 1) * LANE) for j in range(chunks)]
    hops = near_hops(n_dp, d)
    first_hops = [h for h in range(len(hops)) if hops[h][7] is None]
    later_hops = [h for h in range(len(hops)) if hops[h][7] is not None]
    follow = {h: [k for k in range(len(hops)) if hops[k][7] == h] for h in range(len(hops))}
    drains = []

    loads = {}
    for i, name in enumerate(("out_weight", "out_grad", "up_weight", "down_weight")):
        target = r.out_all.at[rows_of(m), :] if name == "out_weight" else getattr(r, name + "_held")
        loads[name] = pltpu.make_async_copy(getattr(r, name), target, r.load_sem.at[i])
        loads[name].start()

    def emit(name):
        i = RESULTS.index(name)
        copy = pltpu.make_async_copy(getattr(r, name + "_held"), getattr(r, name), r.emit_sem.at[i])
        copy.start()
        drains.append(copy.wait)

    def weight_copy(k, block):
        return remote(
            r.out_all.at[rows_of(block), :], r.out_all.at[rows_of(block), :],
            r.weight_send.at[k], r.weight_recv.at[k], (d, lax.rem(m + k, n_mp)),
        )

    def near_copy(hop, chunk):
        _, source, target, there = hops[hop][:4]
        part = rows_of(chunk)
        return remote(
            r.kv.at[source, part, :], r.kv.at[there, part, :],
            r.kv_send.at[hop, chunk], r.kv_recv.at[hop, chunk], (target, m),
        )

    def near_arrival(hop, chunk):
        part = rows_of(chunk)
        return remote(
            r.kv.at[OWN, part, :], r.kv.at[hops[hop][5], part, :],
            r.kv_send.at[hop, chunk], r.kv_recv.at[hop, chunk], (hops[hop][6], m),
        )

    id_steps = (1, -1, 2, -2)

    def id_copy(i):
        step = id_steps[i]
        return remote(
            r.ids.at[OWN], r.ids.at[OWN - step], r.id_send.at[i], r.id_recv.at[i],
            (lax.rem(d + step + n_dp, n_dp), m),
        )

    def wide_copy(k, source):
        return remote(
            r.wide.at[source], r.wide.at[source],
            r.wide_send.at[k], r.wide_recv.at[k], (lax.rem(d + k, n_dp), m),
        )

    leave_barrier = entry_barrier(n_dp, n_mp, d, m)
    query_ids = r.row_table[...].astype(f32).reshape(1, rows)
    support = r.row_kind[...].astype(f32).reshape(1, rows) == 1.0
    r.ids[OWN] = jnp.where(support & (query_ids != 0.0), query_ids, -1.0)
    wide_held = jnp.where(support & (query_ids == 0.0), 1.0, 0.0)[:, :1]
    r.vec[...] = jnp.zeros_like(r.vec)

    def send_early():
        leave_barrier()
        for h in first_hops:
            when(hops[h][0], near_copy(h, 0).start)
        for i, step in enumerate(id_steps):
            when((d + step >= 0) & (d + step < n_dp), id_copy(i).start)
        loads["out_weight"].wait()
        for k in range(1, n_mp):
            weight_copy(k, m).start()

    def drain_early():
        for i, step in enumerate(id_steps):
            when((d + step >= 0) & (d + step < n_dp), id_copy(i).wait_send)
        for k in range(1, n_mp):
            weight_copy(k, m).wait_send()
        for h in range(len(hops)):
            for c in range(chunks):
                when(hops[h][0], near_copy(h, c).wait_send)

    drains.append(drain_early)
    gain, shift = r.first_gain[...], r.first_shift[...]
    for i, w in enumerate((r.query_weight, r.key_weight, r.value_weight)):
        r.qkv_weight[:, i * HD:(i + 1) * HD] = w[...]
    for c in range(chunks):
        part = slice(c * CHUNK, (c + 1) * CHUNK)
        centred, scale = layer_stats(r.row_input[part, :].astype(f32))
        normed = (centred * scale * gain + shift).astype(bf16)
        r.normed[part, :] = normed
        qkv = mm(normed, r.qkv_weight[:, HD:])
        r.kv[OWN, part, :] = qkv.astype(bf16)
        if c == 0:
            r.wide[d, :, :2 * HD] = qkv[:1, :].astype(bf16).astype(f32)
            r.wide[d, :, 2 * HD:] = jnp.broadcast_to(wide_held, (1, HD))
            send_early()
        else:
            for h in first_hops:
                when(hops[h][0], near_copy(h, c).start)

    def wide_start(k, _):
        wide_copy(k, d).start()
        return 0

    lax.fori_loop(1, n_dp, wide_start, 0)
    for c in range(chunks):
        part = slice(c * CHUNK, (c + 1) * CHUNK)
        query = mm(r.normed[part, :], r.qkv_weight[:, :HD])
        r.query[part, :] = query.astype(bf16)
        r.query_t[:, part] = query.T.astype(bf16)

    def wide_sent(k, _):
        wide_copy(k, d).wait_send()
        return 0

    drains.append(lambda: lax.fori_loop(1, n_dp, wide_sent, 0))

    r.top[...] = jnp.full_like(r.top, masked_score)
    r.total[...] = jnp.zeros_like(r.total)
    r.mixed_t[...] = jnp.zeros_like(r.mixed_t)

    def absorb(key_rows, peak):
        for j, lanes in enumerate(tiles):
            old = r.top[:, lanes]
            new = jnp.maximum(old, jnp.broadcast_to(jnp.max(peak[j], axis=0, keepdims=True), (8, LANE)))
            r.top[:, lanes] = new
            fade = jnp.exp2((old - new) * EXP2_SCALE)
            r.total[:, lanes] = r.total[:, lanes] * fade
            r.mixed_t[:, lanes] = r.mixed_t[:, lanes] * fade[:1, :]

        def weigh(t, _):
            size = min(key_rows, CHUNK)
            part = rows_of(t, size)
            for lanes in tiles:
                weight = jnp.exp2((r.scores[part, lanes] - r.top[:1, lanes]) * EXP2_SCALE)
                r.total[:, lanes] += jnp.sum(weight.reshape(size // 8, 8, LANE), axis=0)
                r.weights[part, lanes] = weight.astype(bf16)
            return 0

        lax.fori_loop(0, max(1, key_rows // CHUNK), weigh, 0, unroll=True)

    def score(key, allowed, part, peak):
        scores = mm(key, r.query_t[...])
        result = []
        for j, lanes in enumerate(tiles):
            kept = jnp.where(allowed(lanes), scores[:, lanes], masked_score)
            r.scores[part, lanes] = kept
            result.append(jnp.maximum(peak[j], jnp.max(kept.reshape(-1, 8, LANE), axis=0)))
        return tuple(result)

    no_peak = tuple(jnp.full((8, LANE), masked_score, f32) for _ in tiles)

    def attend(slot):
        spread_ids(r.ids[slot], r.id_columns.at[slot], rows)

        def one(t, peak):
            part = rows_of(t)
            ids = r.id_columns[slot, part, :]
            return score(
                r.kv[slot, part, :HD], lambda lanes: ids == query_ids[:, lanes], part, peak
            )

        absorb(rows, lax.fori_loop(0, chunks, one, no_peak, unroll=True))
        r.mixed_t[...] += mm(r.kv[slot, :, HD:], r.weights[...], TN)

    attend(OWN)
    for i, step in enumerate(id_steps):
        when((d - step >= 0) & (d - step < n_dp), id_copy(i).wait_recv)

    def idle_work():
        loads["out_grad"].wait()
        loads["down_weight"].wait()
        r.grad_active[...] = mm(r.out_grad_held[...], r.down_weight_held[...], NT)
        loads["up_weight"].wait()
        r.up_weight_t[...] = r.up_weight_held[...].T
        r.qkv_weight_t[...] = r.qkv_weight[...].T

    for h in first_hops + later_hops:
        if h == first_hops[1]:
            idle_work()
        for c in range(chunks):
            when(hops[h][4], near_arrival(h, c).wait_recv)
            for later in follow[h]:
                when(hops[later][0], near_copy(later, c).start)
        when(hops[h][4], lambda h=h: attend(hops[h][5]))

    def wide_arrive(k, _):
        wide_copy(k, lax.rem(d - k + n_dp, n_dp)).wait_recv()
        return 0

    lax.fori_loop(1, n_dp, wide_arrive, 0)
    wide_rows = n_dp
    r.wide_rows[...] = r.wide[...].reshape(n_dp, 3 * HD)

    def wide_allowed(lanes):
        return (r.wide_rows[:, 2 * HD:] > 0.5) & (query_ids[:, lanes] == 0.0)

    absorb(wide_rows, score(r.wide_rows[:, :HD].astype(bf16), wide_allowed, slice(0, wide_rows), no_peak))
    r.mixed_t[...] += mm(r.wide_rows[:, HD:2 * HD].astype(bf16), r.weights[:wide_rows, :], TN)

    for j, lanes in enumerate(tiles):
        total = jnp.sum(r.total[:, lanes], axis=0, keepdims=True)
        mixed = r.mixed_t[:, lanes] / total
        r.mixed_t[:, lanes] = mixed
        r.log_total[:, lanes] = jnp.broadcast_to(
            r.top[:1, lanes] * EXP2_SCALE + jnp.log2(total), (8, LANE)
        )
        r.mixed[lanes, lanes_of(m)] = mixed.T.astype(bf16)

    def head_copy(way, block, c):
        to = m + (1 if way == 0 else -1)
        distance = m - block if way == 0 else block - m
        at = r.mixed.at[rows_of(c), lanes_of(lax.rem(block + n_mp, n_mp))]
        return remote(
            at, at, r.head_send.at[way, distance, c], r.head_recv.at[way, distance, c],
            (d, lax.rem(to + n_mp, n_mp)),
        )

    def head_arrival(way, block, c):
        distance = (m - block if way == 0 else block - m) - 1
        at = r.mixed.at[rows_of(c), lanes_of(lax.rem(block + n_mp, n_mp))]
        return remote(
            at, at, r.head_send.at[way, distance, c], r.head_recv.at[way, distance, c], (d, m),
        )

    def head_step(s):
        c = jnp.clip(s, 0, chunks - 1)
        for way in (0, 1):
            room = m + 1 < n_mp if way == 0 else m > 0

            @pl.when((s < chunks) & room)
            def _(way=way):
                head_copy(way, m, c).start()
        for distance in range(1, n_mp):
            t = s - distance * HEAD_LAG
            valid = (t >= 0) & (t < chunks)
            t = jnp.clip(t, 0, chunks - 1)
            for way in (0, 1):
                block = m - distance if way == 0 else m + distance
                room = m + 1 < n_mp if way == 0 else m > 0

                @pl.when(valid & (block >= 0) & (block < n_mp))
                def _(way=way, block=block, t=t, room=room):
                    head_arrival(way, block, t).wait_recv()

                    @pl.when(room)
                    def _():
                        head_copy(way, block, t).start()

    def add_vector(name, values):
        i = VECTORS.index(name)
        r.vec[i] += jnp.sum(values.reshape(-1, 8, values.shape[-1]), axis=0)

    def feed_forward(c):
        part = rows_of(c)
        branch = mm(r.mixed[part, :], r.out_all[...]) + r.out_bias[...]
        middle = r.row_input[part, :].astype(f32) + branch
        r.middle[part, :] = middle
        centred, scale = layer_stats(middle)
        normed = (centred * scale * r.second_gain[...] + r.second_shift[...]).astype(bf16)
        r.normed_mid[part, :] = normed
        active, slope = gelu_parts(mm(normed, r.up_weight_held[...]) + r.up_bias[...])
        active = active.astype(bf16)
        r.active[part, :] = active
        grad_upper = (slope * r.grad_active[part, :]).astype(bf16)
        r.grad_upper[part, :] = grad_upper
        add_vector("up_bias", grad_upper.astype(f32))
        r.mid_terms[part, :] = mm(grad_upper, r.up_weight_t[...]).astype(bf16)
        for u in range(SUB):
            tree_mid.send(c * SUB + u)

    def finish_mid(part, grad):
        centred, scale = layer_stats(r.middle[part, :])
        back, gain_terms = layer_back(grad, r.second_gain[...], centred, scale)
        grad_middle = r.out_grad_held[part, :].astype(f32) + back
        r.grad_middle[part, :] = grad_middle
        branch = grad_middle.astype(bf16)
        r.grad_branch[part, :] = branch
        heads = mm(branch, r.out_all_t[...]).astype(bf16)
        r.heads_terms[part, :] = heads
        for head in range(1, n_mp - 1):
            @pl.when(m == head)
            def _(head=head):
                r.grad_heads[part, :] = heads[:, head * HD:(head + 1) * HD]
        add_vector("second_gain", gain_terms)
        add_vector("second_shift", grad)
        add_vector("out_bias", branch.astype(f32))

    def finish_out(part, total):
        r.block_output_held[part, :] = (r.middle[part, :] + total + r.down_bias[...]).astype(bf16)

    def finish_first(part, grad):
        centred, scale = layer_stats(r.row_input[part, :].astype(f32))
        back, gain_terms = layer_back(grad, r.first_gain[...], centred, scale)
        r.grad_low_held[part, :] = (r.grad_middle[part, :] + back).astype(bf16)
        add_vector("first_gain", gain_terms)
        add_vector("first_shift", grad)

    tree_mid, tree_out, tree_first = trees
    tree_mid.bind(r, d, m, r.mid_terms, (r.heads_terms, r.grad_heads), finish_mid)
    tree_out.bind(r, d, m, r.out_terms, r.block_output_held, finish_out)
    tree_first.bind(r, d, m, r.first_terms, r.grad_low_held, finish_first)
    up_sum, down_sum, out_sum, qkv_sum = reductions
    up_sum.bind(r, r.up_weight_sum, d, m)
    down_sum.bind(r, r.down_weight_sum, d, m)
    out_sum.bind(r, r.out_weight_sum, d, m)
    qkv_sum.bind(r, r.qkv_weight_sum, d, m)

    def probabilities(slot):
        def one(t, _):
            part = rows_of(t)
            ids = r.id_columns[slot, part, :]
            scores = mm(r.kv[slot, part, :HD], r.query_t[...])
            for lanes in tiles:
                prob = jnp.exp2(scores[:, lanes] * EXP2_SCALE - r.log_total[:1, lanes])
                r.probs[slot, part, lanes] = jnp.where(
                    ids == query_ids[:, lanes], prob, 0.0
                ).astype(bf16)
            return 0

        lax.fori_loop(0, chunks, one, 0, unroll=True)

    for k in range(1, n_mp):
        weight_copy(k, lax.rem(m - k + n_mp, n_mp)).wait_recv()
    feed_from = (n_mp - 1) * HEAD_LAG
    stages = [(True, OWN)] + [(hops[h][4], hops[h][5]) for h in range(len(hops))]

    def middle_step(s, _):
        head_step(s)
        for i, (cond, slot) in enumerate(stages):
            pl.when(both(s == i, cond))(lambda slot=slot: probabilities(slot))

        @pl.when(s == 0)
        def _():
            r.out_all_t[...] = r.out_all[...].T

        c = s - feed_from

        @pl.when((c >= 0) & (c < chunks))
        def _():
            feed_forward(c)

        for lag, act in ((GATHER_LAG, tree_mid.gather), (WORK_LAG, tree_mid.work)):
            @pl.when((c >= lag) & (c < chunks + lag))
            def _(lag=lag, act=act):
                for u in range(SUB):
                    act((c - lag) * SUB + u)
        return 0

    lax.fori_loop(0, feed_from + chunks, middle_step, 0)

    def drain_heads():
        for way in (0, 1):
            room = m + 1 < n_mp if way == 0 else m > 0
            for distance in range(n_mp - 1):
                block = m - distance if way == 0 else m + distance

                @pl.when(room & (block >= 0) & (block < n_mp))
                def _(way=way, block=block):
                    for c in range(chunks):
                        head_copy(way, block, c).wait_send()

    drains.append(drain_heads)

    def down_weight_grad():
        r.down_weight_sum[...] = mm(r.active[...], r.out_grad_held[...], TN)
        down_sum.event(0)

    def up_weight_grad():
        r.up_weight_sum[...] = mm(r.normed_mid[...], r.grad_upper[...], TN)
        up_sum.event(0)

    parts = chunks * SUB
    tree_parts = [list(range(c * SUB, (c + 1) * SUB)) for c in range(chunks)]

    def act(tree, chunk, what):
        if 0 <= chunk < chunks:
            for c in tree_parts[chunk]:
                getattr(tree, what)(c)

    down_weight_grad()
    for i in range(chunks - WORK_LAG, chunks):
        if i + WORK_LAG - GATHER_LAG < chunks:
            act(tree_mid, i + WORK_LAG - GATHER_LAG, "gather")
        if i < chunks - 1:
            act(tree_mid, i, "work")
    up_weight_grad()
    r.out_terms[...] = mm(r.active[...], r.down_weight_held[...]).astype(bf16)
    act(tree_mid, chunks - 1, "work")
    for c in range(parts):
        tree_out.send(c)

    def branch_copy(c):
        rows_c = rows_of(c, PART)
        return remote(
            r.grad_branch.at[rows_c, :], r.grad_branch.at[rows_c, :],
            r.branch_send.at[c], r.branch_recv.at[c], (d, tree_mid.inward),
        )

    for c in range(parts):
        pl.when(tree_mid.mine(c))(branch_copy(c).start)
    down_sum.event(1)
    up_sum.event(1)
    for c in range(parts):
        tree_mid.forward(c)
        tree_mid.collect(c)
    drains.append(tree_mid.drain)

    for c in range(chunks):
        part = slice(c * CHUNK, (c + 1) * CHUNK)
        turned = r.grad_heads[part, :].astype(f32).T
        r.grad_heads_t[:, part] = turned.astype(bf16)
        r.row_delta[:, part] = jnp.broadcast_to(
            jnp.sum(turned * r.mixed_t[:, part], axis=0, keepdims=True), (8, LANE)
        )
    r.grad_query_t[...] = jnp.zeros_like(r.grad_query_t)

    def score_back(prob, value, part):
        grad_probs = mm(value, r.grad_heads_t[...])
        for lanes in tiles:
            r.weights[part, lanes] = (
                prob(lanes).astype(f32) * (grad_probs[:, lanes] - r.row_delta[:1, lanes])
            ).astype(bf16)

    def attend_back(slot, store):
        def one(t, _):
            part = rows_of(t)
            score_back(lambda lanes: r.probs[slot, part, lanes], r.kv[slot, part, HD:], part)
            store(
                t, part, mm(r.weights[part, :], r.query[...]) * SCALE,
                mm(r.probs[slot, part, :], r.grad_heads[...]),
            )
            return 0

        lax.fori_loop(0, chunks, one, 0, unroll=True)
        r.grad_query_t[...] += mm(r.kv[slot, :, :HD], r.weights[...], TN)

    def store_terms(slot, sent):
        def store(t, part, key_grad, value_grad):
            r.kv_terms[slot, part, :HD] = key_grad.astype(bf16)
            r.kv_terms[slot, part, HD:] = value_grad.astype(bf16)
            sent(t)
        return store

    def store_own(t, part, key_grad, value_grad):
        r.kv_grad[part, :HD] = key_grad
        r.kv_grad[part, HD:] = value_grad

    def back_copy(hop, chunk):
        part = rows_of(chunk)
        return remote(
            r.kv_terms.at[hops[hop][5], part, :], r.kv_back.at[hop, part, :],
            r.back_send.at[hop, chunk], r.back_recv.at[hop, chunk], (hops[hop][6], m),
        )

    def add_back(hop, chunk):
        part = rows_of(chunk)
        back_copy(hop, chunk).wait_recv()
        slot = hops[hop][1]
        r.kv_terms[slot, part, :] = (
            r.kv_terms[slot, part, :].astype(f32) + r.kv_back[hop, part, :].astype(f32)
        ).astype(bf16)

    def pass_back(h, cond):
        for c in range(chunks):
            for later in follow[h]:
                when(both(hops[later][0], cond), lambda later=later, c=c: add_back(later, c))
            when(both(hops[h][4], cond), back_copy(h, c).start)

    def back_stage(h, sends):
        def sent(t):
            when(sends, back_copy(h, t).start)

        when(hops[h][4], lambda: attend_back(hops[h][5], store_terms(hops[h][5], sent)))

    out_work = []
    for i in range(chunks + 2):
        out_work.append(lambda i=i: (
            act(tree_out, i, "gather"), act(tree_out, i - 1, "work"), act(tree_out, i - 2, "forward")
        ))

    def side_work():
        if out_work:
            out_work.pop(0)()

    def head_pair_grad():
        for c in range(parts):
            pl.when(tree_mid.other(c))(branch_copy(c).wait_recv)

        @pl.when(tree_mid.inner)
        def _():
            pair = pl.ds(pl.multiple_of(tree_mid.half * 2 * HD, 2 * HD), 2 * HD)
            r.out_weight_sum[...] = mm(r.mixed[:, pair], r.grad_branch[...], TN)
            out_sum.event(0)

    def branch_drain():
        for c in range(parts):
            pl.when(tree_mid.mine(c))(branch_copy(c).wait_send)

    drains.append(branch_drain)
    inner = tree_mid.inner

    def out_event(e):
        pl.when(inner)(lambda: out_sum.event(e))

    if len(hops) == 5 and later_hops:
        adds_core, adds_row, adds_corner = hops[4][0], hops[2][0], hops[3][0]
        no = jnp.logical_not
        back_stage(3, no(adds_core))
        back_stage(4, True)
        back_stage(2, True)
        side_work()
        pass_back(3, adds_core)
        back_stage(1, no(adds_row) & no(adds_corner))
        down_sum.event(2)
        up_sum.event(2)
        back_stage(0, True)
        side_work()
        pass_back(1, adds_row & no(adds_corner))
        late_back = [(1, adds_corner)]
    else:
        for h in range(len(hops)):
            back_stage(h, True)
            side_work()
        down_sum.event(2)
        up_sum.event(2)
        late_back = []
    attend_back(OWN, store_own)
    side_work()
    wide_scores = mm(r.wide_rows[:, :HD].astype(bf16), r.query_t[...])

    def wide_prob(lanes):
        prob = jnp.exp2(wide_scores[:, lanes] * EXP2_SCALE - r.log_total[:1, lanes])
        return jnp.where(wide_allowed(lanes), prob, 0.0)

    wide_part = slice(0, wide_rows)
    score_back(wide_prob, r.wide_rows[:, HD:2 * HD].astype(bf16), wide_part)
    grads = r.weights[wide_part, :]
    r.grad_query_t[...] += mm(r.wide_rows[:, :HD].astype(bf16), grads, TN)
    wide_probs = jnp.concatenate([wide_prob(lanes).astype(bf16) for lanes in tiles], axis=1)
    wide_terms = jnp.concatenate(
        (mm(grads, r.query[...]) * SCALE, mm(wide_probs, r.grad_heads[...])), axis=1
    )
    r.wide_terms[...] = wide_terms.reshape(n_dp, 1, 2 * HD)

    def wide_back_copy(k, target, source):
        return remote(
            r.wide_terms.at[target], r.wide_back.at[source],
            r.wide_back_send.at[k], r.wide_back_recv.at[k], (target, m),
        )

    def wide_back_start(k, _):
        wide_back_copy(k, lax.rem(d + k, n_dp), d).start()
        return 0

    def wide_back_arrive(k, _):
        wide_back_copy(k, lax.rem(d + k, n_dp), lax.rem(d - k + n_dp, n_dp)).wait_recv()
        return 0

    lax.fori_loop(1, n_dp, wide_back_start, 0)

    def back_sent(k, _):
        wide_back_copy(k, lax.rem(d + k, n_dp), d).wait_send()
        return 0

    def drain_back():
        lax.fori_loop(1, n_dp, back_sent, 0)
        for h in range(len(hops)):
            for c in range(chunks):
                when(hops[h][4], back_copy(h, c).wait_send)

    drains.append(drain_back)
    r.wide_back[d] = r.wide_terms[d]
    for h, cond in late_back:
        pass_back(h, cond)
    side_work()
    for c in range(chunks):
        part = slice(c * CHUNK, (c + 1) * CHUNK)
        r.qkv_grad[part, :HD] = (r.grad_query_t[:, part].T * SCALE).astype(bf16)
    lax.fori_loop(1, n_dp, wide_back_arrive, 0)
    r.kv_grad[:1, :] += jnp.sum(r.wide_back[...], axis=0)
    head_pair_grad()
    side_work()

    inner_rows = [VECTORS.index(name) for name in VECTORS if name not in ("up_bias", "down_bias")]

    def line_vec_copy(k, half):
        return remote(
            r.line_vec.at[half], r.line_vec.at[half],
            r.line_vec_send.at[k], r.line_vec_recv.at[half], (d, lax.rem(m + k, n_mp)),
        )

    def vectors_along_line():
        for i in range(len(VECTORS)):
            r.own_vec[i:i + 1, :] = jnp.sum(r.vec[i], axis=0, keepdims=True)
        r.own_vec[len(VECTORS):, :] = jnp.zeros_like(r.own_vec[len(VECTORS):, :])

        @pl.when(inner)
        def _():
            r.line_vec[tree_mid.half] = r.own_vec[...]
            for k in range(1, n_mp):
                line_vec_copy(k, tree_mid.half).start()

    def all_vec_copy(k, block):
        return remote(
            r.all_vec.at[block], r.all_vec.at[block],
            r.all_vec_send.at[k], r.all_vec_recv.at[k], (lax.rem(d + k, n_dp), m),
        )

    def all_vec_start(k, _):
        all_vec_copy(k, d).start()
        return 0

    def all_vec_arrive(k, _):
        all_vec_copy(k, lax.rem(d - k + n_dp, n_dp)).wait_recv()
        return 0

    def vec_sent(k, _):
        all_vec_copy(k, d).wait_send()
        return 0

    def vectors_over_all():
        for half in (0, 1):
            pl.when(tree_mid.end | (tree_mid.half != half))(line_vec_copy(1, half).wait_recv)
        row = lax.broadcasted_iota(jnp.int32, r.own_vec.shape, 0)
        summed = row < 0
        for i in inner_rows:
            summed = summed | (row == i)
        r.all_vec[d] = jnp.where(summed, r.line_vec[0] + r.line_vec[1], r.own_vec[...])
        lax.fori_loop(1, n_dp, all_vec_start, 0)

    def vectors_done():
        lax.fori_loop(1, n_dp, all_vec_arrive, 0)
        r.vectors_held[...] = jnp.sum(r.all_vec[...], axis=0)
        emit("vectors")

    def drain_vectors():
        @pl.when(inner)
        def _():
            for k in range(1, n_mp):
                line_vec_copy(k, tree_mid.half).wait_send()
        lax.fori_loop(1, n_dp, vec_sent, 0)

    def last_step(s):
        part = slice(s * CHUNK, (s + 1) * CHUNK)
        for h in first_hops:
            def add(h=h):
                back_copy(h, s).wait_recv()
                r.kv_grad[part, :] += r.kv_back[h, part, :].astype(f32)
            when(hops[h][0], add)
        r.qkv_grad[part, HD:] = r.kv_grad[part, :].astype(bf16)
        r.first_terms[part, :] = mm(r.qkv_grad[part, :], r.qkv_weight_t[...]).astype(bf16)
        act(tree_first, s, "send")

    def out_share_copy():
        block = rows_of(tree_mid.half, HD)
        return remote(
            r.out_sum_all_held.at[block, :], r.out_final_held,
            r.share_sem.at[0], r.share_sem.at[1], (d, lax.rem(tree_mid.outward + n_mp, n_mp)),
        )

    def out_share():
        @pl.when(inner)
        def _():
            r.out_final_held[...] = r.out_sum_all_held[rows_of(1 - tree_mid.half, HD), :]
            out_share_copy().start()

    for s in range(chunks):
        last_step(s)
        act(tree_first, s - 1, "gather")
        act(tree_first, s - 2, "work")
        act(tree_first, s - 3, "forward")
        side_work()
        if s == 1:
            add_vector("down_bias", r.out_grad_held[...].astype(f32))
            down_sum.event(3)
            up_sum.event(3)
            out_event(1)
    r.qkv_weight_sum[...] = mm(r.normed[...], r.qkv_grad[...], TN)
    qkv_sum.event(0)
    act(tree_first, chunks - 1, "gather")
    act(tree_first, chunks - 2, "work")
    act(tree_first, chunks - 3, "forward")
    out_event(2)
    qkv_sum.event(1)
    act(tree_first, chunks - 1, "work")
    vectors_along_line()
    act(tree_first, chunks - 2, "forward")
    down_sum.event(4)
    up_sum.event(4)
    for level in range(5, up_sum.events):
        down_sum.event(level)
        up_sum.event(level)
    emit("up_sum_all")
    emit("down_sum_all")
    qkv_sum.event(2)
    out_event(3)
    act(tree_first, chunks - 1, "forward")
    vectors_over_all()
    while out_work:
        side_work()
    for c in range(parts):
        tree_out.collect(c)
    emit("block_output")
    qkv_sum.event(3)
    for level in range(4, out_sum.events):
        out_event(level)
    out_share()
    for c in range(parts):
        tree_first.collect(c)
    emit("grad_low")
    for level in range(4, qkv_sum.events):
        qkv_sum.event(level)
    emit("qkv_sum_all")
    pl.when(tree_mid.end)(out_share_copy().wait_recv)
    emit("out_final")
    pl.when(inner)(out_share_copy().wait_send)
    vectors_done()
    drains.append(drain_vectors)
    drains.append(tree_first.drain)
    drains.append(tree_out.drain)

    for drain in drains:
        drain()


def layer(n_dp, n_mp, args):
    rows, width = args["row_input"].shape
    hidden = args["up_weight"].shape[1]
    chunks = rows // CHUNK
    names = tuple(args)
    outs = dict(
        block_output=((rows, width), bf16), grad_low=((rows, width), bf16),
        up_sum_all=((width, hidden), bf16), down_sum_all=((hidden, width), bf16),
        out_final=((HD, width), bf16), qkv_sum_all=((width, 3 * HD), bf16),
        vectors=((8, width), f32),
    )
    bits = list(range(n_dp.bit_length() - 1))
    groups = [tuple(bits[:1])] + [tuple(bits[i:i + 2]) for i in range(1, len(bits), 2)]
    reductions = (
        Reduction("up_sum", width, hidden, groups), Reduction("down_sum", hidden, width, groups),
        Reduction("out_sum", 2 * HD, width, groups), Reduction("qkv_sum", width, 3 * HD, groups),
    )
    trees = (
        Tree("tree_mid", n_mp, chunks * SUB, width, scatter=True),
        Tree("tree_out", n_mp, chunks * SUB, width), Tree("tree_first", n_mp, chunks * SUB, width),
    )
    dma = pltpu.SemaphoreType.DMA
    v = pltpu.VMEM
    scratch = dict(
        normed=v((rows, width), bf16), query=v((rows, HD), bf16), query_t=v((HD, rows), bf16),
        mixed=v((rows, width), bf16), mixed_t=v((HD, rows), f32), log_total=v((8, rows), f32),
        ids=v((SLOTS, 1, rows), f32), id_columns=v((SLOTS, rows, LANE), f32),
        qkv_weight=v((width, 3 * HD), bf16), qkv_weight_t=v((3 * HD, width), bf16),
        up_weight_t=v((hidden, width), bf16), out_all=v((width, width), bf16),
        kv=v((SLOTS, rows, 2 * HD), bf16), kv_terms=v((SLOTS, rows, 2 * HD), bf16),
        kv_back=v((5, rows, 2 * HD), bf16), kv_grad=v((rows, 2 * HD), f32),
        wide=v((n_dp, 1, 3 * HD), f32), wide_rows=v((n_dp, 3 * HD), f32),
        wide_terms=v((n_dp, 1, 2 * HD), f32), wide_back=v((n_dp, 1, 2 * HD), f32),
        top=v((8, rows), f32), total=v((8, rows), f32),
        scores=v((rows, rows), f32), weights=v((rows, rows), bf16),
        out_grad_held=v((rows, width), bf16), up_weight_held=v((width, hidden), bf16),
        down_weight_held=v((hidden, width), bf16), block_output_held=v((rows, width), bf16),
        grad_low_held=v((rows, width), bf16), vectors_held=v((8, width), f32),
        probs=v((SLOTS, rows, rows), bf16), grad_active=v((rows, hidden), f32),
        middle=v((rows, width), f32), normed_mid=v((rows, width), bf16),
        active=v((rows, hidden), bf16), grad_upper=v((rows, hidden), bf16),
        mid_terms=v((rows, width), bf16), out_terms=v((rows, width), bf16),
        first_terms=v((rows, width), bf16), grad_middle=v((rows, width), f32),
        grad_branch=v((rows, width), bf16),
        grad_heads=v((rows, HD), bf16), grad_heads_t=v((HD, rows), bf16),
        row_delta=v((8, rows), f32), grad_query_t=v((HD, rows), f32),
        qkv_grad=v((rows, 3 * HD), bf16),
        up_weight_sum=v((width, hidden), f32), down_weight_sum=v((hidden, width), f32),
        out_weight_sum=v((2 * HD, width), f32), qkv_weight_sum=v((width, 3 * HD), f32),
        vec=v((len(VECTORS), 8, width), f32), line_vec=v((2, 8, width), f32), own_vec=v((8, width), f32),
        heads_terms=v((rows, width), bf16), out_all_t=v((width, width), bf16),
        out_final_held=v((HD, width), bf16),
        all_vec=v((n_dp, 8, width), f32),
        kv_send=dma((5, chunks)), kv_recv=dma((5, chunks)),
        back_send=dma((5, chunks)), back_recv=dma((5, chunks)),
        id_send=dma((4,)), id_recv=dma((4,)),
        weight_send=dma((n_mp,)), weight_recv=dma((n_mp,)),
        wide_send=dma((n_dp,)), wide_recv=dma((n_dp,)),
        wide_back_send=dma((n_dp,)), wide_back_recv=dma((n_dp,)),
        head_send=dma((2, n_mp, chunks)), head_recv=dma((2, n_mp, chunks)),
        line_vec_send=dma((n_mp,)), line_vec_recv=dma((2,)),
        branch_send=dma((chunks * SUB,)), branch_recv=dma((chunks * SUB,)), share_sem=dma((2,)),
        load_sem=dma((4,)), emit_sem=dma((len(RESULTS),)),
        all_vec_send=dma((n_dp,)), all_vec_recv=dma((n_dp,)),
    )
    for part in reductions + trees:
        found = part.scratch()
        scratch.update({k + "_held" if k.endswith("_all") else k: held for k, held in found.items()})

    def kernel(*refs):
        r = types.SimpleNamespace(**dict(zip(names + tuple(outs) + tuple(scratch), refs)))
        layer_kernel(r, n_dp, n_mp, rows, reductions, trees)

    vmem, hbm = pl.BlockSpec(memory_space=pltpu.VMEM), pl.BlockSpec(memory_space=pl.ANY)
    late = ("out_weight", "out_grad", "up_weight", "down_weight")
    result = pl.pallas_call(
        kernel,
        out_shape=[jax.ShapeDtypeStruct(*o) for o in outs.values()],
        in_specs=[hbm if name in late else vmem for name in names],
        out_specs=[hbm] * len(outs),
        scratch_shapes=list(scratch.values()),
        compiler_params=pltpu.CompilerParams(
            collective_id=0, has_side_effects=True, vmem_limit_bytes=58 * 1024 * 1024),
        name="layer",
    )(*args.values())
    return dict(zip(outs, result))


def write_out(got):
    names = tuple(got)
    rows, width = got["block_output"].shape
    hidden = got["up_sum_all"].shape[1]
    wide = dict(
        input_grad=(rows, width), query=(width, HD), key=(width, HD), value=(width, HD),
        out=(HD, width), up=(width, hidden), down=(hidden, width),
    )
    outs = dict(block_output=((rows, width), bf16))
    outs.update({name: (shape, f32) for name, shape in wide.items()})
    outs.update({name: ((1, width), f32) for name in VECTORS})

    def kernel(*refs):
        given = dict(zip(names, refs))
        out = dict(zip(outs, refs[len(names):]))
        held = dict(zip(tuple(given) + tuple(wide), refs[len(names) + len(outs):]))
        in_sems, out_sems = refs[-2:]
        loads, copies = {}, []
        for i, name in enumerate(names):
            loads[name] = pltpu.make_async_copy(given[name], held[name], in_sems.at[i])
            loads[name].start()

        def send(source, name):
            copy = pltpu.make_async_copy(source, out[name], out_sems.at[len(copies)])
            copy.start()
            copies.append(copy)

        for name, low in (
            ("input_grad", "grad_low"), ("up", "up_sum_all"), ("down", "down_sum_all"),
            ("out", "out_final"),
        ):
            loads[low].wait()
            held[name][...] = held[low][...].astype(f32)
            send(held[name], name)
        loads["qkv_sum_all"].wait()
        for i, name in enumerate(("query", "key", "value")):
            held[name][...] = held["qkv_sum_all"][:, i * HD:(i + 1) * HD].astype(f32)
            send(held[name], name)
        loads["block_output"].wait()
        send(held["block_output"], "block_output")
        loads["vectors"].wait()
        for i, name in enumerate(VECTORS):
            send(held["vectors"].at[i:i + 1, :], name)
        for copy in copies:
            copy.wait()

    hbm = pl.BlockSpec(memory_space=pl.ANY)
    result = pl.pallas_call(
        kernel,
        out_shape=[jax.ShapeDtypeStruct(*o) for o in outs.values()],
        in_specs=[hbm] * len(names),
        out_specs=[hbm] * len(outs),
        scratch_shapes=[pltpu.VMEM(a.shape, a.dtype) for a in got.values()]
        + [pltpu.VMEM(shape, f32) for shape in wide.values()]
        + [pltpu.SemaphoreType.DMA((len(names),)), pltpu.SemaphoreType.DMA((len(outs),))],
        compiler_params=pltpu.CompilerParams(vmem_limit_bytes=60 * 1024 * 1024),
        name="write_out",
    )(*got.values())
    return dict(zip(outs, result))


def shards(
    n_dp, n_mp, row_input, first_gain, first_shift, query_weight, key_weight, value_weight,
    out_weight, out_bias, second_gain, second_shift, up_weight, up_bias, down_weight, down_bias,
    row_table, row_kind, out_grad,
):
    got = write_out(layer(n_dp, n_mp, dict(
        row_input=row_input, first_gain=first_gain[None], first_shift=first_shift[None],
        query_weight=query_weight, key_weight=key_weight, value_weight=value_weight,
        out_weight=out_weight, out_bias=out_bias[None], second_gain=second_gain[None],
        second_shift=second_shift[None], up_weight=up_weight, up_bias=up_bias[None],
        down_weight=down_weight, down_bias=down_bias[None], row_table=row_table,
        row_kind=row_kind, out_grad=out_grad,
    )))
    vector = {name: got[name][0] for name in VECTORS}
    return (
        got["block_output"], got["input_grad"], vector["first_gain"], vector["first_shift"],
        got["query"], got["key"], got["value"], got["out"],
        vector["out_bias"], vector["second_gain"], vector["second_shift"],
        got["up"], vector["up_bias"], got["down"], vector["down_bias"],
    )


def solution(mesh):
    n_dp, n_mp = mesh.shape["dp"], mesh.shape["mp"]
    in_specs = (
        P("dp", None), P(), P(), P(None, "mp"), P(None, "mp"), P(None, "mp"), P("mp", None),
        P(), P(), P(), P(None, "mp"), P("mp"), P("mp", None), P(), P("dp"), P("dp"), P("dp", None),
    )
    out_specs = (
        P("dp", None), P("dp", None), P(), P(), P(None, "mp"), P(None, "mp"), P(None, "mp"),
        P("mp", None), P(), P(), P(), P(None, "mp"), P("mp"), P("mp", None), P(),
    )
    return jax.shard_map(
        lambda *a: shards(n_dp, n_mp, *a), mesh=mesh, in_specs=in_specs, out_specs=out_specs,
        check_vma=False,
    )
```
